32 devices in a mesh: dp: 16 (over z, y, x), seq: 2 (over core).
Axes of the slice: x: 2, y: 2, z: 4, core: 2. Of those that a mesh axis runs over, the one named last changes fastest.
Arguments:
- tokens: bfloat16 [32, 512, 768], P('dp', 'seq'), may hold values from -6 to 6
- lengths: int32 [32], P('dp'), may hold values from 128 to 512, as said below
- cotangent: bfloat16 [32, 512, 768], P('dp', 'seq'), may hold values from -6 to 6
- w_query: bfloat16 [768, 768], P(('dp', 'seq')), may hold values from -0.3125 to 0.3125
- b_query: bfloat16 [768], P(('dp', 'seq')), may hold values from -3 to 3
- w_key: bfloat16 [768, 768], P(('dp', 'seq')), may hold values from -0.21875 to 0.21875
- w_value: bfloat16 [768, 768], P(('dp', 'seq')), may hold values from -0.21875 to 0.21875
- b_value: bfloat16 [768], P(('dp', 'seq')), may hold values from -3 to 3
- w_out: bfloat16 [768, 768], P(('dp', 'seq')), may hold values from -1.5 to 1.5
- b_out: bfloat16 [768], P(('dp', 'seq')), may hold values from -3 to 3
- gain_one: bfloat16 [768], P(('dp', 'seq')), may hold values from 0.25 to 1.75
- shift_one: bfloat16 [768], P(('dp', 'seq')), may hold values from -3 to 3
- w_inner: bfloat16 [768, 3072], P(('dp', 'seq')), may hold values from -0.21875 to 0.21875
- b_inner: bfloat16 [3072], P(('dp', 'seq')), may hold values from -3 to 3
- w_outer: bfloat16 [3072, 768], P(('dp', 'seq')), may hold values from -0.15625 to 0.15625
- b_outer: bfloat16 [768], P(('dp', 'seq')), may hold values from -3 to 3
- gain_two: bfloat16 [768], P(('dp', 'seq')), may hold values from 0.25 to 1.75
- shift_two: bfloat16 [768], P(('dp', 'seq')), may hold values from -3 to 3
Outputs:
- output: float32 [32, 512, 768], P('dp', 'seq')
- grad_tokens: float32 [32, 512, 768], P('dp', 'seq')
- grad_w_query: float32 [768, 768], P(('dp', 'seq'))
- grad_b_query: float32 [768], P(('dp', 'seq'))
- grad_w_key: float32 [768, 768], P(('dp', 'seq'))
- grad_w_value: float32 [768, 768], P(('dp', 'seq'))
- grad_b_value: float32 [768], P(('dp', 'seq'))
- grad_w_out: float32 [768, 768], P(('dp', 'seq'))
- grad_b_out: float32 [768], P(('dp', 'seq'))
- grad_gain_one: float32 [768], P(('dp', 'seq'))
- grad_shift_one: float32 [768], P(('dp', 'seq'))
- grad_w_inner: float32 [768, 3072], P(('dp', 'seq'))
- grad_b_inner: float32 [3072], P(('dp', 'seq'))
- grad_w_outer: float32 [3072, 768], P(('dp', 'seq'))
- grad_b_outer: float32 [768], P(('dp', 'seq'))
- grad_gain_two: float32 [768], P(('dp', 'seq'))
- grad_shift_two: float32 [768], P(('dp', 'seq'))
The draws below stay inside these ranges and needn't reach their ends.
Inputs may be any that keep to these rules, and one draw needn't show every extreme that they name: lengths[s] counts the valid leading positions of sequence s; in every draw some sequence has exactly 512 and some exactly 128.
All inputs are finite; a program needn't handle non-finite values.
Results may differ from the reference program's by a relative error of at most 0.015.
Values may be sent and summed in bfloat16 or wider, within the bound.
No kernel may reach another device: no remote copies, remote signals or barrier semaphores. Data moves between devices by JAX's collectives and lax.ppermute only.
A program may use at most 192 MiB of HBM per device.

```python
import jax
import jax.numpy as jnp
from jax import lax

D = 768
HEADS = 12
FF = 3072
HEAD_DIM = 64
LEN = 512
SEQS = 32


def draw_lengths(key, part):
    base = jax.random.randint(jax.random.fold_in(key, 11), (SEQS,), LEN // 4, LEN + 1, dtype=jnp.int32)
    longest = jax.random.randint(jax.random.fold_in(key, 12), (), 0, SEQS, dtype=jnp.int32)
    offset = jax.random.randint(jax.random.fold_in(key, 13), (), 1, SEQS, dtype=jnp.int32)
    shortest = (longest + offset) % SEQS
    slots = jnp.arange(SEQS, dtype=jnp.int32)
    base = jnp.where(slots == longest, LEN, base)
    return jnp.where(slots == shortest, LEN // 4, base).astype(jnp.int32)


def raised(array, rng, source, target, shards_of, factor):
    owner, partner = [(jnp.arange(array.shape[dim]) // (array.shape[dim] // shards_of)).reshape([-1 if axis == dim else 1 for axis in range(array.ndim)]) for dim in (source, target)]
    chosen = jax.random.permutation(rng, shards_of)[partner]
    strong = (owner == chosen) | (owner == (partner + shards_of // 2) % shards_of)
    return jnp.where(strong, factor * array, array)


def levels(rng, extent, split, smallest, top_value):
    level = 1.0
    for position, parts in split:
        heights = jax.random.uniform(jax.random.fold_in(jax.random.fold_in(rng, 6), position), (parts,), jnp.float32, smallest / len(split), top_value / len(split))
        level = level * jnp.repeat(jnp.exp(heights), extent[position] // parts).reshape((-1,) + (1,) * (len(extent) - 1 - position))
    return level


def bell_draw(key, shape, deviation, bound, pieces=(), kind=jnp.bfloat16):
    level = levels(key, shape, pieces, -0.22, 0.18) if pieces else 1.0
    drawn = jax.random.normal(key, shape, jnp.float32) * deviation * level
    return jnp.minimum(jnp.maximum(drawn, -bound), bound).astype(kind)


def noise_with(key, shape, width, reach, pieces, heavy, kind=jnp.bfloat16):
    entries = width * jax.random.normal(key, shape, jnp.float32)
    if pieces:
        entries = entries * levels(key, shape, pieces, -0.22, 0.18)
    return jnp.clip(raised(entries, jax.random.fold_in(key, 3), *heavy), -reach, reach).astype(kind)


def setup_inputs(seed: int = 0) -> dict:
    key_of = jax.random.split(jax.random.key(seed), 19)
    tokens = bell_draw(key_of[0], (SEQS, LEN, D), 1.0, 6.0, ((0, 16), (1, 2)))
    lengths = draw_lengths(jax.random.fold_in(key_of[18], 71), 0)
    cotangent = noise_with(key_of[2], (SEQS, LEN, D), 1.0, 6.0, ((0, 16), (1, 2)), (0, 2, 16, 2.0))
    w_query = bell_draw(key_of[3], (D, D), (D // 2) ** -0.5, 0.3125, ((0, 32),))
    b_query = bell_draw(key_of[4], (D,), 0.5, 3.0, ((0, 32),))
    w_key = bell_draw(key_of[5], (D, D), D ** -0.5, 0.21875, ((0, 32),))
    w_value = bell_draw(key_of[6], (D, D), D ** -0.5, 0.21875, ((0, 32),))
    b_value = bell_draw(key_of[7], (D,), 0.5, 3.0, ((0, 32),))
    w_out = bell_draw(key_of[8], (D, D), (D // 48) ** -0.5, 1.5, ((0, 32),))
    b_out = bell_draw(key_of[9], (D,), 0.5, 3.0, ((0, 32),))
    gain_one = jnp.clip(1.0 + 0.15 * jax.random.normal(key_of[10], (D,), jnp.float32), 0.25, 1.75).astype(jnp.bfloat16)
    shift_one = bell_draw(key_of[11], (D,), 0.5, 3.0, ((0, 32),))
    w_inner = bell_draw(key_of[12], (D, FF), D ** -0.5, 0.21875, ((0, 32),))
    b_inner = bell_draw(key_of[13], (FF,), 0.5, 3.0, ((0, 32),))
    w_outer = bell_draw(key_of[14], (FF, D), (FF // 2) ** -0.5, 0.15625, ((0, 32),))
    b_outer = bell_draw(key_of[15], (D,), 0.5, 3.0, ((0, 32),))
    gain_two = jnp.clip(1.0 + 0.15 * jax.random.normal(key_of[16], (D,), jnp.float32), 0.25, 1.75).astype(jnp.bfloat16)
    shift_two = bell_draw(key_of[17], (D,), 0.5, 3.0, ((0, 32),))
    return dict(tokens=tokens, lengths=lengths, cotangent=cotangent, w_query=w_query, b_query=b_query, w_key=w_key, w_value=w_value, b_value=b_value, w_out=w_out, b_out=b_out, gain_one=gain_one, shift_one=shift_one, w_inner=w_inner, b_inner=b_inner, w_outer=w_outer, b_outer=b_outer, gain_two=gain_two, shift_two=shift_two)


NEG_BIG = -1000000000.0
EPSILON = 1e-05
HIGH = lax.Precision.HIGHEST

@jax.custom_vjp
def low(v):
    return lax.optimization_barrier(v.astype(jnp.bfloat16)).astype(jnp.float32)

@jax.custom_vjp
def low_back(v):
    return v

def low_keep(v):
    return (low(v), None)

def low_pass(kept, grad):
    return (grad,)

def back_keep(v):
    return (v, None)

def back_low(kept, grad):
    return (low(grad),)
low.defvjp(low_keep, low_pass)
low_back.defvjp(back_keep, back_low)

def matmul(left, right):
    return jnp.dot(left, right, precision=HIGH)

def normalize(values, gain, shift):
    center = values - lax.optimization_barrier(jnp.mean(values, axis=-1, keepdims=True))
    spread = lax.optimization_barrier(jnp.mean(center * center, axis=-1, keepdims=True))
    return center * lax.rsqrt(spread + EPSILON) * gain + shift

def gelu_exact(values):
    return 0.5 * values * (1.0 + jax.scipy.special.erf(values * 0.7071067811865476))

def block_forward(params, rows_in, lens):
    w_query, b_query, w_key, w_value, b_value, w_out, b_out, gain_one, shift_one, w_inner, b_inner, w_outer, b_outer, gain_two, shift_two = params
    count = lens.shape[0]
    flat = rows_in.reshape(count * LEN, D)
    queries = low(low_back(matmul(flat, w_query) + b_query))
    keys = low(low_back(matmul(flat, w_key)))
    values = low(low_back(matmul(flat, w_value) + b_value))
    shape_four = (count, LEN, HEADS, HEAD_DIM)
    scores = jnp.einsum('bqhd,bkhd->bhqk', queries.reshape(shape_four), keys.reshape(shape_four), precision=HIGH)
    scores = low_back(scores * HEAD_DIM ** (-0.5))
    visible = (jnp.arange(LEN)[None, :] < lens[:, None])[:, None, None, :]
    masked = jnp.where(visible, scores, NEG_BIG)
    shifted = masked - lax.optimization_barrier(jnp.max(masked, axis=-1, keepdims=True))
    weights = jnp.exp(shifted)
    probs = low(weights / lax.optimization_barrier(jnp.sum(weights, axis=-1, keepdims=True)))
    context = jnp.einsum('bhqk,bkhd->bqhd', probs, values.reshape(shape_four), precision=HIGH)
    context = low(low_back(context.reshape(count * LEN, D)))
    attn_out = low_back(matmul(context, w_out) + b_out)
    hidden = normalize(flat + attn_out, gain_one, shift_one)
    inner = low_back(matmul(low(hidden), w_inner) + b_inner)
    active = low(gelu_exact(inner))
    outer = low_back(matmul(active, w_outer) + b_outer)
    output = normalize(hidden + outer, gain_two, shift_two)
    return output.reshape(count, LEN, D)

def reference(tokens, lengths, cotangent, w_query, b_query, w_key, w_value, b_value, w_out, b_out, gain_one, shift_one, w_inner, b_inner, w_outer, b_outer, gain_two, shift_two):
    params = (w_query.astype(jnp.float32), b_query.astype(jnp.float32), w_key.astype(jnp.float32), w_value.astype(jnp.float32), b_value.astype(jnp.float32), w_out.astype(jnp.float32), b_out.astype(jnp.float32), gain_one.astype(jnp.float32), shift_one.astype(jnp.float32), w_inner.astype(jnp.float32), b_inner.astype(jnp.float32), w_outer.astype(jnp.float32), b_outer.astype(jnp.float32), gain_two.astype(jnp.float32), shift_two.astype(jnp.float32))
    per_block = 4
    blocks = SEQS // per_block
    positions = jnp.arange(LEN)

    def one_block(totals, items):
        tok_blk, len_blk, cot_blk = items

        def forward(weights_in, rows_in):
            return block_forward(weights_in, rows_in, len_blk)
        result, pullback = jax.vjp(forward, params, tok_blk.astype(jnp.float32))
        live = (positions[None, :] < len_blk[:, None]).astype(jnp.float32)[:, :, None]
        grads, grad_in = pullback(cot_blk.astype(jnp.float32) * live)
        totals = jax.tree.map(lambda running, fresh: running + fresh, totals, grads)
        return (totals, (result, grad_in))
    zeros = jax.tree.map(jnp.zeros_like, params)
    items = (tokens.reshape(blocks, per_block, LEN, D), lengths.reshape(blocks, per_block), cotangent.reshape(blocks, per_block, LEN, D))
    totals, (outputs, grad_in) = lax.scan(one_block, zeros, items)
    g_query, gb_query, g_key, g_value, gb_value, g_out, gb_out, gg_one, gs_one, g_inner, gb_inner, g_outer, gb_outer, gg_two, gs_two = totals
    return (outputs.reshape(SEQS, LEN, D), grad_in.reshape(SEQS, LEN, D), g_query, gb_query, g_key, g_value, gb_value, g_out, gb_out, gg_one, gs_one, g_inner, gb_inner, g_outer, gb_outer, gg_two, gs_two)
```

```python
import jax
import jax.numpy as jnp
from jax import lax
from jax.experimental import pallas as pl
from jax.experimental.pallas import tpu as pltpu
from jax.sharding import PartitionSpec as P

HEAD_DIM = 64
PAIR = 2 * HEAD_DIM
NEG_BIG = -1000000000.0
EPSILON = 1e-05
ROOT_HALF = 0.7071067811865476
INV_ROOT_TAU = 0.3989422804014327
BF = jnp.bfloat16
F32 = jnp.float32


def product(left, right):
    return jnp.dot(left, right, preferred_element_type=F32)


def product_tn(left, right):
    return lax.dot_general(left, right, (((0,), (0,)), ((), ())), preferred_element_type=F32)


def product_nt(left, right):
    return lax.dot_general(left, right, (((1,), (1,)), ((), ())), preferred_element_type=F32)


def column_sum(values):
    return jnp.sum(values, axis=0, dtype=F32)


def normalize_keep(values, gain, shift):
    center = values - jnp.mean(values, axis=-1, keepdims=True)
    inv_spread = lax.rsqrt(jnp.mean(center * center, axis=-1, keepdims=True) + EPSILON)
    normed = center * inv_spread
    return (normed * gain + shift, normed, inv_spread)


def normalize_back(grad_out, normed, inv_spread, gain):
    grad_normed = grad_out * gain
    centered = grad_normed - jnp.mean(grad_normed, axis=-1, keepdims=True)
    grad_in = inv_spread * (
        centered - normed * jnp.mean(grad_normed * normed, axis=-1, keepdims=True)
    )
    return (grad_in, jnp.sum(grad_out * normed, axis=0), jnp.sum(grad_out, axis=0))


def attend_kernel(len_ref, q_ref, k_ref, v_ref, out_ref, lse_ref):
    count = len_ref[pl.program_id(0)]
    queries = q_ref[...] * BF(HEAD_DIM ** (-0.5))
    keys = k_ref[...]
    values_t = v_ref[...].T
    length = keys.shape[0]
    lane = lax.broadcasted_iota(jnp.int32, keys.shape, 1)
    seen = lax.broadcasted_iota(jnp.int32, (length, length), 0) < count
    parts = []
    for head in range(2):
        own = (lane >= head * HEAD_DIM) & (lane < (head + 1) * HEAD_DIM)
        scores = product_nt(jnp.where(own, keys, BF(0)), queries)
        scores = jnp.where(seen, scores, NEG_BIG)
        top = jnp.max(scores, axis=0, keepdims=True)
        weights = jnp.exp(scores - top)
        total = jnp.sum(weights, axis=0, keepdims=True)
        probs = (weights * (1.0 / total)).astype(BF)
        parts.append(product(values_t[head * HEAD_DIM : (head + 1) * HEAD_DIM], probs))
        lse_ref[0, 0, head : head + 1, :] = top + jnp.log(total)
    out_ref[...] = jnp.concatenate(parts, axis=0).T.astype(BF)


def attend_back_kernel(len_ref, q_ref, k_ref, v_ref, g_ref, lse_ref, dq_ref, dk_ref, dv_ref):
    count = len_ref[pl.program_id(0)]
    scale = BF(HEAD_DIM ** (-0.5))
    queries = q_ref[...] * scale
    keys = k_ref[...]
    values = v_ref[...]
    grad = g_ref[...]
    keys_t = (keys * scale).T
    length = keys.shape[0]
    lane = lax.broadcasted_iota(jnp.int32, keys.shape, 1)
    seen = lax.broadcasted_iota(jnp.int32, (length, length), 0) < count
    dq, dk, dv = [], [], []
    for head in range(2):
        own = (lane >= head * HEAD_DIM) & (lane < (head + 1) * HEAD_DIM)
        scores = product_nt(jnp.where(own, keys, BF(0)), queries)
        scores = jnp.where(seen, scores, NEG_BIG)
        probs = jnp.exp(scores - lse_ref[0, 0, head : head + 1, :])
        grad_probs = product_nt(jnp.where(own, values, BF(0)), grad)
        row_term = jnp.sum(probs * grad_probs, axis=0, keepdims=True)
        grad_scores = (probs * (grad_probs - row_term)).astype(BF)
        dv.append(product(probs.astype(BF), grad))
        dk.append(product(grad_scores, queries))
        dq.append(product(keys_t[head * HEAD_DIM : (head + 1) * HEAD_DIM], grad_scores))
    first = lane < HEAD_DIM
    dv_ref[...] = jnp.where(first, dv[0], dv[1]).astype(BF)
    dk_ref[...] = jnp.where(first, dk[0], dk[1]).astype(BF)
    dq_ref[...] = jnp.concatenate(dq, axis=0).T.astype(BF)


def attention_specs(length, pairs):
    def at(offset):
        return pl.BlockSpec((length, PAIR), lambda s, p, n: (s, offset + p))

    lse = pl.BlockSpec((1, 1, 2, length), lambda s, p, n: (s, p, 0, 0))
    return at, lse


def attend(lengths, query_key, values, length):
    rows, width = values.shape
    pairs = width // PAIR
    seqs = rows // length
    at, lse = attention_specs(length, pairs)
    return pl.pallas_call(
        attend_kernel,
        out_shape=(
            jax.ShapeDtypeStruct((rows, width), BF),
            jax.ShapeDtypeStruct((seqs, pairs, 2, length), F32),
        ),
        grid_spec=pltpu.PrefetchScalarGridSpec(
            num_scalar_prefetch=1,
            grid=(seqs, pairs),
            in_specs=[at(0), at(pairs), at(0)],
            out_specs=(at(0), lse),
        ),
        compiler_params=pltpu.CompilerParams(vmem_limit_bytes=32 << 20),
        cost_estimate=pl.CostEstimate(
            flops=4 * rows * length * width,
            transcendentals=rows * length * width // HEAD_DIM,
            bytes_accessed=8 * rows * width,
        ),
        name="attend",
    )(lengths, query_key, query_key, values)


def attend_back(lengths, query_key, values, grad, lse_all, length):
    rows, width = values.shape
    pairs = width // PAIR
    seqs = rows // length
    at, lse = attention_specs(length, pairs)
    shape = jax.ShapeDtypeStruct((rows, width), BF)
    return pl.pallas_call(
        attend_back_kernel,
        out_shape=(shape, shape, shape),
        grid_spec=pltpu.PrefetchScalarGridSpec(
            num_scalar_prefetch=1,
            grid=(seqs, pairs),
            in_specs=[at(0), at(pairs), at(0), at(0), lse],
            out_specs=(at(0), at(0), at(0)),
        ),
        compiler_params=pltpu.CompilerParams(vmem_limit_bytes=32 << 20),
        cost_estimate=pl.CostEstimate(
            flops=10 * rows * length * width,
            transcendentals=rows * length * width // HEAD_DIM,
            bytes_accessed=14 * rows * width,
        ),
        name="attend_back",
    )(lengths, query_key, query_key, values, grad, lse_all)


class Wires:
    def __init__(self):
        self.chips = lax.axis_size("dp")
        self.bits = self.chips.bit_length() - 1
        self.chip = lax.axis_index("dp")
        self.core = lax.axis_index("seq")

    def side(self, bit):
        return (self.chip >> bit) & 1

    def swap(self, values, bit):
        return lax.ppermute(values, "dp", [(i, i ^ (1 << bit)) for i in range(self.chips)])

    def swap_core(self, values):
        return lax.ppermute(values, "seq", [(0, 1), (1, 0)])

    def beside(self, mine, theirs, side, axis):
        shape = [1] * (mine.ndim + 1)
        shape[axis] = 2
        here = jnp.arange(2).reshape(shape) == side
        return jnp.where(here, jnp.expand_dims(mine, axis), jnp.expand_dims(theirs, axis))

    def orders(self):
        far = list(range(self.bits - 1, -1, -1))
        return far, far[:-2] + [far[-1], far[-2]]

    def gather(self, values, order, flip=None):
        held = []
        for bit in order:
            other = self.swap(values, bit)
            axis = sum(1 for one in held if one > bit)
            side = self.side(bit)
            if flip is not None and bit == self.bits - 1:
                side = side ^ flip
            values = self.beside(values, other, side, axis)
            held.append(bit)
        return values.reshape(-1, values.shape[-1])

    def scatter(self, values, order, flip=None):
        left = list(range(self.bits - 1, -1, -1))
        values = values.reshape([2] * self.bits + [-1, values.shape[-1]])
        for step, bit in enumerate(reversed(order)):
            axis = left.index(bit)
            left.remove(bit)
            side = self.side(bit)
            if flip is not None and bit == self.bits - 1:
                side = side ^ flip
            away = lax.dynamic_index_in_dim(values, 1 - side, axis, keepdims=False)
            keep = lax.dynamic_index_in_dim(values, side, axis, keepdims=False)
            other = self.swap(away.astype(BF), bit)
            values = keep.astype(F32) + other.astype(F32)
            if left:
                values = values.astype(BF)
        return values

    def halves(self, shard):
        rows, width = shard.shape
        split = shard.reshape(rows, 2, width // 2)
        mine = lax.dynamic_index_in_dim(split, self.core, 1, keepdims=False)
        away = lax.dynamic_index_in_dim(split, 1 - self.core, 1, keepdims=False)
        return mine, away

    def paired(self, mine, theirs):
        return self.beside(mine, theirs, self.core, 0).reshape(-1, mine.shape[-1])

    def unpaired(self, block):
        split = block.reshape(2, -1, block.shape[-1])
        mine = lax.dynamic_index_in_dim(split, self.core, 0, keepdims=False)
        away = lax.dynamic_index_in_dim(split, 1 - self.core, 0, keepdims=False)
        theirs = self.swap_core(away)
        return self.beside(mine, theirs, self.core, 1).reshape(mine.shape[0], -1)

    def total(self, values):
        values = values + self.swap_core(values)
        for bit in range(self.bits):
            values = values + self.swap(values, bit)
        return values


def body(
    tokens,
    lengths,
    cotangent,
    w_query,
    b_query,
    w_key,
    w_value,
    b_value,
    w_out,
    b_out,
    gain_one,
    shift_one,
    w_inner,
    b_inner,
    w_outer,
    b_outer,
    gain_two,
    shift_two,
):
    wires = Wires()
    core = wires.core
    devices = 2 * wires.chips
    device = 2 * wires.chip + core
    seqs, half, width = tokens.shape
    length = 2 * half
    rows = seqs * half
    order_one, order_two = wires.orders()

    vectors = (b_query, b_value, b_out, gain_one, shift_one, b_outer, gain_two, shift_two)
    slot = b_query.shape[0]
    inner_slot = b_inner.shape[0]
    packed = jnp.concatenate(vectors + (b_inner,))
    packed = jnp.pad(packed, (0, -packed.shape[0] % 128))
    own_row = jnp.arange(devices)[:, None] == device
    packed = wires.total(jnp.where(own_row, packed[None, :], BF(0)))
    spread = [
        packed[:, i * slot : (i + 1) * slot].reshape(1, width).astype(F32)
        for i in range(len(vectors))
    ]
    bias_query, bias_value, bias_out, gain_a, shift_a, bias_outer, gain_b, shift_b = spread
    bias_inner = packed[:, len(vectors) * slot : len(vectors) * slot + inner_slot]
    bias_inner = bias_inner.reshape(1, -1).astype(F32)

    q_mine, q_away = wires.halves(w_query)
    k_mine, k_away = wires.halves(w_key)
    v_mine, v_away = wires.halves(w_value)
    first = jnp.concatenate([q_mine, k_mine, v_mine], axis=1)
    first_away = jnp.concatenate([q_away, k_away, v_away], axis=1)
    first = wires.paired(first, wires.swap_core(first_away))
    cols = width // 2
    w_qk = wires.gather(first[:, : 2 * cols], order_one)
    w_v = wires.gather(first[:, 2 * cols :], order_two)

    o_mine, o_away = wires.halves(w_out)
    w_out_mine = wires.gather(wires.paired(o_mine, wires.swap_core(o_away)), order_two)
    i_mine, i_away = wires.halves(w_inner)
    w_inner_mine = wires.gather(wires.paired(i_mine, wires.swap_core(i_away)), order_one)
    u_mine, u_away = wires.halves(w_outer)
    w_outer_mine = wires.gather(wires.paired(u_mine, wires.swap_core(u_away)), order_two, flip=core)
    w_out_theirs = wires.swap_core(w_out_mine)
    w_inner_theirs = wires.swap_core(w_inner_mine)
    hidden_units = w_inner_mine.shape[1] * 2
    outer_theirs = wires.swap_core(w_outer_mine)
    w_outer_theirs = jnp.concatenate(
        [outer_theirs[hidden_units // 2 :], outer_theirs[: hidden_units // 2]], axis=0
    )

    def natural(mine, theirs):
        return wires.beside(mine, theirs, core, 1).reshape(mine.shape[0], -1)

    def own_columns(values):
        split = values.reshape(values.shape[0], 2, -1)
        mine = lax.dynamic_index_in_dim(split, core, 1, keepdims=False)
        theirs = lax.dynamic_index_in_dim(split, 1 - core, 1, keepdims=False)
        return mine, theirs

    def all_positions(mine):
        theirs = wires.swap_core(mine)
        return wires.beside(mine, theirs, core, 1).reshape(seqs * length, -1)

    def split_positions(values):
        split = values.reshape(seqs, 2, half, -1)
        mine = lax.dynamic_index_in_dim(split, core, 1, keepdims=False)
        away = lax.dynamic_index_in_dim(split, 1 - core, 1, keepdims=False)
        return mine, away

    tok_rows = tokens.reshape(rows, width)
    tok_all = all_positions(tokens)
    bias_q, _ = own_columns(bias_query)
    bias_v, _ = own_columns(bias_value)
    bias_qk = jnp.concatenate([bias_q, jnp.zeros_like(bias_q)], axis=1)
    query_key = (product(tok_all, w_qk) + bias_qk).astype(BF)
    values = (product(tok_all, w_v) + bias_v).astype(BF)
    context_heads, lse = attend(lengths, query_key, values, length)
    ctx_mine, ctx_away = split_positions(context_heads)
    ctx_theirs = wires.swap_core(ctx_away)
    context = natural(ctx_mine.reshape(rows, -1), ctx_theirs.reshape(rows, -1))
    attn_out = natural(product(context, w_out_mine), product(context, w_out_theirs)) + bias_out
    hidden, normed_one, inv_one = normalize_keep(tok_rows.astype(F32) + attn_out, gain_a, shift_a)
    hidden_low = hidden.astype(BF)
    bias_in = own_columns(bias_inner)
    inner, active, slope = [], [], []
    for weight, bias in zip((w_inner_mine, w_inner_theirs), bias_in):
        pre = product(hidden_low, weight) + bias
        cumulative = 0.5 * (1.0 + lax.erf(pre * ROOT_HALF))
        active.append((pre * cumulative).astype(BF))
        slope.append((cumulative + pre * jnp.exp(-0.5 * pre * pre) * INV_ROOT_TAU).astype(BF))
    active = jnp.concatenate(active, axis=1)
    outer = natural(product(active, w_outer_mine), product(active, w_outer_theirs)) + bias_outer
    output, normed_two, inv_two = normalize_keep(hidden + outer, gain_b, shift_b)

    positions = core * half + jnp.arange(half, dtype=jnp.int32)
    live = (positions[None, :] < lengths[:, None]).astype(F32).reshape(rows, 1)
    grad_y = cotangent.reshape(rows, width).astype(F32) * live
    grad_resid_two, grad_gain_two, grad_shift_two = normalize_back(
        grad_y, normed_two, inv_two, gain_b
    )
    grad_outer = grad_resid_two.astype(BF)
    grad_b_outer = column_sum(grad_outer)
    go_mine, go_theirs = own_columns(grad_outer)
    g_outer = product_tn(active, go_mine).astype(BF)
    g_outer_away = product_tn(active, go_theirs).astype(BF)
    g_outer_away = jnp.concatenate(
        [g_outer_away[hidden_units // 2 :], g_outer_away[: hidden_units // 2]], axis=0
    )
    g_outer = g_outer.astype(F32) + wires.swap_core(g_outer_away).astype(F32)
    g_outer = wires.scatter(g_outer.astype(BF), order_two, flip=core)

    grad_active = product_nt(go_mine, w_outer_mine) + product_nt(go_theirs, w_outer_theirs)
    part = hidden_units // 2
    grad_inner = [
        (grad_active[:, i * part : (i + 1) * part] * slope[i].astype(F32)).astype(BF)
        for i in range(2)
    ]
    sums_inner = [column_sum(one) for one in grad_inner]
    grad_b_inner = natural(sums_inner[0][None], sums_inner[1][None]).reshape(-1)
    g_inner_away = wires.swap_core(product_tn(hidden_low, grad_inner[1]).astype(BF))
    g_inner = product_tn(hidden_low, grad_inner[0]).astype(BF)
    g_inner = g_inner.astype(F32) + g_inner_away.astype(F32)
    g_inner = wires.scatter(g_inner.astype(BF), order_one)

    grad_hidden = (
        grad_resid_two
        + product_nt(grad_inner[0], w_inner_mine)
        + product_nt(grad_inner[1], w_inner_theirs)
    )
    grad_resid_one, grad_gain_one, grad_shift_one = normalize_back(
        grad_hidden, normed_one, inv_one, gain_a
    )
    grad_attn = grad_resid_one.astype(BF)
    grad_b_out = column_sum(grad_attn)
    ga_mine, ga_theirs = own_columns(grad_attn)
    grad_context = product_nt(ga_mine, w_out_mine) + product_nt(ga_theirs, w_out_theirs)
    gc_mine, gc_theirs = own_columns(grad_context.astype(BF))
    gc_other = wires.swap_core(gc_theirs)
    grad_heads = wires.beside(
        gc_mine.reshape(seqs, half, -1), gc_other.reshape(seqs, half, -1), core, 1
    ).reshape(seqs * length, -1)
    g_out_away = wires.swap_core(product_tn(context, ga_theirs).astype(BF))
    g_out = product_tn(context, ga_mine).astype(BF)
    g_out = g_out.astype(F32) + g_out_away.astype(F32)
    g_out = wires.scatter(g_out.astype(BF), order_two)

    dq, dk, dv = attend_back(lengths, query_key, values, grad_heads, lse, length)
    g_qk = jnp.concatenate(
        [product_tn(tok_all, dq).astype(BF), product_tn(tok_all, dk).astype(BF)], axis=1
    )
    g_qk = wires.scatter(g_qk, order_one)
    g_v = wires.scatter(product_tn(tok_all, dv).astype(BF), order_two)

    zero = jnp.zeros((cols,), F32)
    sum_q = natural_half(column_sum(dq), zero, core)
    sum_v = natural_half(column_sum(dv), zero, core)
    sums = jnp.stack(
        [
            sum_q,
            sum_v,
            grad_b_out,
            grad_gain_one,
            grad_shift_one,
            grad_b_outer,
            grad_gain_two,
            grad_shift_two,
        ]
    )
    sums = jnp.concatenate([sums, grad_b_inner.reshape(-1, width)], axis=0)
    sums = wires.total(sums)
    small = lax.dynamic_index_in_dim(
        sums[: len(vectors)].reshape(len(vectors), devices, slot), device, 1, keepdims=False
    )
    small_inner = lax.dynamic_index_in_dim(
        sums[len(vectors) :].reshape(devices, inner_slot), device, 0, keepdims=False
    )

    partial = (
        product_nt(dq, w_qk[:, :cols]) + product_nt(dk, w_qk[:, cols:]) + product_nt(dv, w_v)
    )
    part_mine, part_away = split_positions(partial)
    part_theirs = wires.swap_core(part_away.astype(BF))
    grad_tok = (
        grad_resid_one
        + part_mine.reshape(rows, width)
        + part_theirs.reshape(rows, width).astype(F32)
    )

    w_cols = jnp.concatenate([g_qk, g_v, g_out, g_inner], axis=1)
    w_grads = wires.unpaired(w_cols)
    at = [0, cols, 2 * cols, 3 * cols, 4 * cols, 4 * cols + part]
    w_grads = w_grads.reshape(slot, 2, -1)
    pieces = [w_grads[:, :, at[i] : at[i + 1]].reshape(slot, -1) for i in range(5)]
    outer_grad = wires.unpaired(g_outer)

    return (
        output.reshape(seqs, half, width),
        grad_tok.reshape(seqs, half, width),
        pieces[0],
        small[0],
        pieces[1],
        pieces[2],
        small[1],
        pieces[3],
        small[2],
        small[3],
        small[4],
        pieces[4],
        small_inner,
        outer_grad,
        small[5],
        small[6],
        small[7],
    )


def natural_half(mine, zero, core):
    here = jnp.arange(2)[:, None] == core
    return jnp.where(here, mine[None], zero[None]).reshape(-1)


def solution(mesh):
    every = ("dp", "seq")
    matrix, vector = P(every, None), P(every)
    rows = P("dp", "seq", None)
    kinds = (matrix, vector, matrix, matrix, vector, matrix, vector, vector, vector, matrix, vector, matrix, vector, vector, vector)
    return jax.shard_map(
        body,
        mesh=mesh,
        in_specs=(rows, P("dp"), rows) + kinds,
        out_specs=(rows, rows) + kinds,
        check_vma=False,
    )
```

```python
import functools

import jax
import jax.numpy as jnp
from jax import lax
from jax.experimental import pallas as pl
from jax.experimental.pallas import tpu as pltpu
from jax.sharding import Mesh
from jax.sharding import PartitionSpec as P

HEAD_DIM = 64
PAIR = 2 * HEAD_DIM
LANES = 128
NEG_BIG = -1000000000.0
EPSILON = 1e-05
ROOT_HALF = 0.7071067811865476
INV_ROOT_TAU = 0.3989422804014327
BF = jnp.bfloat16
CHIPS = ("far", "mid", "low")
F32 = jnp.float32
VMEM_LIMIT = 20 << 20
SMALL = pl.CostEstimate(flops=1024, transcendentals=0, bytes_accessed=1024)

B_QUERY, B_VALUE, B_OUT, GAIN_ONE, SHIFT_ONE, B_OUTER, GAIN_TWO, SHIFT_TWO, B_INNER = range(9)
TABLE = 16


def product(left, right):
    return jnp.dot(left, right, preferred_element_type=F32)


def product_tn(left, right):
    return lax.dot_general(left, right, (((0,), (0,)), ((), ())), preferred_element_type=F32)


def product_nt(left, right):
    return lax.dot_general(left, right, (((1,), (1,)), ((), ())), preferred_element_type=F32)


def ordered(first, mine, theirs, axis):
    return jnp.concatenate([jnp.where(first, mine, theirs), jnp.where(first, theirs, mine)], axis)


def row_mean(values):
    return jnp.mean(values, axis=-1, keepdims=True)


def normalize(values):
    center = values - row_mean(values)
    inv_spread = lax.rsqrt(row_mean(center * center) + EPSILON)
    return center * inv_spread, inv_spread


def normalize_back(grad_out, normed, inv_spread, gain):
    grad_normed = grad_out * gain
    centered = grad_normed - row_mean(grad_normed)
    return inv_spread * (centered - normed * row_mean(grad_normed * normed))


def column_sums(*values):
    rows = [jnp.sum(one.astype(F32), axis=0, keepdims=True) for one in values]
    pad = jnp.zeros((8 - len(rows), rows[0].shape[1]), F32)
    return jnp.concatenate(rows + [pad], axis=0)


def attend_kernel(count, where_ref, len_ref, mine_ref, theirs_ref, *refs):
    held = (refs[:count], refs[count : 2 * count])
    qkv_ref, ctx_mine_ref, ctx_theirs_ref, lse_ref, weight_ref, table_ref = refs[2 * count :]
    core = where_ref[0]
    first = core == 0
    seen_to = len_ref[pl.program_id(0)]
    width = weight_ref.shape[0]
    cols = width // 2

    @pl.when(pl.program_id(0) == 0)
    def _():
        start = 0
        for stream, pieces in enumerate(held):
            side = where_ref[3 + stream]
            extent = pieces[0].shape[-1]
            fill(weight_ref.at[:, start : start + extent], pieces, (side, 1 - side))
            start += extent
        last = weight_ref.shape[1] - LANES
        chosen = lax.broadcasted_iota(jnp.int32, (TABLE, LANES), 0)
        chosen = chosen == lax.broadcasted_iota(jnp.int32, (TABLE, LANES), 1)
        table_ref[...] = product_nt(
            jnp.where(chosen, 1.0, 0.0).astype(BF), weight_ref[:, last:]
        )

    def own(row):
        return jnp.where(first, table_ref[row : row + 1, :cols], table_ref[row : row + 1, cols:])

    seq = pl.program_id(0)
    tokens = ordered(first, mine_ref[seq], theirs_ref[seq], 0)
    length = tokens.shape[0]
    all_rows, half_rows = span(seq, length), span(seq, length // 2)
    bias_q, bias_v = own(B_QUERY), own(B_VALUE)
    seen = lax.broadcasted_iota(jnp.int32, (length, length), 0) < seen_to
    lane = lax.broadcasted_iota(jnp.int32, (length, PAIR), 1)
    for pair in range(cols // PAIR):
        lanes = slice(pair * PAIR, (pair + 1) * PAIR)
        project = product(tokens, weight_ref[:, 3 * pair * PAIR : 3 * (pair + 1) * PAIR])
        queries = (project[:, :PAIR] + bias_q[:, lanes]).astype(BF)
        keys = project[:, PAIR : 2 * PAIR].astype(BF)
        values = (project[:, 2 * PAIR :] + bias_v[:, lanes]).astype(BF)
        qkv_ref[all_rows, 3 * pair * PAIR : 3 * (pair + 1) * PAIR] = jnp.concatenate(
            [queries, keys, values], axis=1
        )
        queries = queries * BF(HEAD_DIM ** (-0.5))
        values_t = values.T
        parts = []
        for head in range(2):
            mask = (lane >= head * HEAD_DIM) & (lane < (head + 1) * HEAD_DIM)
            scores = product_nt(jnp.where(mask, keys, BF(0)), queries)
            scores = jnp.where(seen, scores, NEG_BIG)
            top = jnp.max(scores, axis=0, keepdims=True)
            weights = jnp.exp(scores - top)
            total = jnp.sum(weights, axis=0, keepdims=True)
            probs = (weights * (1.0 / total)).astype(BF)
            parts.append(product(values_t[head * HEAD_DIM : (head + 1) * HEAD_DIM], probs))
            row = 2 * pair + head
            lse_ref[seq, row : row + 1, :] = top + jnp.log(total)
        context = jnp.concatenate(parts, axis=0).T.astype(BF)
        low, high = context[: length // 2], context[length // 2 :]
        ctx_mine_ref[half_rows, lanes] = jnp.where(first, low, high)
        ctx_theirs_ref[half_rows, lanes] = jnp.where(first, high, low)


def attend_back_kernel(pair, extras, where_ref, len_ref, qkv_ref, mine_ref, theirs_ref, lse_ref, tok_ref, *refs):
    held, refs = refs[:extras], refs[extras:]
    grad_ref, sums_ref, weight_refs, total_ref = refs[0], refs[1], refs[2:-1], refs[-1]
    seq = pl.program_id(0)
    first = where_ref[0] == 0
    seen_to = len_ref[seq]
    scale = BF(HEAD_DIM ** (-0.5))
    length = qkv_ref.shape[0] // len_ref.shape[0]
    rows, half_rows = span(seq, length), span(seq, length // 2)
    start = 3 * pair * PAIR
    queries = qkv_ref[rows, start : start + PAIR] * scale
    keys = qkv_ref[rows, start + PAIR : start + 2 * PAIR]
    values = qkv_ref[rows, start + 2 * PAIR : start + 3 * PAIR]
    lanes = slice(pair * PAIR, (pair + 1) * PAIR)
    grad = ordered(first, mine_ref[half_rows, lanes], theirs_ref[half_rows, lanes], 0)
    keys_t = (keys * scale).T
    lane = lax.broadcasted_iota(jnp.int32, keys.shape, 1)
    seen = lax.broadcasted_iota(jnp.int32, (length, length), 0) < seen_to
    dq, dk, dv = [], [], []
    for head in range(2):
        own = (lane >= head * HEAD_DIM) & (lane < (head + 1) * HEAD_DIM)
        scores = product_nt(jnp.where(own, keys, BF(0)), queries)
        scores = jnp.where(seen, scores, NEG_BIG)
        row = 2 * pair + head
        probs = jnp.exp(scores - lse_ref[seq, row : row + 1, :])
        grad_probs = product_nt(jnp.where(own, values, BF(0)), grad)
        row_term = jnp.sum(probs * grad_probs, axis=0, keepdims=True)
        grad_scores = (probs * (grad_probs - row_term)).astype(BF)
        dv.append(product(probs.astype(BF), grad))
        dk.append(product(grad_scores, queries))
        dq.append(product(keys_t[head * HEAD_DIM : (head + 1) * HEAD_DIM], grad_scores))
    own = lane < HEAD_DIM
    all_three = [
        jnp.concatenate(dq, axis=0).T.astype(BF),
        jnp.where(own, dk[0], dk[1]).astype(BF),
        jnp.where(own, dv[0], dv[1]).astype(BF),
    ]
    grads = jnp.concatenate(all_three, axis=1)
    grad_ref[rows, :] = grads
    sums = jnp.sum(grads.astype(F32), axis=0, keepdims=True)
    weight = product(tok_ref[rows, :].T, grads)

    @pl.when(seq == 0)
    def _():
        sums_ref[...] = sums
        total_ref[...] = weight

    @pl.when(seq > 0)
    def _():
        sums_ref[...] += sums
        total_ref[...] += weight

    @pl.when(seq == pl.num_programs(0) - 1)
    def _():
        found = total_ref[...].astype(BF)
        extent = found.shape[1]
        if pair == 0:
            weight_refs[0][...] = found
        elif extras == 1:
            more = weight_refs[0].shape[1] - extent
            weight_refs[0][:, :extent] = held[0][...]
            weight_refs[0][:, extent:] = found[:, :more]
            weight_refs[1][...] = found[:, more:]
        else:
            kept = held[0].shape[1]
            weight_refs[0][:, :kept] = held[0][...]
            weight_refs[0][:, kept : kept + extent] = found
            many = [one[...] for one in held[2:]] + [sums_ref[...]]
            blank = jnp.zeros((1, many[0].shape[1] // 3 * len(many)), F32)
            table = held[1][...]
            place = lax.broadcasted_iota(jnp.int32, table.shape, 0)
            for number, begin in ((B_QUERY, 0), (B_VALUE, 2 * PAIR)):
                row = jnp.concatenate([one[:, begin : begin + PAIR] for one in many], axis=1)
                row = jnp.concatenate(
                    [jnp.where(first, row, blank), jnp.where(first, blank, row)], axis=1
                )
                table = jnp.where(place == number, row, table)
            chosen = lax.broadcasted_iota(jnp.int32, (TABLE, LANES), 0)
            chosen = chosen == lax.broadcasted_iota(jnp.int32, (TABLE, LANES), 1)
            weight_refs[0][:, kept + extent :] = product_tn(
                table.astype(BF), jnp.where(chosen, 1.0, 0.0).astype(BF)
            ).astype(BF)


def attend(where, lengths, mine, theirs, pieces_one, pieces_two):
    seqs, half, width = mine.shape
    length = 2 * half
    cols = width // 2
    total = pieces_one[0].shape[-1] + pieces_two[0].shape[-1]
    return run(
        functools.partial(attend_kernel, len(pieces_one)),
        "attend",
        (where, lengths),
        (mine, theirs, *pieces_one, *pieces_two),
        (
            ((seqs * length, 3 * cols), BF),
            ((seqs * half, cols), BF),
            ((seqs * half, cols), BF),
            ((seqs, cols // HEAD_DIM, length), F32),
            ((width, total), BF),
            ((TABLE, width), F32),
        ),
        grid=(seqs,),
    )


def attend_back(pair, where, lengths, qkv, mine, theirs, lse_all, tokens, held, widths):
    width = tokens.shape[1]
    return run(
        functools.partial(attend_back_kernel, pair, len(held)),
        "attend_back",
        (where, lengths),
        (qkv, mine, theirs, lse_all, tokens, *held),
        (((qkv.shape[0], 3 * PAIR), BF), ((1, 3 * PAIR), F32))
        + tuple(((width, one), BF) for one in widths),
        grid=lengths.shape,
        scratch=[pltpu.VMEM((width, 3 * PAIR), F32)],
    )


def on_chip(count):
    return [pl.BlockSpec(memory_space=pltpu.VMEM)] * count


def run(kernel, name, scalars, arrays, outs, grid=(1,), scratch=()):
    return pl.pallas_call(
        kernel,
        out_shape=tuple(jax.ShapeDtypeStruct(shape, kind) for shape, kind in outs),
        grid_spec=pltpu.PrefetchScalarGridSpec(
            num_scalar_prefetch=len(scalars),
            grid=grid,
            in_specs=on_chip(len(arrays)),
            out_specs=tuple(on_chip(len(outs))),
            scratch_shapes=scratch,
        ),
        compiler_params=pltpu.CompilerParams(vmem_limit_bytes=VMEM_LIMIT),
        cost_estimate=SMALL,
        name=name,
    )(*scalars, *arrays)


def span(step, extent):
    if isinstance(step, int):
        return pl.ds(step * extent, extent)
    return pl.ds(pl.multiple_of(step * extent, extent), extent)


def fill(target, pieces, sides):
    for piece, side in zip(pieces, sides):
        blocks, rows, _ = piece.shape
        for block in range(blocks):
            start = block * len(pieces) * rows
            if len(pieces) > 1:
                start = pl.multiple_of(start + side * rows, rows)
            target[pl.ds(start, rows), :] = piece[block]


class Layout:
    def __init__(self, chips, width, units):
        self.chips, self.width, self.units = chips, width, units
        self.cols = width // 2
        self.rows = width // chips
        self.block = units // chips
        self.fold = units // width
        self.split = self.rows % 16 == 0 and chips == 16
        self.packed = (self.fold + 1) * self.rows

    def scratch(self, rows):
        width, units, cols = self.width, self.units, self.cols
        if self.split:
            weights = [(self.chips, self.rows, units), (self.chips, self.rows, width)]
            weights += [(4, 4, self.block, width)]
        else:
            weights = [(width, units), (width, width), (units, width)]
        full, wide = (rows, width), (rows, units)
        low = weights + [full, (rows, cols), (rows, cols), full, wide, wide, full, full]
        low += [(2, units, cols), (2, self.fold, width, cols), (2, width, cols), (2, rows, cols)]
        high = [full, full, full, full]
        return [pltpu.VMEM(one, BF) for one in low] + [pltpu.VMEM(one, F32) for one in high]


def ffn_kernel(layout, count, where_ref, len_ref, table_ref, bias_ref, *refs):
    (tok_hbm, cot_hbm, ctx_mine_hbm, ctx_theirs_hbm), refs = refs[:4], refs[4:]
    weights, refs = refs[:count], refs[count:]
    grads = 4 if layout.split else 6
    sums_two_ref, sums_one_ref, sums_inner_ref = refs[:3]
    (out_hbm, resid_hbm, gc_mine_hbm, gc_theirs_hbm), refs = refs[3:7], refs[7:]
    grad_hbm, refs = refs[:grads], refs[grads:]
    (
        inner_ref,
        mix_ref,
        outer_ref,
        tok_ref,
        mine_ref,
        theirs_ref,
        cot_ref,
        active_ref,
        slope_ref,
        low_ref,
        context_ref,
        stage_outer,
        stage_inner,
        stage_mix,
        stage_ctx,
        hidden_ref,
        normed_ref,
        out_ref,
        resid_ref,
        in_sems,
        out_sems,
    ) = refs
    width, units, cols = layout.width, layout.units, layout.cols
    core = where_ref[0]
    first = core == 0
    extent = units // 4
    loads = []

    def load(source, target):
        copy = pltpu.make_async_copy(source, target, in_sems.at[len(loads)])
        copy.start()
        loads.append(copy)
        return copy

    small = [
        load(*pair)
        for pair in (
            (ctx_mine_hbm, mine_ref),
            (ctx_theirs_hbm, theirs_ref),
            (tok_hbm, tok_ref),
        )
    ]
    if layout.split:
        together = weights[0]
        rows = layout.rows
        last = layout.fold * rows
        mix_loads = [
            load(
                together.at[:, half, last : last + rows, :],
                mix_ref.at[:, :, half * cols : (half + 1) * cols],
            )
            for half in range(2)
        ]
        inner_loads = [
            [
                load(
                    together.at[:, tile // 2, place * rows : (place + 1) * rows, :],
                    inner_ref.at[
                        :,
                        :,
                        ((tile // 2) * layout.fold + place) * cols : (
                            (tile // 2) * layout.fold + place + 1
                        )
                        * cols,
                    ],
                )
                for place in range(
                    (tile % 2) * layout.fold // 2, (tile % 2 + 1) * layout.fold // 2
                )
            ]
            for tile in range(4)
        ]
        outer_loads = []
        for other in range(2):
            half = core ^ other
            for mask in range(4):
                outer_loads.append(
                    load(
                        weights[1 + 4 * other + mask],
                        outer_ref.at[:, where_ref[2] ^ mask, :, span(half, cols)],
                    )
                )
    else:
        mix_loads = [load(weights[0], mix_ref)]
        inner_loads = [[load(weights[1], inner_ref)], [], [], []]
        outer_loads = [load(weights[2], outer_ref)]
    cot_load = load(cot_hbm, cot_ref)

    def mix_half(half):
        lanes = slice(half * cols, (half + 1) * cols)
        if layout.split:
            return mix_ref[:, :, lanes].reshape(width, cols)
        return mix_ref[:, lanes]

    def inner_tile(tile):
        if layout.split:
            return inner_ref[:, :, span(tile, extent)].reshape(width, extent)
        return inner_ref[:, span(tile, extent)]

    def outer_tile(tile):
        if layout.split:
            return outer_ref[tile].reshape(extent, width)
        return outer_ref[span(tile, extent), :]

    stores = []

    def store(source, target):
        copy = pltpu.make_async_copy(source, target, out_sems.at[len(stores)])
        copy.start()
        stores.append(copy)

    for copy in small:
        copy.wait()
    context = ordered(first, mine_ref[...], theirs_ref[...], 1)
    context_ref[...] = context
    for copy in mix_loads:
        copy.wait()
    attn = jnp.concatenate([product(context, mix_half(half)) for half in range(2)], axis=1)
    normed, inv_one = normalize(
        tok_ref[...].astype(F32) + (attn + table_ref[B_OUT : B_OUT + 1])
    )
    normed_ref[...] = normed
    hidden = normed * table_ref[GAIN_ONE : GAIN_ONE + 1] + table_ref[SHIFT_ONE : SHIFT_ONE + 1]
    hidden_ref[...] = hidden
    low_ref[...] = hidden.astype(BF)
    for tile in range(4):
        for copy in inner_loads[tile]:
            copy.wait()
        lanes = slice(tile * extent, (tile + 1) * extent)
        pre = product(low_ref[...], inner_tile(tile)) + bias_ref[:, lanes]
        cumulative = 0.5 * (1.0 + lax.erf(pre * ROOT_HALF))
        active_ref[:, lanes] = (pre * cumulative).astype(BF)
        slope = cumulative + pre * jnp.exp(-0.5 * pre * pre) * INV_ROOT_TAU
        slope_ref[:, lanes] = slope.astype(BF)
    for copy in outer_loads:
        copy.wait()
    total = hidden_ref[...] + table_ref[B_OUTER : B_OUTER + 1]
    for tile in range(4):
        total += product(active_ref[:, tile * extent : (tile + 1) * extent], outer_tile(tile))
    normed, inv = normalize(total)
    gain = table_ref[GAIN_TWO : GAIN_TWO + 1]
    out_ref[...] = normed * gain + table_ref[SHIFT_TWO : SHIFT_TWO + 1]
    store(out_ref, out_hbm)
    seqs = len_ref.shape[0]
    half_length = normed.shape[0] // seqs
    position = core * half_length + lax.broadcasted_iota(jnp.int32, (half_length, 1), 0)
    live = jnp.concatenate(
        [jnp.where(position < len_ref[s], 1.0, 0.0) for s in range(seqs)], axis=0
    )
    cot_load.wait()
    grad = cot_ref[...].astype(F32) * live
    resid = normalize_back(grad, normed, inv, gain)
    grad_outer = resid.astype(BF)
    sums_two_ref[...] = column_sums(grad_outer, grad * normed, grad)
    resid_ref[...] = resid

    def halves(values):
        left, right = values[:, :cols], values[:, cols:]
        return jnp.where(first, right, left), jnp.where(first, left, right)

    rows = layout.rows
    for other, columns in zip((1, 0), halves(grad_outer)):
        for tile in range(4):
            lanes = slice(tile * extent, (tile + 1) * extent)
            found = product(active_ref[:, lanes].T, columns).astype(BF)
            stage_outer[other, lanes, :] = found
            if layout.split:
                near = extent // layout.block
                for chip in range(near):
                    start = tile * extent + chip * layout.block
                    store(
                        stage_outer.at[other, start : start + layout.block, :],
                        grad_hbm[other].at[tile * near + chip],
                    )
            else:
                store(
                    stage_outer.at[other, lanes, :],
                    grad_hbm[3 * other].at[lanes, :],
                )
    low_t = low_ref[...].T
    total = resid_ref[...]
    for other in (1, 0):
        for part in range(2):
            place = 2 * (core ^ other) + part
            grad = product_nt(grad_outer, outer_tile(place))
            grad = (grad * slope_ref[:, span(place, extent)].astype(F32)).astype(BF)
            sums_inner_ref[:, span(place, extent)] = jnp.sum(
                grad.astype(F32), axis=0, keepdims=True
            )
            total += product_nt(grad, inner_tile(place))
            found = product(low_t, grad).astype(BF)
            for i in range(layout.fold // 2):
                index = part * (layout.fold // 2) + i
                stage_inner[other, index] = found[:, i * cols : (i + 1) * cols]
                if layout.split:
                    start = index * rows
                    for chip in range(layout.chips):
                        store(
                            stage_inner.at[other, index, chip * rows : (chip + 1) * rows, :],
                            grad_hbm[2 + other].at[chip, start : start + rows, :],
                        )
                else:
                    store(
                        stage_inner.at[other, index],
                        grad_hbm[3 * other + 1].at[:, index * cols : (index + 1) * cols],
                    )
    normed = normed_ref[...]
    resid = normalize_back(total, normed, inv_one, table_ref[GAIN_ONE : GAIN_ONE + 1])
    resid_ref[...] = resid
    store(resid_ref, resid_hbm)
    attn = resid.astype(BF)
    sums_one_ref[...] = column_sums(attn, total * normed, total)
    back = product_nt(attn[:, :cols], mix_half(0)) + product_nt(attn[:, cols:], mix_half(1))
    for other, columns, target in zip(
        (1, 0), halves(back.astype(BF)), (gc_theirs_hbm, gc_mine_hbm)
    ):
        stage_ctx[other] = columns
        store(stage_ctx.at[other], target)
    context_t = context_ref[...].T
    for other, columns in zip((1, 0), halves(attn)):
        stage_mix[other] = product(context_t, columns).astype(BF)
        if layout.split:
            start = layout.fold * rows
            for chip in range(layout.chips):
                store(
                    stage_mix.at[other, chip * rows : (chip + 1) * rows, :],
                    grad_hbm[2 + other].at[chip, start : start + rows, :],
                )
        else:
            store(stage_mix.at[other], grad_hbm[3 * other + 2])
    for copy in stores:
        copy.wait()


def ffn(layout, where, lengths, table, bias, tokens, cotangent, mine, theirs, weights):
    rows, width = tokens.shape
    units, cols = layout.units, layout.cols
    full, part = (rows, width), (rows, cols)
    if layout.split:
        grads = [(layout.chips, layout.block, cols)] * 2
        grads += [(layout.chips, layout.packed, cols)] * 2
        loads = 3 + 2 + 2 * layout.fold + 8 + 1
        stores = 4 + 2 * layout.chips * (layout.fold + 2)
    else:
        grads = [(units, cols), (width, units // 2), (width, cols)] * 2
        loads = 7
        stores = 4 + 2 * (4 + layout.fold + 1)
    anywhere = pl.BlockSpec(memory_space=pl.ANY)
    arrays = (tokens, cotangent, mine, theirs, *weights)
    outs = [((8, width), F32), ((8, width), F32), ((1, units), F32), (full, F32), (full, F32)]
    outs += [(part, BF)] * 2 + [(one, BF) for one in grads]
    return pl.pallas_call(
        functools.partial(ffn_kernel, layout, len(weights)),
        out_shape=tuple(jax.ShapeDtypeStruct(shape, kind) for shape, kind in outs),
        grid_spec=pltpu.PrefetchScalarGridSpec(
            num_scalar_prefetch=2,
            grid=(1,),
            in_specs=on_chip(2) + [anywhere] * len(arrays),
            out_specs=tuple(on_chip(3) + [anywhere] * (len(outs) - 3)),
            scratch_shapes=layout.scratch(rows)
            + [pltpu.SemaphoreType.DMA((loads,)), pltpu.SemaphoreType.DMA((stores,))],
        ),
        compiler_params=pltpu.CompilerParams(vmem_limit_bytes=58 << 20),
        cost_estimate=SMALL,
        name="ffn",
    )(where, lengths, table, bias, *arrays)


def token_kernel(count, where_ref, *refs):
    grad_refs = refs[:count]
    weight_ref, resid_ref, keep_ref, away_ref = refs[count:]
    half = resid_ref.shape[0]
    extent = grad_refs[0].shape[1]
    mine = where_ref[0] * half
    for start, target in ((half - mine, away_ref), (mine, keep_ref)):
        rows = pl.ds(pl.multiple_of(start, half), half)
        part = product_nt(grad_refs[0][rows, :], weight_ref[:, :extent])
        for i in range(1, count):
            part += product_nt(
                grad_refs[i][rows, :], weight_ref[:, i * extent : (i + 1) * extent]
            )
        if target is keep_ref:
            part += resid_ref[...]
        target[...] = part.astype(target.dtype)


def token_grads(where, grads, weight, resid, seqs):
    rows, cols = grads[0].shape
    width = resid.shape[1]
    length = rows // seqs

    def rowwise(extent, columns):
        return pl.BlockSpec((extent, columns), lambda i, *_: (i, 0))

    return pl.pallas_call(
        functools.partial(token_kernel, len(grads)),
        out_shape=(
            jax.ShapeDtypeStruct((rows // 2, width), F32),
            jax.ShapeDtypeStruct((rows // 2, width), BF),
        ),
        grid_spec=pltpu.PrefetchScalarGridSpec(
            num_scalar_prefetch=1,
            grid=(seqs,),
            in_specs=[rowwise(length, cols)] * len(grads)
            + [pl.BlockSpec(weight.shape, lambda *_: (0, 0)), rowwise(length // 2, width)],
            out_specs=(rowwise(length // 2, width), rowwise(length // 2, width)),
        ),
        compiler_params=pltpu.CompilerParams(vmem_limit_bytes=44 << 20),
        cost_estimate=SMALL,
        name="token_grads",
    )(where, *grads, weight, resid)


class Sum:
    def __init__(self, terms, flying=()):
        self.terms, self.flying = list(terms), list(flying)


jax.tree_util.register_pytree_node(
    Sum,
    lambda held: (
        ([array for array, _, _ in held.terms], [array for array, _ in held.flying]),
        (
            tuple((bits, window) for _, bits, window in held.terms),
            tuple(mask for _, mask in held.flying),
        ),
    ),
    lambda fixed, arrays: Sum(
        [(array, *about) for array, about in zip(arrays[0], fixed[0])], zip(arrays[1], fixed[1])
    ),
)


def tie(values):
    return lax.optimization_barrier(values)


def masks(digit):
    found = [0]
    for bit in digit:
        found += [one | (1 << bit) for one in found]
    return found[1:]


class Wires:
    def __init__(self):
        self.chips = lax.axis_size(CHIPS)
        self.bits = self.chips.bit_length() - 1
        self.chip = lax.axis_index(CHIPS)
        self.core = lax.axis_index("seq")
        self.first = self.core == 0
        far = list(range(self.bits - 1, 1, -1))
        self.far = [tuple(far[i : i + 2]) for i in range(0, len(far), 2)]

    def side(self, bit):
        return (self.chip >> bit) & 1

    def meet(self, values, mask):
        return lax.ppermute(values, CHIPS, [(i, i ^ mask) for i in range(self.chips)])

    def swap_core(self, values):
        return lax.ppermute(values, "seq", [(0, 1), (1, 0)])

    def pick(self, low, high):
        return jnp.where(self.first, low, high), jnp.where(self.first, high, low)

    def columns(self, values):
        cols = values.shape[1] // 2
        return self.pick(values[:, :cols], values[:, cols:])

    def beside(self, mine, theirs, side, axis):
        shape = [1] * (mine.ndim + 1)
        shape[axis] = 2
        here = lax.broadcasted_iota(jnp.int32, tuple(shape), axis) == side
        return jnp.where(here, jnp.expand_dims(mine, axis), jnp.expand_dims(theirs, axis))


    def gather_far(self, values, digit):
        found = {0: values}
        found.update({mask: self.meet(values, mask) for mask in masks(digit)})
        for bit in reversed(digit):
            known = {mask for mask in found if not mask & (1 << bit)}
            found = {
                mask: self.beside(found[mask], found[mask | (1 << bit)], self.side(bit), 1)
                for mask in known
            }
        return found[0].reshape((-1,) + values.shape[1:])

    def gather_near(self, values, bit):
        return self.beside(values, self.meet(values, 1 << bit), self.side(bit), 1)

    def pieces(self, values, bit):
        width = values.shape[-1]
        rows = values.shape[-2] << bit
        values = values.reshape(-1, rows, width)
        return values, self.meet(values, 1 << bit)

    def gather_plane(self, values):
        return [values] + [self.meet(values, mask) for mask in masks((0, 1))]

    def plane(self, pieces):
        own = self.chip & 3
        stacked = jnp.stack(pieces, axis=1)
        parts = [
            lax.dynamic_index_in_dim(stacked, own ^ place, 1, keepdims=False) for place in range(4)
        ]
        return jnp.concatenate(parts, axis=1)

    def whole(self, pieces, bit):
        width = pieces[0].shape[-1]
        return self.beside(pieces[0], pieces[1], self.side(bit), 1).reshape(-1, width)


    def spread(self, terms, tail, windows):
        bits = tuple(range(self.bits - 1, -1, -1))
        arrays = [one.reshape([2] * self.bits + list(tail)) for one in terms]
        return [Sum([(one, bits, window) for one in arrays]) for window in windows]

    def part(self, held, fixed):
        total = None
        for array, bits, window in held.terms:
            tail = array.shape[len(bits) :]
            first, size = window if window else ((0,) * len(tail), tail)
            starts = [fixed.get(bit, 0) for bit in bits] + list(first)
            sizes = [1 if bit in fixed else 2 for bit in bits] + list(size)
            shape = [2 for bit in bits if bit not in fixed] + list(size)[-2:]
            one = lax.dynamic_slice(array, starts, sizes).reshape(shape).astype(F32)
            total = one if total is None else total + one
        return total

    def left(self, held):
        return held.terms[-1][1]

    def settled(self, held):
        return {bit: self.side(bit) for bit in range(self.bits) if bit not in self.left(held)}

    def ready(self, held, digit):
        fixed = self.settled(held)
        sent = []
        for mask in masks(digit):
            away = {bit: self.side(bit) ^ ((mask >> bit) & 1) for bit in digit}
            sent.append((self.part(held, {**fixed, **away}).astype(BF), mask))
        return Sum(held.terms, sent)

    def go(self, held):
        return Sum(held.terms, [(self.meet(one, mask), mask) for one, mask in held.flying])

    def land(self, held, digit):
        bits = tuple(bit for bit in self.left(held) if bit not in digit)
        return Sum(held.terms + [(one, bits, None) for one, _ in held.flying])

    def total(self, held):
        return self.part(held, self.settled(held))


    def near_ready(self, pair, step):
        return [self.ready(held, (stream ^ step,)) for stream, held in enumerate(pair)]

    def near_go(self, pair):
        return [self.go(held) for held in pair]

    def near_land(self, pair, step):
        return [self.land(held, (stream ^ step,)) for stream, held in enumerate(pair)]

    def joined(self, pair, axis):
        sums = [self.total(held).astype(BF) for held in pair]
        return Sum([(jnp.concatenate(sums, axis=axis), self.left(pair[0]), None)])

    def far_sum(self, held):
        array = held.terms[0][0]
        return lax.psum_scatter(
            array.reshape(-1, array.shape[-1]), "far", scatter_dimension=0, tiled=True
        )

    def far_steps(self, held):
        for digit in self.far[:-1]:
            held = self.land(self.go(self.ready(held, digit)), digit)
        return held

    def owned(self, block):
        rows = block.shape[0] // 2
        return self.pick(block[:rows], block[rows:])


def body(tokens, lengths, cotangent, *shards):
    (
        w_query,
        b_query,
        w_key,
        w_value,
        b_value,
        w_out,
        b_out,
        gain_one,
        shift_one,
        w_inner,
        b_inner,
        w_outer,
        b_outer,
        gain_two,
        shift_two,
    ) = shards
    wires = Wires()
    core = wires.core
    devices = 2 * wires.chips
    seqs, half, width = tokens.shape
    rows = seqs * half
    cols = width // 2
    slot = b_query.shape[0]
    fold = b_inner.shape[0] // slot
    plane = wires.chip & 3
    where = jnp.stack([core, wires.chip, plane, wires.side(0), wires.side(1)]).astype(jnp.int32)

    vectors = jnp.stack(
        [b_query, b_value, b_out, gain_one, shift_one, b_outer, gain_two, shift_two]
    )
    vectors = jnp.concatenate([vectors, b_inner.reshape(fold, slot)], axis=0)
    vectors = jnp.pad(vectors.T, ((0, 0), (0, LANES - vectors.shape[0])))
    mine, away = zip(*[wires.columns(one) for one in (w_query, w_key, w_value, w_out, w_inner)])
    pairs = cols // PAIR

    def by_pair(parts):
        spans = [slice(p * PAIR, (p + 1) * PAIR) for p in range(pairs)]
        return jnp.concatenate([one[:, span] for span in spans for one in parts] + [vectors], axis=1)

    def both_rows(kept, sent):
        return ordered(wires.first, kept, wires.swap_core(sent), 0)

    units = w_inner.shape[1]
    paired = 2 * slot
    layout = Layout(wires.chips, width, units)
    aligned = layout.split
    first = both_rows(by_pair(mine[:3]), by_pair(away[:3]))[None]
    outer_mine, outer_away = wires.columns(w_outer)
    outer_held = both_rows(outer_mine, outer_away)[None]
    if aligned:
        parts = [jnp.concatenate([inner, out], axis=1) for out, inner in (mine[3:], away[3:])]
        second = both_rows(*parts)
        second = jnp.concatenate(
            [second[:, i : i + cols] for i in range(0, second.shape[1], cols)], axis=0
        )
        second = lax.all_gather(second, CHIPS + ("seq",), axis=0, tiled=True)
        weights = [second.reshape(wires.chips, 2, -1, cols)]
    else:
        weights = [
            lax.all_gather(one, CHIPS + ("seq",), axis=0, tiled=True)
            for one in (w_out, w_inner, w_outer)
        ]
    for digit in wires.far:
        first = wires.gather_far(first, digit)
    first, outer_held = tie((first, outer_held))
    for digit in wires.far:
        outer_held = wires.gather_far(outer_held, digit)
    cut = (3 * pairs + 1) // 2 * LANES
    one = wires.gather_near(first[..., :cut], 1)
    two = wires.gather_near(first[..., cut:], 0)
    pieces_one, pieces_two = wires.pieces(one, 0), wires.pieces(two, 1)
    if not aligned:
        pieces_one, pieces_two = [
            (wires.whole(pieces, bit)[None],)
            for bit, pieces in enumerate((pieces_one, pieces_two))
        ]
    if aligned:
        pieces_one, pieces_two, outer_held = tie((pieces_one, pieces_two, outer_held))
        outer_held = wires.gather_plane(outer_held)
    tok_rows = tokens.reshape(rows, width)
    tok_other = wires.swap_core(tokens)
    tok_all = ordered(wires.first, tokens, tok_other, 1).reshape(2 * rows, width)

    qkv, ctx_mine, ctx_away, lse, w_qkv, table = attend(
        where, lengths, tokens, tok_other, pieces_one, pieces_two
    )
    ctx_theirs = wires.swap_core(ctx_away)
    if aligned:
        ctx_theirs, outer_held = tie((ctx_theirs, outer_held))
        weights += outer_held + [wires.swap_core(one) for one in outer_held]
    kept = 8 + fold
    bias_inner = table[8:kept].reshape(fold, devices, slot).transpose(1, 0, 2).reshape(1, -1)
    results = ffn(
        layout,
        where,
        lengths,
        table,
        bias_inner,
        tok_rows,
        cotangent.reshape(rows, width),
        ctx_mine,
        ctx_theirs,
        weights,
    )
    sums_two, sums_one, sums_inner, output, resid_one, gc_mine, gc_away = results[:7]
    grad_parts = results[7:]
    if not aligned:

        def by_chip(many):
            g_outer, g_inner, g_out = many
            g_inner = g_inner.reshape(wires.chips, -1, fold, cols).transpose(0, 2, 1, 3)
            others = (g_inner.reshape(wires.chips, -1, cols), g_out.reshape(wires.chips, -1, cols))
            return g_outer.reshape(wires.chips, -1, cols), jnp.concatenate(others, axis=1)

        mine, away = by_chip(grad_parts[:3]), by_chip(grad_parts[3:])
        grad_parts = (mine[0], away[0], mine[1], away[1])
    g_outer, g_outer_away, g_rest, g_rest_away = grad_parts

    last = wires.far[-1]
    rows_chip = 2 * slot
    gc_theirs = wires.swap_core(gc_away)
    base = jnp.concatenate(
        [
            jnp.zeros((2, width), F32),
            sums_one[:3],
            sums_two[:3],
            sums_inner.reshape(devices, fold, slot).transpose(1, 0, 2).reshape(fold, width),
            jnp.zeros((TABLE - kept, width), F32),
        ],
        axis=0,
    )

    def two_windows(held, theirs):
        extent = held.shape[1]
        cut = extent // 2 // 16 * 16 if aligned else extent // 2
        return wires.spread(
            [held, theirs],
            (extent, cols),
            [((0, 0), (cut, cols)), ((cut, 0), (extent - cut, cols))],
        )

    def attention_grad(pair, held, widths):
        return attend_back(
            pair, where, lengths, qkv, gc_mine, gc_theirs, lse, tok_all, held, widths
        )

    pair_width = 3 * PAIR
    more = (3 * pairs + 1) // 2 * LANES - pair_width
    grad_one, sums_first, g_first = attention_grad(0, (), (pair_width,))
    arrived = wires.swap_core(g_outer_away)
    grad_one, arrived, base = tie((grad_one, arrived, base))
    outer = wires.near_ready(two_windows(g_outer, arrived), 0)
    gc_mine, outer = tie((gc_mine, outer))
    outer = wires.near_go(outer)
    grad_two, sums_second, g_one, g_kept = attention_grad(
        1, (g_first,), (pair_width + more, pair_width - more)
    )
    arrived = wires.swap_core(g_rest_away)
    grad_two, arrived = tie((grad_two, arrived))
    rest = wires.near_ready(two_windows(g_rest, arrived), 0)
    gc_mine, rest = tie((gc_mine, rest))
    rest = wires.near_go(rest)
    grad_three, _, g_two = attention_grad(
        2,
        (g_kept, base, sums_first, sums_second),
        (2 * pair_width - more + LANES,),
    )
    grads = [grad_one, grad_two, grad_three]
    grads, outer = tie((grads, outer))
    outer = wires.near_ready(wires.near_land(outer, 0), 1)
    both = [wires.spread([one], (rows_chip, one.shape[1]), [None])[0] for one in (g_one, g_two)]
    both = wires.near_ready(both, 0)
    grads, outer, both = tie((grads, outer, both))
    outer, both = wires.near_go(outer), wires.near_go(both)
    tok_keep, tok_away = token_grads(where, grads, w_qkv, resid_one, seqs)
    tok_away, tok_keep, outer, rest = tie((tok_away, tok_keep, outer, rest))
    rest = wires.near_ready(wires.near_land(rest, 0), 1)
    tok_away, rest = tie((tok_away, rest))
    rest = wires.near_go(rest)
    tok_theirs = wires.swap_core(tok_away)
    g_outer = wires.far_sum(wires.joined(wires.near_land(outer, 1), -2))
    tok_theirs, both = tie((tok_theirs, both))
    both = wires.near_ready(wires.near_land(both, 0), 1)
    tok_theirs, both = tie((tok_theirs, both))
    both = wires.near_go(both)
    grad_tok = tok_keep + tok_theirs.astype(F32)
    rest, both = tie((rest, both))
    rest = wires.joined(wires.near_land(rest, 1), -2)
    rest = wires.ready(wires.far_steps(rest), last)
    both = wires.joined(wires.near_land(both, 1), -1)
    both = wires.ready(wires.far_steps(both), last)
    rest, both = tie((rest, both))
    rest, both = wires.go(rest), wires.go(both)
    g_rest = wires.total(wires.land(rest, last))
    g_both = wires.total(wires.land(both, last))

    columns = [g_both] + [
        g_rest[i * rows_chip : (i + 1) * rows_chip] for i in range(fold + 1)
    ]
    mine, away = wires.owned(jnp.concatenate(columns, axis=1))
    theirs = wires.swap_core(away)
    mine_outer, away = wires.owned(g_outer.astype(F32))
    g_outer = ordered(wires.first, mine_outer, wires.swap_core(away), 1)
    begin = g_both.shape[1]

    def full(spans):
        return jnp.concatenate(
            [one[:, span] for one in wires.pick(mine, theirs) for span in spans], axis=1
        )

    pieces = [
        full([slice((3 * p + i) * PAIR, (3 * p + i + 1) * PAIR) for p in range(pairs)])
        for i in range(3)
    ]
    pieces.append(full([slice(begin + fold * cols, begin + (fold + 1) * cols)]))
    pieces.append(full([slice(begin, begin + fold * cols)]))
    vectors = slice(begin - LANES, begin)
    small = (mine[:, vectors] + theirs[:, vectors]).T

    return (
        output.reshape(seqs, half, width),
        grad_tok.reshape(seqs, half, width),
        pieces[0],
        small[0],
        pieces[1],
        pieces[2],
        small[1],
        pieces[3],
        small[2],
        small[3],
        small[4],
        pieces[4],
        small[8:kept].reshape(-1),
        g_outer,
        small[5],
        small[6],
        small[7],
    )


def solution(mesh):
    cores = mesh.shape["seq"]
    split = Mesh(mesh.devices.reshape(-1, 2, 2, cores), CHIPS + ("seq",))
    every = CHIPS + ("seq",)
    matrix, vector = P(every, None), P(every)
    rows = P(CHIPS, "seq", None)
    weights = (matrix, vector, matrix, matrix, vector, matrix, vector, vector, vector)
    weights += (matrix, vector, matrix, vector, vector, vector)
    return jax.shard_map(
        body,
        mesh=split,
        in_specs=(rows, P(CHIPS), rows) + weights,
        out_specs=(rows, rows) + weights,
        check_vma=False,
    )
```

```python
import functools

import jax
import jax.numpy as jnp
from jax import lax
from jax.experimental import pallas as pl
from jax.experimental.pallas import tpu as pltpu
from jax.sharding import Mesh
from jax.sharding import PartitionSpec as P

HEAD_DIM = 64
PAIR = 2 * HEAD_DIM
LANES = 128
NEG_BIG = -1000000000.0
EPSILON = 1e-05
ROOT_HALF = 0.7071067811865476
INV_ROOT_TAU = 0.3989422804014327
BF = jnp.bfloat16
CHIPS = ("far", "mid", "low")
F32 = jnp.float32
VMEM_LIMIT = 20 << 20
SMALL = pl.CostEstimate(flops=1024, transcendentals=0, bytes_accessed=1024)

B_QUERY, B_VALUE, B_OUT, GAIN_ONE, SHIFT_ONE, B_OUTER, GAIN_TWO, SHIFT_TWO, B_INNER = range(9)
TABLE = 16


def product(left, right):
    return jnp.dot(left, right, preferred_element_type=F32)


def product_tn(left, right):
    return lax.dot_general(left, right, (((0,), (0,)), ((), ())), preferred_element_type=F32)


def product_nt(left, right):
    return lax.dot_general(left, right, (((1,), (1,)), ((), ())), preferred_element_type=F32)


def ordered(first, mine, theirs, axis):
    return jnp.concatenate([jnp.where(first, mine, theirs), jnp.where(first, theirs, mine)], axis)


def row_mean(values):
    return jnp.mean(values, axis=-1, keepdims=True)


def normalize(values):
    center = values - row_mean(values)
    inv_spread = lax.rsqrt(row_mean(center * center) + EPSILON)
    return center * inv_spread, inv_spread


def normalize_back(grad_out, normed, inv_spread, gain):
    grad_normed = grad_out * gain
    centered = grad_normed - row_mean(grad_normed)
    return inv_spread * (centered - normed * row_mean(grad_normed * normed))


def column_sums(*values):
    rows = [jnp.sum(one.astype(F32), axis=0, keepdims=True) for one in values]
    pad = jnp.zeros((8 - len(rows), rows[0].shape[1]), F32)
    return jnp.concatenate(rows + [pad], axis=0)


def attend_kernel(seq, count, where_ref, len_ref, mine_ref, theirs_ref, *refs):
    held = (refs[:count], refs[count : 2 * count])
    refs = refs[2 * count :]
    if count == 0:
        refs = refs[2:] + refs[:2]
    qkv_ref, ctx_mine_ref, ctx_theirs_ref, lse_ref, weight_ref, table_ref = refs
    core = where_ref[0]
    first = core == 0
    seen_to = len_ref[seq]
    width = weight_ref.shape[0]
    cols = width // 2

    if count > 0:
        start = 0
        for stream, pieces in enumerate(held):
            side = where_ref[3 + stream]
            extent = pieces[0].shape[-1]
            fill(weight_ref.at[:, start : start + extent], pieces, (side, 1 - side))
            start += extent
        last = weight_ref.shape[1] - LANES
        chosen = lax.broadcasted_iota(jnp.int32, (TABLE, LANES), 0)
        chosen = chosen == lax.broadcasted_iota(jnp.int32, (TABLE, LANES), 1)
        table_ref[...] = product_nt(
            jnp.where(chosen, 1.0, 0.0).astype(BF), weight_ref[:, last:]
        )

    def own(row):
        return jnp.where(first, table_ref[row : row + 1, :cols], table_ref[row : row + 1, cols:])

    tokens = ordered(first, mine_ref[seq], theirs_ref[seq], 0)
    length = tokens.shape[0]
    bias_q, bias_v = own(B_QUERY), own(B_VALUE)
    seen = lax.broadcasted_iota(jnp.int32, (length, length), 0) < seen_to
    lane = lax.broadcasted_iota(jnp.int32, (length, PAIR), 1)
    for pair in range(cols // PAIR):
        lanes = slice(pair * PAIR, (pair + 1) * PAIR)
        project = product(tokens, weight_ref[:, 3 * pair * PAIR : 3 * (pair + 1) * PAIR])
        queries = (project[:, :PAIR] + bias_q[:, lanes]).astype(BF)
        keys = project[:, PAIR : 2 * PAIR].astype(BF)
        values = (project[:, 2 * PAIR :] + bias_v[:, lanes]).astype(BF)
        qkv_ref[:, 3 * pair * PAIR : 3 * (pair + 1) * PAIR] = jnp.concatenate(
            [queries, keys, values], axis=1
        )
        queries = queries * BF(HEAD_DIM ** (-0.5))
        values_t = values.T
        parts = []
        for head in range(2):
            mask = (lane >= head * HEAD_DIM) & (lane < (head + 1) * HEAD_DIM)
            scores = product_nt(jnp.where(mask, keys, BF(0)), queries)
            scores = jnp.where(seen, scores, NEG_BIG)
            top = jnp.max(scores, axis=0, keepdims=True)
            weights = jnp.exp(scores - top)
            total = jnp.sum(weights, axis=0, keepdims=True)
            probs = (weights * (1.0 / total)).astype(BF)
            parts.append(product(values_t[head * HEAD_DIM : (head + 1) * HEAD_DIM], probs))
            row = 2 * pair + head
            lse_ref[row : row + 1, :] = top + jnp.log(total)
        context = jnp.concatenate(parts, axis=0).T.astype(BF)
        low, high = context[: length // 2], context[length // 2 :]
        ctx_mine_ref[:, lanes] = jnp.where(first, low, high)
        ctx_theirs_ref[:, lanes] = jnp.where(first, high, low)


def attend_back_kernel(pair, extras, seqs, where_ref, len_ref, *refs):
    qkv_refs, lse_refs, refs = refs[:seqs], refs[seqs : 2 * seqs], refs[2 * seqs :]
    mine_ref, theirs_ref, tok_ref, *refs = refs
    held, refs = refs[:extras], refs[extras:]
    grad_ref, sums_ref, *weight_refs = refs
    first = where_ref[0] == 0
    scale = BF(HEAD_DIM ** (-0.5))
    length = qkv_refs[0].shape[0]
    start = 3 * pair * PAIR
    lanes = slice(pair * PAIR, (pair + 1) * PAIR)
    lane = lax.broadcasted_iota(jnp.int32, (length, PAIR), 1)
    key_row = lax.broadcasted_iota(jnp.int32, (length, length), 0)
    sums = total = None
    for seq, (qkv_ref, lse_ref) in enumerate(zip(qkv_refs, lse_refs)):
        rows = slice(seq * length, (seq + 1) * length)
        half_rows = slice(seq * length // 2, (seq + 1) * length // 2)
        seen = key_row < len_ref[seq]
        queries = qkv_ref[:, start : start + PAIR] * scale
        keys = qkv_ref[:, start + PAIR : start + 2 * PAIR]
        values = qkv_ref[:, start + 2 * PAIR : start + 3 * PAIR]
        grad = ordered(first, mine_ref[half_rows, lanes], theirs_ref[half_rows, lanes], 0)
        keys_t = (keys * scale).T
        dq, dk, dv = [], [], []
        for head in range(2):
            own = (lane >= head * HEAD_DIM) & (lane < (head + 1) * HEAD_DIM)
            scores = product_nt(jnp.where(own, keys, BF(0)), queries)
            scores = jnp.where(seen, scores, NEG_BIG)
            row = 2 * pair + head
            probs = jnp.exp(scores - lse_ref[row : row + 1, :])
            grad_probs = product_nt(jnp.where(own, values, BF(0)), grad)
            row_term = jnp.sum(probs * grad_probs, axis=0, keepdims=True)
            grad_scores = (probs * (grad_probs - row_term)).astype(BF)
            dv.append(product(probs.astype(BF), grad))
            dk.append(product(grad_scores, queries))
            dq.append(product(keys_t[head * HEAD_DIM : (head + 1) * HEAD_DIM], grad_scores))
        own = lane < HEAD_DIM
        all_three = [
            jnp.concatenate(dq, axis=0).T.astype(BF),
            jnp.where(own, dk[0], dk[1]).astype(BF),
            jnp.where(own, dv[0], dv[1]).astype(BF),
        ]
        grads = jnp.concatenate(all_three, axis=1)
        grad_ref[rows, :] = grads
        one = jnp.sum(grads.astype(F32), axis=0, keepdims=True)
        weight = product(tok_ref[rows, :].T, grads)
        sums = one if sums is None else sums + one
        total = weight if total is None else total + weight
    sums_ref[...] = sums
    found = total.astype(BF)
    extent = found.shape[1]
    if pair == 0:
        weight_refs[0][...] = found
    elif extras == 1:
        more = weight_refs[0].shape[1] - extent
        weight_refs[0][:, :extent] = held[0][...]
        weight_refs[0][:, extent:] = found[:, :more]
        weight_refs[1][...] = found[:, more:]
    else:
        kept = held[0].shape[1]
        weight_refs[0][:, :kept] = held[0][...]
        weight_refs[0][:, kept : kept + extent] = found
        many = [one[...] for one in held[2:]] + [sums]
        blank = jnp.zeros((1, many[0].shape[1] // 3 * len(many)), F32)
        table = held[1][...]
        place = lax.broadcasted_iota(jnp.int32, table.shape, 0)
        for number, begin in ((B_QUERY, 0), (B_VALUE, 2 * PAIR)):
            row = jnp.concatenate([one[:, begin : begin + PAIR] for one in many], axis=1)
            row = jnp.concatenate(
                [jnp.where(first, row, blank), jnp.where(first, blank, row)], axis=1
            )
            table = jnp.where(place == number, row, table)
        chosen = lax.broadcasted_iota(jnp.int32, (TABLE, LANES), 0)
        chosen = chosen == lax.broadcasted_iota(jnp.int32, (TABLE, LANES), 1)
        weight_refs[0][:, kept + extent :] = product_tn(
            table.astype(BF), jnp.where(chosen, 1.0, 0.0).astype(BF)
        ).astype(BF)


def attend(seq, where, lengths, mine, theirs, held):
    half, width = mine.shape[1:]
    length = 2 * half
    cols = width // 2
    outs = [
        ((length, 3 * cols), BF),
        ((half, cols), BF),
        ((half, cols), BF),
        ((cols // HEAD_DIM, length), F32),
    ]
    count = 0
    if seq == 0:
        count = len(held[0])
        total = sum(pieces[0].shape[-1] for pieces in held)
        outs += [((width, total), BF), ((TABLE, width), F32)]
        held = [one for pieces in held for one in pieces]
    return run(
        functools.partial(attend_kernel, seq, count),
        "attend",
        (where, lengths),
        (mine, theirs, *held),
        outs,
    )


def attend_back(pair, where, lengths, qkv, lse, mine, theirs, tokens, held, widths):
    rows, width = tokens.shape
    return run(
        functools.partial(attend_back_kernel, pair, len(held), len(qkv)),
        "attend_back",
        (where, lengths),
        (*qkv, *lse, mine, theirs, tokens, *held),
        (((rows, 3 * PAIR), BF), ((1, 3 * PAIR), F32))
        + tuple(((width, one), BF) for one in widths),
    )


def on_chip(count):
    return [pl.BlockSpec(memory_space=pltpu.VMEM)] * count


def run(kernel, name, scalars, arrays, outs, grid=(1,), scratch=()):
    return pl.pallas_call(
        kernel,
        out_shape=tuple(jax.ShapeDtypeStruct(shape, kind) for shape, kind in outs),
        grid_spec=pltpu.PrefetchScalarGridSpec(
            num_scalar_prefetch=len(scalars),
            grid=grid,
            in_specs=on_chip(len(arrays)),
            out_specs=tuple(on_chip(len(outs))),
            scratch_shapes=scratch,
        ),
        compiler_params=pltpu.CompilerParams(vmem_limit_bytes=VMEM_LIMIT),
        cost_estimate=SMALL,
        name=name,
    )(*scalars, *arrays)


def span(step, extent):
    if isinstance(step, int):
        return pl.ds(step * extent, extent)
    return pl.ds(pl.multiple_of(step * extent, extent), extent)


def fill(target, pieces, sides):
    for piece, side in zip(pieces, sides):
        blocks, rows, _ = piece.shape
        for block in range(blocks):
            start = block * len(pieces) * rows
            if len(pieces) > 1:
                start = pl.multiple_of(start + side * rows, rows)
            target[pl.ds(start, rows), :] = piece[block]


class Layout:
    def __init__(self, chips, width, units):
        self.chips, self.width, self.units = chips, width, units
        self.cols = width // 2
        self.rows = width // chips
        self.block = units // chips
        self.fold = units // width
        self.split = self.rows % 16 == 0 and chips == 16
        self.packed = (self.fold + 1) * self.rows

    def scratch(self, rows):
        width, units, cols = self.width, self.units, self.cols
        if self.split:
            weights = [(self.chips, self.rows, units), (self.chips, self.rows, width)]
            weights += [(4, 4, self.block, width)]
        else:
            weights = [(width, units), (width, width), (units, width)]
        full, wide = (rows, width), (rows, units)
        low = weights + [full, (rows, cols), (rows, cols), full, wide, wide, full, full]
        low += [(2, units, cols), (2, self.fold, width, cols), (2, width, cols), (2, rows, cols)]
        high = [full, full, full, full]
        return [pltpu.VMEM(one, BF) for one in low] + [pltpu.VMEM(one, F32) for one in high]


def ffn_kernel(layout, count, where_ref, len_ref, table_ref, bias_ref, *refs):
    seqs = len_ref.shape[0]
    (tok_hbm, cot_hbm), refs = refs[:2], refs[2:]
    ctx_mine_hbm, ctx_theirs_hbm, refs = refs[:seqs], refs[seqs : 2 * seqs], refs[2 * seqs :]
    weights, refs = refs[:count], refs[count:]
    grads = 4 if layout.split else 6
    sums_two_ref, sums_one_ref, sums_inner_ref = refs[:3]
    (out_hbm, resid_hbm, gc_mine_hbm, gc_theirs_hbm), refs = refs[3:7], refs[7:]
    grad_hbm, refs = refs[:grads], refs[grads:]
    (
        inner_ref,
        mix_ref,
        outer_ref,
        tok_ref,
        mine_ref,
        theirs_ref,
        cot_ref,
        active_ref,
        slope_ref,
        low_ref,
        context_ref,
        stage_outer,
        stage_inner,
        stage_mix,
        stage_ctx,
        hidden_ref,
        normed_ref,
        out_ref,
        resid_ref,
        in_sems,
        out_sems,
    ) = refs
    width, units, cols = layout.width, layout.units, layout.cols
    core = where_ref[0]
    first = core == 0
    extent = units // 4
    loads = []

    def load(source, target):
        copy = pltpu.make_async_copy(source, target, in_sems.at[len(loads)])
        copy.start()
        loads.append(copy)
        return copy

    part = mine_ref.shape[0] // seqs
    small = [load(tok_hbm, tok_ref)]
    for seq in range(seqs):
        some = slice(seq * part, (seq + 1) * part)
        small.append(load(ctx_mine_hbm[seq], mine_ref.at[some, :]))
        small.append(load(ctx_theirs_hbm[seq], theirs_ref.at[some, :]))
    if layout.split:
        together = weights[0]
        rows = layout.rows
        last = layout.fold * rows
        mix_loads = [
            load(
                together.at[:, half, last : last + rows, :],
                mix_ref.at[:, :, half * cols : (half + 1) * cols],
            )
            for half in range(2)
        ]
        inner_loads = [
            [
                load(
                    together.at[:, tile // 2, place * rows : (place + 1) * rows, :],
                    inner_ref.at[
                        :,
                        :,
                        ((tile // 2) * layout.fold + place) * cols : (
                            (tile // 2) * layout.fold + place + 1
                        )
                        * cols,
                    ],
                )
                for place in range(
                    (tile % 2) * layout.fold // 2, (tile % 2 + 1) * layout.fold // 2
                )
            ]
            for tile in range(4)
        ]
        outer_loads = []
        for other in range(2):
            half = core ^ other
            for mask in range(4):
                outer_loads.append(
                    load(
                        weights[1 + 4 * other + mask],
                        outer_ref.at[:, where_ref[2] ^ mask, :, span(half, cols)],
                    )
                )
    else:
        mix_loads = [load(weights[0], mix_ref)]
        inner_loads = [[load(weights[1], inner_ref)], [], [], []]
        outer_loads = [load(weights[2], outer_ref)]
    cot_load = load(cot_hbm, cot_ref)

    def mix_half(half):
        lanes = slice(half * cols, (half + 1) * cols)
        if layout.split:
            return mix_ref[:, :, lanes].reshape(width, cols)
        return mix_ref[:, lanes]

    def inner_tile(tile):
        if layout.split:
            return inner_ref[:, :, span(tile, extent)].reshape(width, extent)
        return inner_ref[:, span(tile, extent)]

    def outer_tile(tile):
        if layout.split:
            return outer_ref[tile].reshape(extent, width)
        return outer_ref[span(tile, extent), :]

    stores = []

    def store(source, target):
        copy = pltpu.make_async_copy(source, target, out_sems.at[len(stores)])
        copy.start()
        stores.append(copy)

    for copy in small:
        copy.wait()
    context = ordered(first, mine_ref[...], theirs_ref[...], 1)
    context_ref[...] = context
    for copy in mix_loads:
        copy.wait()
    attn = jnp.concatenate([product(context, mix_half(half)) for half in range(2)], axis=1)
    normed, inv_one = normalize(
        tok_ref[...].astype(F32) + (attn + table_ref[B_OUT : B_OUT + 1])
    )
    normed_ref[...] = normed
    hidden = normed * table_ref[GAIN_ONE : GAIN_ONE + 1] + table_ref[SHIFT_ONE : SHIFT_ONE + 1]
    hidden_ref[...] = hidden
    low_ref[...] = hidden.astype(BF)
    for tile in range(4):
        for copy in inner_loads[tile]:
            copy.wait()
        lanes = slice(tile * extent, (tile + 1) * extent)
        pre = product(low_ref[...], inner_tile(tile)) + bias_ref[:, lanes]
        cumulative = 0.5 * (1.0 + lax.erf(pre * ROOT_HALF))
        active_ref[:, lanes] = (pre * cumulative).astype(BF)
        slope = cumulative + pre * jnp.exp(-0.5 * pre * pre) * INV_ROOT_TAU
        slope_ref[:, lanes] = slope.astype(BF)
    for copy in outer_loads:
        copy.wait()
    total = hidden_ref[...] + table_ref[B_OUTER : B_OUTER + 1]
    for tile in range(4):
        total += product(active_ref[:, tile * extent : (tile + 1) * extent], outer_tile(tile))
    normed, inv = normalize(total)
    gain = table_ref[GAIN_TWO : GAIN_TWO + 1]
    out_ref[...] = normed * gain + table_ref[SHIFT_TWO : SHIFT_TWO + 1]
    store(out_ref, out_hbm)
    half_length = normed.shape[0] // seqs
    position = core * half_length + lax.broadcasted_iota(jnp.int32, (half_length, 1), 0)
    live = jnp.concatenate(
        [jnp.where(position < len_ref[s], 1.0, 0.0) for s in range(seqs)], axis=0
    )
    cot_load.wait()
    grad = cot_ref[...].astype(F32) * live
    resid = normalize_back(grad, normed, inv, gain)
    grad_outer = resid.astype(BF)
    sums_two_ref[...] = column_sums(grad_outer, grad * normed, grad)
    resid_ref[...] = resid

    def halves(values):
        left, right = values[:, :cols], values[:, cols:]
        return jnp.where(first, right, left), jnp.where(first, left, right)

    rows = layout.rows
    for tile in range(4):
        lanes = slice(tile * extent, (tile + 1) * extent)
        found = product(active_ref[:, lanes].T, grad_outer).astype(BF)
        for other, columns in zip((1, 0), halves(found)):
            stage_outer[other, lanes, :] = columns
            if layout.split:
                near = extent // layout.block
                for chip in range(near):
                    start = tile * extent + chip * layout.block
                    store(
                        stage_outer.at[other, start : start + layout.block, :],
                        grad_hbm[other].at[tile * near + chip],
                    )
            else:
                store(
                    stage_outer.at[other, lanes, :],
                    grad_hbm[3 * other].at[lanes, :],
                )
    low_t = low_ref[...].T
    total = resid_ref[...]
    for other in (1, 0):
        for part in range(2):
            place = 2 * (core ^ other) + part
            grad = product_nt(grad_outer, outer_tile(place))
            grad = (grad * slope_ref[:, span(place, extent)].astype(F32)).astype(BF)
            sums_inner_ref[:, span(place, extent)] = jnp.sum(
                grad.astype(F32), axis=0, keepdims=True
            )
            total += product_nt(grad, inner_tile(place))
            found = product(low_t, grad).astype(BF)
            for i in range(layout.fold // 2):
                index = part * (layout.fold // 2) + i
                stage_inner[other, index] = found[:, i * cols : (i + 1) * cols]
                if layout.split:
                    start = index * rows
                    for chip in range(layout.chips):
                        store(
                            stage_inner.at[other, index, chip * rows : (chip + 1) * rows, :],
                            grad_hbm[2 + other].at[chip, start : start + rows, :],
                        )
                else:
                    store(
                        stage_inner.at[other, index],
                        grad_hbm[3 * other + 1].at[:, index * cols : (index + 1) * cols],
                    )
    normed = normed_ref[...]
    resid = normalize_back(total, normed, inv_one, table_ref[GAIN_ONE : GAIN_ONE + 1])
    resid_ref[...] = resid
    store(resid_ref, resid_hbm)
    attn = resid.astype(BF)
    sums_one_ref[...] = column_sums(attn, total * normed, total)
    back = product_nt(attn[:, :cols], mix_half(0)) + product_nt(attn[:, cols:], mix_half(1))
    for other, columns, target in zip(
        (1, 0), halves(back.astype(BF)), (gc_theirs_hbm, gc_mine_hbm)
    ):
        stage_ctx[other] = columns
        store(stage_ctx.at[other], target)
    context_t = context_ref[...].T
    for other, columns in zip((1, 0), halves(attn)):
        stage_mix[other] = product(context_t, columns).astype(BF)
        if layout.split:
            start = layout.fold * rows
            for chip in range(layout.chips):
                store(
                    stage_mix.at[other, chip * rows : (chip + 1) * rows, :],
                    grad_hbm[2 + other].at[chip, start : start + rows, :],
                )
        else:
            store(stage_mix.at[other], grad_hbm[3 * other + 2])
    for copy in stores:
        copy.wait()


def ffn(layout, where, lengths, table, bias, tokens, cotangent, mine, theirs, weights):
    rows, width = tokens.shape
    units, cols = layout.units, layout.cols
    full, part = (rows, width), (rows, cols)
    if layout.split:
        grads = [(layout.chips, layout.block, cols)] * 2
        grads += [(layout.chips, layout.packed, cols)] * 2
        loads = 1 + 2 * len(mine) + 2 + 2 * layout.fold + 8 + 1
        stores = 4 + 2 * layout.chips * (layout.fold + 2)
    else:
        grads = [(units, cols), (width, units // 2), (width, cols)] * 2
        loads = 5 + 2 * len(mine)
        stores = 4 + 2 * (4 + layout.fold + 1)
    anywhere = pl.BlockSpec(memory_space=pl.ANY)
    arrays = (tokens, cotangent, *mine, *theirs, *weights)
    outs = [((8, width), F32), ((8, width), F32), ((1, units), F32), (full, F32), (full, F32)]
    outs += [(part, BF)] * 2 + [(one, BF) for one in grads]
    return pl.pallas_call(
        functools.partial(ffn_kernel, layout, len(weights)),
        out_shape=tuple(jax.ShapeDtypeStruct(shape, kind) for shape, kind in outs),
        grid_spec=pltpu.PrefetchScalarGridSpec(
            num_scalar_prefetch=2,
            grid=(1,),
            in_specs=on_chip(2) + [anywhere] * len(arrays),
            out_specs=tuple(on_chip(3) + [anywhere] * (len(outs) - 3)),
            scratch_shapes=layout.scratch(rows)
            + [pltpu.SemaphoreType.DMA((loads,)), pltpu.SemaphoreType.DMA((stores,))],
        ),
        compiler_params=pltpu.CompilerParams(vmem_limit_bytes=58 << 20),
        cost_estimate=SMALL,
        name="ffn",
    )(where, lengths, table, bias, *arrays)


def token_kernel(count, where_ref, *refs):
    grad_refs = refs[:count]
    weight_ref, resid_ref, keep_ref, away_ref = refs[count:]
    half = resid_ref.shape[0]
    extent = grad_refs[0].shape[1]
    mine = where_ref[0] * half
    for start, target in ((half - mine, away_ref), (mine, keep_ref)):
        rows = pl.ds(pl.multiple_of(start, half), half)
        part = product_nt(grad_refs[0][rows, :], weight_ref[:, :extent])
        for i in range(1, count):
            part += product_nt(
                grad_refs[i][rows, :], weight_ref[:, i * extent : (i + 1) * extent]
            )
        if target is keep_ref:
            part += resid_ref[...]
        target[...] = part.astype(target.dtype)


def token_grads(where, grads, weight, resid, seqs):
    rows, cols = grads[0].shape
    width = resid.shape[1]
    length = rows // seqs

    def rowwise(extent, columns):
        return pl.BlockSpec((extent, columns), lambda i, *_: (i, 0))

    return pl.pallas_call(
        functools.partial(token_kernel, len(grads)),
        out_shape=(
            jax.ShapeDtypeStruct((rows // 2, width), F32),
            jax.ShapeDtypeStruct((rows // 2, width), BF),
        ),
        grid_spec=pltpu.PrefetchScalarGridSpec(
            num_scalar_prefetch=1,
            grid=(seqs,),
            in_specs=[rowwise(length, cols)] * len(grads)
            + [pl.BlockSpec(weight.shape, lambda *_: (0, 0)), rowwise(length // 2, width)],
            out_specs=(rowwise(length // 2, width), rowwise(length // 2, width)),
        ),
        compiler_params=pltpu.CompilerParams(vmem_limit_bytes=44 << 20),
        cost_estimate=SMALL,
        name="token_grads",
    )(where, *grads, weight, resid)


def combine_kernel(plan, count, where_ref, *refs):
    arrays, refs = refs[:count], refs[count:]
    outs, refs = refs[: len(plan)], refs[len(plan) :]
    buffers, sems = refs[:-1], refs[-1]

    def place(entry):
        if entry is None:
            return slice(None)
        if entry[0] == "side":
            return ((where_ref[1] >> entry[1]) & 1) ^ entry[2]
        if entry[0] == "far":
            return (where_ref[1] >> 2) ^ entry[1]
        return pl.ds(*entry)

    copies = []
    for _, parts in plan:
        for terms, _ in parts:
            for number, index in terms:
                source = arrays[number].at[tuple(place(entry) for entry in index)]
                at = len(copies)
                copies.append(pltpu.make_async_copy(source, buffers[at], sems.at[at]))
                copies[-1].start()
    at = 0
    for (kind, parts), out in zip(plan, outs):
        for terms, window in parts:
            total = None
            for _ in terms:
                copies[at].wait()
                one = buffers[at][...].astype(F32)
                total = one if total is None else total + one
                at += 1
            if window is None:
                out[...] = total.astype(kind)
            else:
                out[window] = total.astype(kind)


def combine(where, jobs, room=None):
    arrays, plan, buffers = [], [], []

    def number(array):
        for i, one in enumerate(arrays):
            if one is array:
                return i
        arrays.append(array)
        return len(arrays) - 1

    for kind, _, parts in jobs:
        planned = []
        for terms, window in parts:
            numbered = []
            for array, index in terms:
                shape = []
                for extent, entry in zip(array.shape, index):
                    if entry is None:
                        shape.append(extent)
                    elif entry[0] not in ("side", "far"):
                        shape.append(entry[1])
                buffers.append(pltpu.VMEM(tuple(shape), array.dtype))
                numbered.append((number(array), tuple(index)))
            planned.append((numbered, window))
        plan.append((kind, planned))
    return pl.pallas_call(
        functools.partial(combine_kernel, plan, len(arrays)),
        out_shape=tuple(jax.ShapeDtypeStruct(shape, kind) for kind, shape, _ in jobs),
        grid_spec=pltpu.PrefetchScalarGridSpec(
            num_scalar_prefetch=1,
            grid=(1,),
            in_specs=[pl.BlockSpec(memory_space=pl.ANY)] * len(arrays),
            out_specs=tuple(on_chip(len(jobs))),
            scratch_shapes=buffers + [pltpu.SemaphoreType.DMA((len(buffers),))],
        ),
        compiler_params=pltpu.CompilerParams(vmem_limit_bytes=room or VMEM_LIMIT),
        cost_estimate=SMALL,
        name="combine",
    )(where, *arrays)


class Sum:
    def __init__(self, terms, flying=()):
        self.terms, self.flying = list(terms), list(flying)


jax.tree_util.register_pytree_node(
    Sum,
    lambda held: (
        ([array for array, _, _ in held.terms], [array for array, _ in held.flying]),
        (
            tuple((bits, window) for _, bits, window in held.terms),
            tuple(mask for _, mask in held.flying),
        ),
    ),
    lambda fixed, arrays: Sum(
        [(array, *about) for array, about in zip(arrays[0], fixed[0])], zip(arrays[1], fixed[1])
    ),
)


def tie(values):
    return lax.optimization_barrier(values)


def after(values, *others):
    return tie((values, others))[0]


def masks(digit):
    found = [0]
    for bit in digit:
        found += [one | (1 << bit) for one in found]
    return found[1:]


class Wires:
    def __init__(self):
        self.chips = lax.axis_size(CHIPS)
        self.bits = self.chips.bit_length() - 1
        self.chip = lax.axis_index(CHIPS)
        self.core = lax.axis_index("seq")
        self.first = self.core == 0
        self.room = None
        far = list(range(self.bits - 1, 1, -1))
        self.far = [tuple(far[i : i + 2]) for i in range(0, len(far), 2)]

    def side(self, bit):
        return (self.chip >> bit) & 1

    def meet(self, values, mask):
        return lax.ppermute(values, CHIPS, [(i, i ^ mask) for i in range(self.chips)])

    def swap_core(self, values):
        return lax.ppermute(values, "seq", [(0, 1), (1, 0)])

    def pick(self, low, high):
        return jnp.where(self.first, low, high), jnp.where(self.first, high, low)

    def columns(self, values):
        cols = values.shape[1] // 2
        return self.pick(values[:, :cols], values[:, cols:])

    def beside(self, mine, theirs, side, axis):
        shape = [1] * (mine.ndim + 1)
        shape[axis] = 2
        here = lax.broadcasted_iota(jnp.int32, tuple(shape), axis) == side
        return jnp.where(here, jnp.expand_dims(mine, axis), jnp.expand_dims(theirs, axis))


    def far_meet(self, values, digit):
        return {0: values} | {mask: self.meet(values, mask) for mask in masks(digit)}

    def far_join(self, found, digit):
        shape = found[0].shape
        for bit in reversed(digit):
            known = {mask for mask in found if not mask & (1 << bit)}
            found = {
                mask: self.beside(found[mask], found[mask | (1 << bit)], self.side(bit), 1)
                for mask in sorted(known)
            }
        return found[0].reshape((-1,) + shape[1:])

    def gather_far(self, values, digit):
        return self.far_join(self.far_meet(values, digit), digit)

    def gather_near(self, values, bit):
        return self.beside(values, self.meet(values, 1 << bit), self.side(bit), 1)

    def pieces(self, values, bit):
        width = values.shape[-1]
        rows = values.shape[-2] << bit
        values = values.reshape(-1, rows, width)
        return values, self.meet(values, 1 << bit)

    def gather_plane(self, values):
        return [values] + [self.meet(values, mask) for mask in masks((0, 1))]

    def plane(self, pieces):
        own = self.chip & 3
        stacked = jnp.stack(pieces, axis=1)
        parts = [
            lax.dynamic_index_in_dim(stacked, own ^ place, 1, keepdims=False) for place in range(4)
        ]
        return jnp.concatenate(parts, axis=1)

    def whole(self, pieces, bit):
        width = pieces[0].shape[-1]
        return self.beside(pieces[0], pieces[1], self.side(bit), 1).reshape(-1, width)


    def spread(self, terms, tail, windows):
        bits = tuple(range(self.bits - 1, -1, -1))
        arrays = [one.reshape([2] * self.bits + list(tail)) for one in terms]
        return [Sum([(one, bits, window) for one in arrays]) for window in windows]

    def part(self, held, fixed):
        total = None
        for array, bits, window in held.terms:
            tail = array.shape[len(bits) :]
            first, size = window if window else ((0,) * len(tail), tail)
            starts = [fixed.get(bit, 0) for bit in bits] + list(first)
            sizes = [1 if bit in fixed else 2 for bit in bits] + list(size)
            shape = [2 for bit in bits if bit not in fixed] + list(size)[-2:]
            one = lax.dynamic_slice(array, starts, sizes).reshape(shape).astype(F32)
            total = one if total is None else total + one
        return total

    def left(self, held):
        return held.terms[-1][1]

    def settled(self, held):
        return {bit: self.side(bit) for bit in range(self.bits) if bit not in self.left(held)}

    def ready(self, held, digit):
        fixed = self.settled(held)
        sent = []
        for mask in masks(digit):
            away = {bit: self.side(bit) ^ ((mask >> bit) & 1) for bit in digit}
            sent.append((self.part(held, {**fixed, **away}).astype(BF), mask))
        return Sum(held.terms, sent)

    def go(self, held):
        return Sum(held.terms, [(self.meet(one, mask), mask) for one, mask in held.flying])

    def land(self, held, digit):
        bits = tuple(bit for bit in self.left(held) if bit not in digit)
        return Sum(held.terms + [(one, bits, None) for one, _ in held.flying])

    def total(self, held):
        return self.part(held, self.settled(held))


    def slices(self, held, stream, step, far=None):
        first, second = stream, 1 - stream
        near = {first: ("side", first, 1 - min(step, 1)), second: None}
        if step > 0:
            near[second] = ("side", second, 2 - step)
        found = []
        for array, bits, window in held.terms:
            tail = array.shape[len(bits) :]
            shape = (4,) + (2,) * (len(bits) - 2) + tail
            index = [far] + [near[bit] for bit in bits[2:]]
            if window is None:
                index += [None] * len(tail)
            else:
                index += list(zip(*window))
            found.append((array.reshape(shape), index))
        return found

    def extent(self, held):
        array, bits, window = held.terms[0]
        return tuple(window[1]) if window else array.shape[len(bits) :]

    def near_ready(self, pair, step):
        if not self.kernels:
            return [self.ready(held, (stream ^ step,)) for stream, held in enumerate(pair)]
        jobs = []
        for stream, held in enumerate(pair):
            shape = (4,) + (2,) * (1 - step) + self.extent(held)
            jobs.append((BF, shape, [(self.slices(held, stream, step), None)]))
        sent = combine(self.where, jobs, self.room)
        return [
            Sum(
                held.terms,
                [(one.reshape((2,) * (3 - step) + self.extent(held)), 1 << (stream ^ step))],
            )
            for stream, (held, one) in enumerate(zip(pair, sent))
        ]

    def far_parts(self, pair, axis, far):
        parts, begin, extents = [], 0, []
        for stream, held in enumerate(pair):
            extent = self.extent(held)
            window = [slice(None)] * (2 + (far is None))
            window[axis] = slice(begin, begin + extent[axis])
            begin += extent[axis]
            extents.append(extent)
            parts.append((self.slices(held, stream, 2, far), tuple(window)))
        shape = list(extents[0])
        shape[axis] = begin
        return tuple(shape), parts

    def far_ready(self, pair, axis):
        if not self.kernels:
            held = self.far_steps(self.joined(pair, axis))
            held = self.ready(held, self.far[-1])
            own = {bit: self.side(bit) for bit in range(self.bits)}
            return self.part(held, own), [one for one, _ in held.flying]
        jobs = []
        for mask in [0] + masks(self.far[-1]):
            shape, parts = self.far_parts(pair, axis, ("far", mask >> 2))
            jobs.append((BF if mask else F32, shape, parts))
        kept, *sent = combine(self.where, jobs, self.room)
        return kept, sent

    def far_go(self, held):
        kept, sent = held
        return kept, [self.meet(one, mask) for one, mask in zip(sent, masks(self.far[-1]))]

    def far_total(self, held):
        kept, arrived = held
        for one in arrived:
            kept = kept + one.astype(F32)
        return kept

    def far_rows(self, pair, axis):
        if self.kernels:
            shape, parts = self.far_parts(pair, axis, None)
            array = combine(self.where, [(BF, (4,) + shape, parts)], self.room)[0]
        else:
            array = self.joined(pair, axis).terms[0][0]
        return lax.psum_scatter(
            array.reshape(-1, array.shape[-1]), "far", scatter_dimension=0, tiled=True
        )

    def near_go(self, pair):
        return [self.go(held) for held in pair]

    def near_land(self, pair, step):
        return [self.land(held, (stream ^ step,)) for stream, held in enumerate(pair)]

    def joined(self, pair, axis):
        sums = [self.total(held).astype(BF) for held in pair]
        return Sum([(jnp.concatenate(sums, axis=axis), self.left(pair[0]), None)])

    def far_steps(self, held):
        for digit in self.far[:-1]:
            held = self.land(self.go(self.ready(held, digit)), digit)
        return held

    def owned(self, block):
        rows = block.shape[0] // 2
        return self.pick(block[:rows], block[rows:])


def body(tokens, lengths, cotangent, *shards):
    (
        w_query,
        b_query,
        w_key,
        w_value,
        b_value,
        w_out,
        b_out,
        gain_one,
        shift_one,
        w_inner,
        b_inner,
        w_outer,
        b_outer,
        gain_two,
        shift_two,
    ) = shards
    wires = Wires()
    core = wires.core
    devices = 2 * wires.chips
    seqs, half, width = tokens.shape
    rows = seqs * half
    cols = width // 2
    slot = b_query.shape[0]
    fold = b_inner.shape[0] // slot
    plane = wires.chip & 3
    where = jnp.stack([core, wires.chip, plane, wires.side(0), wires.side(1)]).astype(jnp.int32)

    vectors = jnp.stack(
        [b_query, b_value, b_out, gain_one, shift_one, b_outer, gain_two, shift_two]
    )
    vectors = jnp.concatenate([vectors, b_inner.reshape(fold, slot)], axis=0)
    vectors = jnp.pad(vectors.T, ((0, 0), (0, LANES - vectors.shape[0])))
    mine, away = zip(*[wires.columns(one) for one in (w_query, w_key, w_value, w_out, w_inner)])
    pairs = cols // PAIR

    def by_pair(parts):
        spans = [slice(p * PAIR, (p + 1) * PAIR) for p in range(pairs)]
        return jnp.concatenate([one[:, span] for span in spans for one in parts] + [vectors], axis=1)

    def both_rows(kept, sent):
        return ordered(wires.first, kept, wires.swap_core(sent), 0)

    units = w_inner.shape[1]
    paired = 2 * slot
    layout = Layout(wires.chips, width, units)
    aligned = wires.kernels = layout.split
    wires.where = where
    first = both_rows(by_pair(mine[:3]), by_pair(away[:3]))[None]
    outer_mine, outer_away = wires.columns(w_outer)
    outer_held = both_rows(outer_mine, outer_away)[None]
    if aligned:
        parts = [jnp.concatenate([inner, out], axis=1) for out, inner in (mine[3:], away[3:])]
        second = both_rows(*parts)
        second = jnp.concatenate(
            [second[:, i : i + cols] for i in range(0, second.shape[1], cols)], axis=0
        )
        second = lax.all_gather(second, CHIPS + ("seq",), axis=0, tiled=True)
        weights = [second.reshape(wires.chips, 2, -1, cols)]
    else:
        weights = [
            lax.all_gather(one, CHIPS + ("seq",), axis=0, tiled=True)
            for one in (w_out, w_inner, w_outer)
        ]
    for digit in wires.far:
        first = wires.gather_far(first, digit)
    first, outer_held = tie((first, outer_held))
    for digit in wires.far[:-1]:
        outer_held = wires.gather_far(outer_held, digit)
    outer_held = wires.far_meet(outer_held, wires.far[-1])
    cut = (3 * pairs + 1) // 2 * LANES
    one = wires.gather_near(first[..., :cut], 1)
    two = wires.gather_near(first[..., cut:], 0)
    pieces_one, pieces_two = wires.pieces(one, 0), wires.pieces(two, 1)
    if not aligned:
        pieces_one, pieces_two = [
            (wires.whole(pieces, bit)[None],)
            for bit, pieces in enumerate((pieces_one, pieces_two))
        ]
    tok_rows = tokens.reshape(rows, width)
    tok_other = wires.swap_core(tokens)
    tok_all = ordered(wires.first, tokens, tok_other, 1).reshape(2 * rows, width)

    held = attend(0, where, lengths, tokens, tok_other, (pieces_one, pieces_two))
    w_qkv, table = held[4:]
    heads = [held[:4]]
    if aligned:
        w_qkv, table, outer_held = tie((w_qkv, table, outer_held))
        outer_held = wires.gather_plane(wires.far_join(outer_held, wires.far[-1]))
    for seq in range(1, seqs):
        heads.append(attend(seq, where, lengths, tokens, tok_other, (w_qkv, table)))
    qkv, ctx_mine, ctx_away, lse = zip(*heads)
    ctx_theirs = [wires.swap_core(one) for one in ctx_away]
    if aligned:
        ctx_theirs, outer_held = tie((ctx_theirs, outer_held))
        weights += outer_held + [wires.swap_core(one) for one in outer_held]
    kept = 8 + fold
    bias_inner = table[8:kept].reshape(fold, devices, slot).transpose(1, 0, 2).reshape(1, -1)
    results = ffn(
        layout,
        where,
        lengths,
        table,
        bias_inner,
        tok_rows,
        cotangent.reshape(rows, width),
        ctx_mine,
        ctx_theirs,
        weights,
    )
    sums_two, sums_one, sums_inner, output, resid_one, gc_mine, gc_away = results[:7]
    grad_parts = results[7:]
    if not aligned:

        def by_chip(many):
            g_outer, g_inner, g_out = many
            g_inner = g_inner.reshape(wires.chips, -1, fold, cols).transpose(0, 2, 1, 3)
            others = (g_inner.reshape(wires.chips, -1, cols), g_out.reshape(wires.chips, -1, cols))
            return g_outer.reshape(wires.chips, -1, cols), jnp.concatenate(others, axis=1)

        mine, away = by_chip(grad_parts[:3]), by_chip(grad_parts[3:])
        grad_parts = (mine[0], away[0], mine[1], away[1])
    g_outer, g_outer_away, g_rest, g_rest_away = grad_parts

    last = wires.far[-1]
    rows_chip = 2 * slot
    gc_theirs = wires.swap_core(gc_away)
    base = jnp.concatenate(
        [
            jnp.zeros((2, width), F32),
            sums_one[:3],
            sums_two[:3],
            sums_inner.reshape(devices, fold, slot).transpose(1, 0, 2).reshape(fold, width),
            jnp.zeros((TABLE - kept, width), F32),
        ],
        axis=0,
    )

    def two_windows(held, theirs):
        extent = held.shape[1]
        cut = extent // 2 // 16 * 16 if aligned else extent // 2
        return wires.spread(
            [held, theirs],
            (extent, cols),
            [((0, 0), (cut, cols)), ((cut, 0), (extent - cut, cols))],
        )

    def attention_grad(pair, held, widths):
        return attend_back(
            pair, where, lengths, qkv, lse, gc_mine, gc_theirs, tok_all, held, widths
        )

    pair_width = 3 * PAIR
    more = (3 * pairs + 1) // 2 * LANES - pair_width
    arrived = wires.swap_core(g_outer_away)
    g_rest_away = after(g_rest_away, arrived)
    outer = wires.near_ready(two_windows(g_outer, arrived), 0)
    gc_mine, outer = tie((gc_mine, outer))
    outer = wires.near_go(outer)
    grad_one, sums_first, g_first = attention_grad(0, (), (pair_width,))
    arrived = wires.swap_core(g_rest_away)
    grad_one, arrived, base = tie((grad_one, arrived, base))
    rest = wires.near_ready(two_windows(g_rest, arrived), 0)
    gc_mine, rest = tie((gc_mine, rest))
    rest = wires.near_go(rest)
    grad_two, sums_second, g_one, g_kept = attention_grad(
        1, (g_first,), (pair_width + more, pair_width - more)
    )
    grad_two, outer = tie((grad_two, outer))
    outer = wires.near_ready(wires.near_land(outer, 0), 1)
    gc_mine, outer = tie((gc_mine, outer))
    outer = wires.near_go(outer)
    grad_three, _, g_two = attention_grad(
        2,
        (g_kept, base, sums_first, sums_second),
        (2 * pair_width - more + LANES,),
    )
    grads = [grad_one, grad_two, grad_three]
    grads, rest = tie((grads, rest))
    rest = wires.near_ready(wires.near_land(rest, 0), 1)
    g_one, g_two, rest = tie((g_one, g_two, rest))
    rest = wires.near_go(rest)
    both = [wires.spread([one], (rows_chip, one.shape[1]), [None])[0] for one in (g_one, g_two)]
    both = wires.near_ready(both, 0)
    grads, both = tie((grads, both))
    both = wires.near_go(both)
    tok_keep, tok_away = token_grads(where, grads, w_qkv, resid_one, seqs)
    tok_away, tok_keep, outer = tie((tok_away, tok_keep, outer))
    g_outer = wires.far_rows(wires.near_land(outer, 1), -2)
    tok_away, rest, both = tie((tok_away, rest, both))
    wires.room = 60 << 20
    tok_theirs = wires.swap_core(tok_away)
    both = wires.near_ready(wires.near_land(both, 0), 1)
    rest = after(rest, both)
    g_rest = wires.far_rows(wires.near_land(rest, 1), -2)
    tok_keep, both = tie((tok_keep, both))
    both = wires.near_go(both)
    both, tok_theirs = tie((both, tok_theirs))
    both = wires.far_ready(wires.near_land(both, 1), -1)
    both, tok_theirs, tok_keep = tie((both, tok_theirs, tok_keep))
    both = wires.far_go(both)
    grad_tok = tok_keep + tok_theirs.astype(F32)
    g_rest = after(g_rest, both[1]).astype(F32)
    g_both = wires.far_total(both)

    columns = [g_both] + [
        g_rest[i * rows_chip : (i + 1) * rows_chip] for i in range(fold + 1)
    ]
    mine, away = wires.owned(jnp.concatenate(columns, axis=1))
    theirs = wires.swap_core(away)
    mine_outer, away = wires.owned(g_outer.astype(F32))
    g_outer = ordered(wires.first, mine_outer, wires.swap_core(away), 1)
    begin = g_both.shape[1]

    def full(spans):
        return jnp.concatenate(
            [one[:, span] for one in wires.pick(mine, theirs) for span in spans], axis=1
        )

    pieces = [
        full([slice((3 * p + i) * PAIR, (3 * p + i + 1) * PAIR) for p in range(pairs)])
        for i in range(3)
    ]
    pieces.append(full([slice(begin + fold * cols, begin + (fold + 1) * cols)]))
    pieces.append(full([slice(begin, begin + fold * cols)]))
    vectors = slice(begin - LANES, begin)
    small = (mine[:, vectors] + theirs[:, vectors]).T

    return (
        output.reshape(seqs, half, width),
        grad_tok.reshape(seqs, half, width),
        pieces[0],
        small[0],
        pieces[1],
        pieces[2],
        small[1],
        pieces[3],
        small[2],
        small[3],
        small[4],
        pieces[4],
        small[8:kept].reshape(-1),
        g_outer,
        small[5],
        small[6],
        small[7],
    )


def solution(mesh):
    cores = mesh.shape["seq"]
    split = Mesh(mesh.devices.reshape(-1, 2, 2, cores), CHIPS + ("seq",))
    every = CHIPS + ("seq",)
    matrix, vector = P(every, None), P(every)
    rows = P(CHIPS, "seq", None)
    weights = (matrix, vector, matrix, matrix, vector, matrix, vector, vector, vector)
    weights += (matrix, vector, matrix, vector, vector, vector)
    return jax.shard_map(
        body,
        mesh=split,
        in_specs=(rows, P(CHIPS), rows) + weights,
        out_specs=(rows, rows) + weights,
        check_vma=False,
    )
```

```python
import functools

import jax
import jax.numpy as jnp
from jax import lax
from jax.experimental import pallas as pl
from jax.experimental.pallas import tpu as pltpu
from jax.sharding import Mesh
from jax.sharding import PartitionSpec as P

HEAD_DIM = 64
PAIR = 2 * HEAD_DIM
LANES = 128
NEG_BIG = -1000000000.0
EPSILON = 1e-05
ROOT_HALF = 0.7071067811865476
INV_ROOT_TAU = 0.3989422804014327
BF = jnp.bfloat16
CHIPS = ("far", "mid", "low")
F32 = jnp.float32
VMEM_LIMIT = 20 << 20
SMALL = pl.CostEstimate(flops=1024, transcendentals=0, bytes_accessed=1024)

B_QUERY, B_VALUE, B_OUT, GAIN_ONE, SHIFT_ONE, B_OUTER, GAIN_TWO, SHIFT_TWO, B_INNER = range(9)
TABLE = 16


def product(left, right):
    return jnp.dot(left, right, preferred_element_type=F32)


def product_tn(left, right):
    return lax.dot_general(left, right, (((0,), (0,)), ((), ())), preferred_element_type=F32)


def product_nt(left, right):
    return lax.dot_general(left, right, (((1,), (1,)), ((), ())), preferred_element_type=F32)


def ordered(first, mine, theirs, axis):
    return jnp.concatenate([jnp.where(first, mine, theirs), jnp.where(first, theirs, mine)], axis)


def row_mean(values):
    return jnp.mean(values, axis=-1, keepdims=True)


def normalize(values):
    center = values - row_mean(values)
    inv_spread = lax.rsqrt(row_mean(center * center) + EPSILON)
    return center * inv_spread, inv_spread


def normalize_back(grad_out, normed, inv_spread, gain):
    grad_normed = grad_out * gain
    centered = grad_normed - row_mean(grad_normed)
    return inv_spread * (centered - normed * row_mean(grad_normed * normed))


def column_sums(*values):
    rows = [jnp.sum(one.astype(F32), axis=0, keepdims=True) for one in values]
    pad = jnp.zeros((8 - len(rows), rows[0].shape[1]), F32)
    return jnp.concatenate(rows + [pad], axis=0)


def attend_kernel(seq, count, where_ref, len_ref, mine_ref, theirs_ref, *refs):
    held = (refs[:count], refs[count : 2 * count])
    refs = refs[2 * count :]
    if count == 0:
        refs = refs[2:] + refs[:2]
    qkv_ref, ctx_mine_ref, ctx_theirs_ref, lse_ref, weight_ref, table_ref = refs
    core = where_ref[0]
    first = core == 0
    seen_to = len_ref[seq]
    width = weight_ref.shape[0]
    cols = width // 2

    if count > 0:
        start = 0
        for stream, pieces in enumerate(held):
            side = where_ref[3 + stream]
            extent = pieces[0].shape[-1]
            fill(weight_ref.at[:, start : start + extent], pieces, (side, 1 - side))
            start += extent
        last = weight_ref.shape[1] - LANES
        chosen = lax.broadcasted_iota(jnp.int32, (TABLE, LANES), 0)
        chosen = chosen == lax.broadcasted_iota(jnp.int32, (TABLE, LANES), 1)
        table_ref[...] = product_nt(
            jnp.where(chosen, 1.0, 0.0).astype(BF), weight_ref[:, last:]
        )

    def own(row):
        return jnp.where(first, table_ref[row : row + 1, :cols], table_ref[row : row + 1, cols:])

    tokens = ordered(first, mine_ref[seq], theirs_ref[seq], 0)
    length = tokens.shape[0]
    bias_q, bias_v = own(B_QUERY), own(B_VALUE)
    seen = lax.broadcasted_iota(jnp.int32, (length, length), 0) < seen_to
    lane = lax.broadcasted_iota(jnp.int32, (length, PAIR), 1)
    for pair in range(cols // PAIR):
        lanes = slice(pair * PAIR, (pair + 1) * PAIR)
        project = product(tokens, weight_ref[:, 3 * pair * PAIR : 3 * (pair + 1) * PAIR])
        queries = (project[:, :PAIR] + bias_q[:, lanes]).astype(BF)
        keys = project[:, PAIR : 2 * PAIR].astype(BF)
        values = (project[:, 2 * PAIR :] + bias_v[:, lanes]).astype(BF)
        qkv_ref[:, 3 * pair * PAIR : 3 * (pair + 1) * PAIR] = jnp.concatenate(
            [queries, keys, values], axis=1
        )
        queries = queries * BF(HEAD_DIM ** (-0.5))
        values_t = values.T
        parts = []
        for head in range(2):
            mask = (lane >= head * HEAD_DIM) & (lane < (head + 1) * HEAD_DIM)
            scores = product_nt(jnp.where(mask, keys, BF(0)), queries)
            scores = jnp.where(seen, scores, NEG_BIG)
            top = jnp.max(scores, axis=0, keepdims=True)
            weights = jnp.exp(scores - top)
            total = jnp.sum(weights, axis=0, keepdims=True)
            probs = (weights * (1.0 / total)).astype(BF)
            parts.append(product(values_t[head * HEAD_DIM : (head + 1) * HEAD_DIM], probs))
            row = 2 * pair + head
            lse_ref[row : row + 1, :] = top + jnp.log(total)
        context = jnp.concatenate(parts, axis=0).T.astype(BF)
        low, high = context[: length // 2], context[length // 2 :]
        ctx_mine_ref[:, lanes] = jnp.where(first, low, high)
        ctx_theirs_ref[:, lanes] = jnp.where(first, high, low)


def attend_back_kernel(pair, extras, seqs, where_ref, len_ref, *refs):
    qkv_refs, lse_refs, refs = refs[:seqs], refs[seqs : 2 * seqs], refs[2 * seqs :]
    mine_ref, theirs_ref, tok_ref, *refs = refs
    held, refs = refs[:extras], refs[extras:]
    grad_ref, sums_ref, *weight_refs = refs
    first = where_ref[0] == 0
    scale = BF(HEAD_DIM ** (-0.5))
    length = qkv_refs[0].shape[0]
    start = 3 * pair * PAIR
    lanes = slice(pair * PAIR, (pair + 1) * PAIR)
    lane = lax.broadcasted_iota(jnp.int32, (length, PAIR), 1)
    key_row = lax.broadcasted_iota(jnp.int32, (length, length), 0)
    sums = total = None
    for seq, (qkv_ref, lse_ref) in enumerate(zip(qkv_refs, lse_refs)):
        rows = slice(seq * length, (seq + 1) * length)
        half_rows = slice(seq * length // 2, (seq + 1) * length // 2)
        seen = key_row < len_ref[seq]
        queries = qkv_ref[:, start : start + PAIR] * scale
        keys = qkv_ref[:, start + PAIR : start + 2 * PAIR]
        values = qkv_ref[:, start + 2 * PAIR : start + 3 * PAIR]
        grad = ordered(first, mine_ref[half_rows, lanes], theirs_ref[half_rows, lanes], 0)
        keys_t = (keys * scale).T
        dq, dk, dv = [], [], []
        for head in range(2):
            own = (lane >= head * HEAD_DIM) & (lane < (head + 1) * HEAD_DIM)
            scores = product_nt(jnp.where(own, keys, BF(0)), queries)
            scores = jnp.where(seen, scores, NEG_BIG)
            row = 2 * pair + head
            probs = jnp.exp(scores - lse_ref[row : row + 1, :])
            grad_probs = product_nt(jnp.where(own, values, BF(0)), grad)
            row_term = jnp.sum(probs * grad_probs, axis=0, keepdims=True)
            grad_scores = (probs * (grad_probs - row_term)).astype(BF)
            dv.append(product(probs.astype(BF), grad))
            dk.append(product(grad_scores, queries))
            dq.append(product(keys_t[head * HEAD_DIM : (head + 1) * HEAD_DIM], grad_scores))
        own = lane < HEAD_DIM
        all_three = [
            jnp.concatenate(dq, axis=0).T.astype(BF),
            jnp.where(own, dk[0], dk[1]).astype(BF),
            jnp.where(own, dv[0], dv[1]).astype(BF),
        ]
        grads = jnp.concatenate(all_three, axis=1)
        grad_ref[rows, :] = grads
        one = jnp.sum(grads.astype(F32), axis=0, keepdims=True)
        weight = product(tok_ref[rows, :].T, grads)
        sums = one if sums is None else sums + one
        total = weight if total is None else total + weight
    sums_ref[...] = sums
    found = total.astype(BF)
    extent = found.shape[1]
    if pair == 0:
        weight_refs[0][...] = found
    elif extras == 1:
        more = weight_refs[0].shape[1] - extent
        weight_refs[0][:, :extent] = held[0][...]
        weight_refs[0][:, extent:] = found[:, :more]
        weight_refs[1][...] = found[:, more:]
    else:
        kept = held[0].shape[1]
        weight_refs[0][:, :kept] = held[0][...]
        weight_refs[0][:, kept : kept + extent] = found
        many = [one[...] for one in held[2:]] + [sums]
        blank = jnp.zeros((1, many[0].shape[1] // 3 * len(many)), F32)
        table = held[1][...]
        place = lax.broadcasted_iota(jnp.int32, table.shape, 0)
        for number, begin in ((B_QUERY, 0), (B_VALUE, 2 * PAIR)):
            row = jnp.concatenate([one[:, begin : begin + PAIR] for one in many], axis=1)
            row = jnp.concatenate(
                [jnp.where(first, row, blank), jnp.where(first, blank, row)], axis=1
            )
            table = jnp.where(place == number, row, table)
        chosen = lax.broadcasted_iota(jnp.int32, (TABLE, LANES), 0)
        chosen = chosen == lax.broadcasted_iota(jnp.int32, (TABLE, LANES), 1)
        weight_refs[0][:, kept + extent :] = product_tn(
            table.astype(BF), jnp.where(chosen, 1.0, 0.0).astype(BF)
        ).astype(BF)


def attend(seq, where, lengths, mine, theirs, held):
    half, width = mine.shape[1:]
    length = 2 * half
    cols = width // 2
    outs = [
        ((length, 3 * cols), BF),
        ((half, cols), BF),
        ((half, cols), BF),
        ((cols // HEAD_DIM, length), F32),
    ]
    count = 0
    if seq == 0:
        count = len(held[0])
        total = sum(pieces[0].shape[-1] for pieces in held)
        outs += [((width, total), BF), ((TABLE, width), F32)]
        held = [one for pieces in held for one in pieces]
    return run(
        functools.partial(attend_kernel, seq, count),
        "attend",
        (where, lengths),
        (mine, theirs, *held),
        outs,
    )


def attend_back(pair, where, lengths, qkv, lse, mine, theirs, tokens, held, widths):
    rows, width = tokens.shape
    return run(
        functools.partial(attend_back_kernel, pair, len(held), len(qkv)),
        "attend_back",
        (where, lengths),
        (*qkv, *lse, mine, theirs, tokens, *held),
        (((rows, 3 * PAIR), BF), ((1, 3 * PAIR), F32))
        + tuple(((width, one), BF) for one in widths),
    )


def on_chip(count):
    return [pl.BlockSpec(memory_space=pltpu.VMEM)] * count


def run(kernel, name, scalars, arrays, outs, grid=(1,), scratch=()):
    return pl.pallas_call(
        kernel,
        out_shape=tuple(jax.ShapeDtypeStruct(shape, kind) for shape, kind in outs),
        grid_spec=pltpu.PrefetchScalarGridSpec(
            num_scalar_prefetch=len(scalars),
            grid=grid,
            in_specs=on_chip(len(arrays)),
            out_specs=tuple(on_chip(len(outs))),
            scratch_shapes=scratch,
        ),
        compiler_params=pltpu.CompilerParams(vmem_limit_bytes=VMEM_LIMIT),
        cost_estimate=SMALL,
        name=name,
    )(*scalars, *arrays)


def span(step, extent):
    if isinstance(step, int):
        return pl.ds(step * extent, extent)
    return pl.ds(pl.multiple_of(step * extent, extent), extent)


def fill(target, pieces, sides):
    for piece, side in zip(pieces, sides):
        blocks, rows, _ = piece.shape
        for block in range(blocks):
            start = block * len(pieces) * rows
            if len(pieces) > 1:
                start = pl.multiple_of(start + side * rows, rows)
            target[pl.ds(start, rows), :] = piece[block]


class Layout:
    def __init__(self, chips, width, units):
        self.chips, self.width, self.units = chips, width, units
        self.cols = width // 2
        self.rows = width // chips
        self.block = units // chips
        self.fold = units // width
        self.split = self.rows % 16 == 0 and chips == 16
        self.packed = (self.fold + 1) * self.rows

    def scratch(self, rows):
        width, units, cols = self.width, self.units, self.cols
        if self.split:
            weights = [(self.chips, self.rows, units), (self.chips, self.rows, width)]
            weights += [(4, 4, self.block, width)]
        else:
            weights = [(width, units), (width, width), (units, width)]
        full, wide = (rows, width), (rows, units)
        low = weights + [full, (rows, cols), (rows, cols), full, wide, wide, full, full]
        low += [(2, units, cols), (2, self.fold, width, cols), (2, width, cols), (2, rows, cols)]
        high = [full, full, full, full]
        return [pltpu.VMEM(one, BF) for one in low] + [pltpu.VMEM(one, F32) for one in high]


def ffn_kernel(layout, count, where_ref, len_ref, table_ref, bias_ref, *refs):
    seqs = len_ref.shape[0]
    (tok_hbm, cot_hbm), refs = refs[:2], refs[2:]
    ctx_mine_hbm, ctx_theirs_hbm, refs = refs[:seqs], refs[seqs : 2 * seqs], refs[2 * seqs :]
    weights, refs = refs[:count], refs[count:]
    grads = 4 if layout.split else 6
    sums_two_ref, sums_one_ref, sums_inner_ref = refs[:3]
    (out_hbm, resid_hbm, gc_mine_hbm, gc_theirs_hbm), refs = refs[3:7], refs[7:]
    grad_hbm, refs = refs[:grads], refs[grads:]
    (
        inner_ref,
        mix_ref,
        outer_ref,
        tok_ref,
        mine_ref,
        theirs_ref,
        cot_ref,
        active_ref,
        slope_ref,
        low_ref,
        context_ref,
        stage_outer,
        stage_inner,
        stage_mix,
        stage_ctx,
        hidden_ref,
        normed_ref,
        out_ref,
        resid_ref,
        in_sems,
        out_sems,
    ) = refs
    width, units, cols = layout.width, layout.units, layout.cols
    core = where_ref[0]
    first = core == 0
    extent = units // 4
    loads = []

    def load(source, target):
        copy = pltpu.make_async_copy(source, target, in_sems.at[len(loads)])
        copy.start()
        loads.append(copy)
        return copy

    part = mine_ref.shape[0] // seqs
    small = [load(tok_hbm, tok_ref)]
    for seq in range(seqs):
        some = slice(seq * part, (seq + 1) * part)
        small.append(load(ctx_mine_hbm[seq], mine_ref.at[some, :]))
        small.append(load(ctx_theirs_hbm[seq], theirs_ref.at[some, :]))
    if layout.split:
        together = weights[0]
        rows = layout.rows
        last = layout.fold * rows
        mix_loads = [
            load(
                together.at[:, half, last : last + rows, :],
                mix_ref.at[:, :, half * cols : (half + 1) * cols],
            )
            for half in range(2)
        ]
        inner_loads = [
            [
                load(
                    together.at[:, tile // 2, place * rows : (place + 1) * rows, :],
                    inner_ref.at[
                        :,
                        :,
                        ((tile // 2) * layout.fold + place) * cols : (
                            (tile // 2) * layout.fold + place + 1
                        )
                        * cols,
                    ],
                )
                for place in range(
                    (tile % 2) * layout.fold // 2, (tile % 2 + 1) * layout.fold // 2
                )
            ]
            for tile in range(4)
        ]
        outer_loads = []
        for other in range(2):
            half = core ^ other
            for mask in range(4):
                outer_loads.append(
                    load(
                        weights[1 + 4 * other + mask],
                        outer_ref.at[:, where_ref[2] ^ mask, :, span(half, cols)],
                    )
                )
    else:
        mix_loads = [load(weights[0], mix_ref)]
        inner_loads = [[load(weights[1], inner_ref)], [], [], []]
        outer_loads = [load(weights[2], outer_ref)]
    cot_load = load(cot_hbm, cot_ref)

    def mix_half(half):
        lanes = slice(half * cols, (half + 1) * cols)
        if layout.split:
            return mix_ref[:, :, lanes].reshape(width, cols)
        return mix_ref[:, lanes]

    def inner_tile(tile):
        if layout.split:
            return inner_ref[:, :, span(tile, extent)].reshape(width, extent)
        return inner_ref[:, span(tile, extent)]

    def outer_tile(tile):
        if layout.split:
            return outer_ref[tile].reshape(extent, width)
        return outer_ref[span(tile, extent), :]

    stores = []

    def store(source, target):
        copy = pltpu.make_async_copy(source, target, out_sems.at[len(stores)])
        copy.start()
        stores.append(copy)

    for copy in small:
        copy.wait()
    context = ordered(first, mine_ref[...], theirs_ref[...], 1)
    context_ref[...] = context
    for copy in mix_loads:
        copy.wait()
    attn = jnp.concatenate([product(context, mix_half(half)) for half in range(2)], axis=1)
    normed, inv_one = normalize(
        tok_ref[...].astype(F32) + (attn + table_ref[B_OUT : B_OUT + 1])
    )
    normed_ref[...] = normed
    hidden = normed * table_ref[GAIN_ONE : GAIN_ONE + 1] + table_ref[SHIFT_ONE : SHIFT_ONE + 1]
    hidden_ref[...] = hidden
    low_ref[...] = hidden.astype(BF)
    total = hidden_ref[...] + table_ref[B_OUTER : B_OUTER + 1]
    for tile in range(5):
        if tile < 4:
            for copy in inner_loads[tile]:
                copy.wait()
            lanes = slice(tile * extent, (tile + 1) * extent)
            pre = product(low_ref[...], inner_tile(tile)) + bias_ref[:, lanes]
            cumulative = 0.5 * (1.0 + lax.erf(pre * ROOT_HALF))
            active_ref[:, lanes] = (pre * cumulative).astype(BF)
            slope = cumulative + pre * jnp.exp(-0.5 * pre * pre) * INV_ROOT_TAU
            slope_ref[:, lanes] = slope.astype(BF)
        if tile == 1:
            for copy in outer_loads:
                copy.wait()
        if tile > 0:
            lanes = slice((tile - 1) * extent, tile * extent)
            total += product(active_ref[:, lanes], outer_tile(tile - 1))
    normed, inv = normalize(total)
    gain = table_ref[GAIN_TWO : GAIN_TWO + 1]
    out_ref[...] = normed * gain + table_ref[SHIFT_TWO : SHIFT_TWO + 1]
    store(out_ref, out_hbm)
    half_length = normed.shape[0] // seqs
    position = core * half_length + lax.broadcasted_iota(jnp.int32, (half_length, 1), 0)
    live = jnp.concatenate(
        [jnp.where(position < len_ref[s], 1.0, 0.0) for s in range(seqs)], axis=0
    )
    cot_load.wait()
    grad = cot_ref[...].astype(F32) * live
    resid = normalize_back(grad, normed, inv, gain)
    grad_outer = resid.astype(BF)
    sums_two_ref[...] = column_sums(grad_outer, grad * normed, grad)
    resid_ref[...] = resid

    def halves(values):
        left, right = values[:, :cols], values[:, cols:]
        return jnp.where(first, right, left), jnp.where(first, left, right)

    rows = layout.rows
    def outer_grad(tile):
        lanes = slice(tile * extent, (tile + 1) * extent)
        found = product(active_ref[:, lanes].T, grad_outer).astype(BF)
        for other, columns in zip((1, 0), halves(found)):
            stage_outer[other, lanes, :] = columns
            if layout.split:
                near = extent // layout.block
                for chip in range(near):
                    start = tile * extent + chip * layout.block
                    store(
                        stage_outer.at[other, start : start + layout.block, :],
                        grad_hbm[other].at[tile * near + chip],
                    )
            else:
                store(
                    stage_outer.at[other, lanes, :],
                    grad_hbm[3 * other].at[lanes, :],
                )
    low_t = low_ref[...].T
    total = resid_ref[...]
    for other in (1, 0):
        for part in range(2):
            outer_grad(2 * (1 - other) + part)
            place = 2 * (core ^ other) + part
            grad = product_nt(grad_outer, outer_tile(place))
            grad = (grad * slope_ref[:, span(place, extent)].astype(F32)).astype(BF)
            sums_inner_ref[:, span(place, extent)] = jnp.sum(
                grad.astype(F32), axis=0, keepdims=True
            )
            total += product_nt(grad, inner_tile(place))
            found = product(low_t, grad).astype(BF)
            for i in range(layout.fold // 2):
                index = part * (layout.fold // 2) + i
                stage_inner[other, index] = found[:, i * cols : (i + 1) * cols]
                if layout.split:
                    start = index * rows
                    for chip in range(layout.chips):
                        store(
                            stage_inner.at[other, index, chip * rows : (chip + 1) * rows, :],
                            grad_hbm[2 + other].at[chip, start : start + rows, :],
                        )
                else:
                    store(
                        stage_inner.at[other, index],
                        grad_hbm[3 * other + 1].at[:, index * cols : (index + 1) * cols],
                    )
    normed = normed_ref[...]
    resid = normalize_back(total, normed, inv_one, table_ref[GAIN_ONE : GAIN_ONE + 1])
    resid_ref[...] = resid
    store(resid_ref, resid_hbm)
    attn = resid.astype(BF)
    sums_one_ref[...] = column_sums(attn, total * normed, total)
    back = product_nt(attn[:, :cols], mix_half(0)) + product_nt(attn[:, cols:], mix_half(1))
    for other, columns, target in zip(
        (1, 0), halves(back.astype(BF)), (gc_theirs_hbm, gc_mine_hbm)
    ):
        stage_ctx[other] = columns
        store(stage_ctx.at[other], target)
    context_t = context_ref[...].T
    for other, columns in zip((1, 0), halves(attn)):
        stage_mix[other] = product(context_t, columns).astype(BF)
        if layout.split:
            start = layout.fold * rows
            for chip in range(layout.chips):
                store(
                    stage_mix.at[other, chip * rows : (chip + 1) * rows, :],
                    grad_hbm[2 + other].at[chip, start : start + rows, :],
                )
        else:
            store(stage_mix.at[other], grad_hbm[3 * other + 2])
    for copy in stores:
        copy.wait()


def ffn(layout, where, lengths, table, bias, tokens, cotangent, mine, theirs, weights):
    rows, width = tokens.shape
    units, cols = layout.units, layout.cols
    full, part = (rows, width), (rows, cols)
    if layout.split:
        grads = [(layout.chips, layout.block, cols)] * 2
        grads += [(layout.chips, layout.packed, cols)] * 2
        loads = 1 + 2 * len(mine) + 2 + 2 * layout.fold + 8 + 1
        stores = 4 + 2 * layout.chips * (layout.fold + 2)
    else:
        grads = [(units, cols), (width, units // 2), (width, cols)] * 2
        loads = 5 + 2 * len(mine)
        stores = 4 + 2 * (4 + layout.fold + 1)
    anywhere = pl.BlockSpec(memory_space=pl.ANY)
    arrays = (tokens, cotangent, *mine, *theirs, *weights)
    outs = [((8, width), F32), ((8, width), F32), ((1, units), F32), (full, F32), (full, F32)]
    outs += [(part, BF)] * 2 + [(one, BF) for one in grads]
    return pl.pallas_call(
        functools.partial(ffn_kernel, layout, len(weights)),
        out_shape=tuple(jax.ShapeDtypeStruct(shape, kind) for shape, kind in outs),
        grid_spec=pltpu.PrefetchScalarGridSpec(
            num_scalar_prefetch=2,
            grid=(1,),
            in_specs=on_chip(2) + [anywhere] * len(arrays),
            out_specs=tuple(on_chip(3) + [anywhere] * (len(outs) - 3)),
            scratch_shapes=layout.scratch(rows)
            + [pltpu.SemaphoreType.DMA((loads,)), pltpu.SemaphoreType.DMA((stores,))],
        ),
        compiler_params=pltpu.CompilerParams(vmem_limit_bytes=58 << 20),
        cost_estimate=SMALL,
        name="ffn",
    )(where, lengths, table, bias, *arrays)


def token_kernel(count, where_ref, *refs):
    grad_refs = refs[:count]
    weight_ref, resid_ref, keep_ref, away_ref = refs[count:]
    half = resid_ref.shape[0]
    extent = grad_refs[0].shape[1]
    mine = where_ref[0] * half
    for start, target in ((half - mine, away_ref), (mine, keep_ref)):
        rows = pl.ds(pl.multiple_of(start, half), half)
        part = product_nt(grad_refs[0][rows, :], weight_ref[:, :extent])
        for i in range(1, count):
            part += product_nt(
                grad_refs[i][rows, :], weight_ref[:, i * extent : (i + 1) * extent]
            )
        if target is keep_ref:
            part += resid_ref[...]
        target[...] = part.astype(target.dtype)


def token_grads(where, grads, weight, resid, seqs):
    rows, cols = grads[0].shape
    width = resid.shape[1]
    length = rows // seqs

    def rowwise(extent, columns):
        return pl.BlockSpec((extent, columns), lambda i, *_: (i, 0))

    return pl.pallas_call(
        functools.partial(token_kernel, len(grads)),
        out_shape=(
            jax.ShapeDtypeStruct((rows // 2, width), F32),
            jax.ShapeDtypeStruct((rows // 2, width), BF),
        ),
        grid_spec=pltpu.PrefetchScalarGridSpec(
            num_scalar_prefetch=1,
            grid=(seqs,),
            in_specs=[rowwise(length, cols)] * len(grads)
            + [pl.BlockSpec(weight.shape, lambda *_: (0, 0)), rowwise(length // 2, width)],
            out_specs=(rowwise(length // 2, width), rowwise(length // 2, width)),
        ),
        compiler_params=pltpu.CompilerParams(vmem_limit_bytes=44 << 20),
        cost_estimate=SMALL,
        name="token_grads",
    )(where, *grads, weight, resid)


def combine_kernel(plan, count, where_ref, *refs):
    arrays, refs = refs[:count], refs[count:]
    outs, refs = refs[: len(plan)], refs[len(plan) :]
    buffers, sems = refs[:-1], refs[-1]

    def place(entry):
        if entry is None:
            return slice(None)
        if entry[0] == "side":
            return ((where_ref[1] >> entry[1]) & 1) ^ entry[2]
        if entry[0] == "far":
            return (where_ref[1] >> 2) ^ entry[1]
        return pl.ds(*entry)

    copies = []
    for _, parts in plan:
        for terms, _ in parts:
            for number, index in terms:
                source = arrays[number].at[tuple(place(entry) for entry in index)]
                at = len(copies)
                copies.append(pltpu.make_async_copy(source, buffers[at], sems.at[at]))
                copies[-1].start()
    at = 0
    for (kind, parts), out in zip(plan, outs):
        for terms, window in parts:
            total = None
            for _ in terms:
                copies[at].wait()
                one = buffers[at][...].astype(F32)
                total = one if total is None else total + one
                at += 1
            if window is None:
                out[...] = total.astype(kind)
            else:
                out[window] = total.astype(kind)


def combine(where, jobs, room=None):
    arrays, plan, buffers = [], [], []

    def number(array):
        for i, one in enumerate(arrays):
            if one is array:
                return i
        arrays.append(array)
        return len(arrays) - 1

    for kind, _, parts in jobs:
        planned = []
        for terms, window in parts:
            numbered = []
            for array, index in terms:
                shape = []
                for extent, entry in zip(array.shape, index):
                    if entry is None:
                        shape.append(extent)
                    elif entry[0] not in ("side", "far"):
                        shape.append(entry[1])
                buffers.append(pltpu.VMEM(tuple(shape), array.dtype))
                numbered.append((number(array), tuple(index)))
            planned.append((numbered, window))
        plan.append((kind, planned))
    return pl.pallas_call(
        functools.partial(combine_kernel, plan, len(arrays)),
        out_shape=tuple(jax.ShapeDtypeStruct(shape, kind) for kind, shape, _ in jobs),
        grid_spec=pltpu.PrefetchScalarGridSpec(
            num_scalar_prefetch=1,
            grid=(1,),
            in_specs=[pl.BlockSpec(memory_space=pl.ANY)] * len(arrays),
            out_specs=tuple(on_chip(len(jobs))),
            scratch_shapes=buffers + [pltpu.SemaphoreType.DMA((len(buffers),))],
        ),
        compiler_params=pltpu.CompilerParams(vmem_limit_bytes=room or VMEM_LIMIT),
        cost_estimate=SMALL,
        name="combine",
    )(where, *arrays)


class Sum:
    def __init__(self, terms, flying=()):
        self.terms, self.flying = list(terms), list(flying)


jax.tree_util.register_pytree_node(
    Sum,
    lambda held: (
        ([array for array, _, _ in held.terms], [array for array, _ in held.flying]),
        (
            tuple((bits, window) for _, bits, window in held.terms),
            tuple(mask for _, mask in held.flying),
        ),
    ),
    lambda fixed, arrays: Sum(
        [(array, *about) for array, about in zip(arrays[0], fixed[0])], zip(arrays[1], fixed[1])
    ),
)


def tie(values):
    return lax.optimization_barrier(values)


def after(values, *others):
    return tie((values, others))[0]


def masks(digit):
    found = [0]
    for bit in digit:
        found += [one | (1 << bit) for one in found]
    return found[1:]


class Wires:
    def __init__(self):
        self.chips = lax.axis_size(CHIPS)
        self.bits = self.chips.bit_length() - 1
        self.chip = lax.axis_index(CHIPS)
        self.core = lax.axis_index("seq")
        self.first = self.core == 0
        self.room = None
        far = list(range(self.bits - 1, 1, -1))
        self.far = [tuple(far[i : i + 2]) for i in range(0, len(far), 2)]

    def side(self, bit):
        return (self.chip >> bit) & 1

    def meet(self, values, mask):
        return lax.ppermute(values, CHIPS, [(i, i ^ mask) for i in range(self.chips)])

    def swap_core(self, values):
        return lax.ppermute(values, "seq", [(0, 1), (1, 0)])

    def pick(self, low, high):
        return jnp.where(self.first, low, high), jnp.where(self.first, high, low)

    def columns(self, values):
        cols = values.shape[1] // 2
        return self.pick(values[:, :cols], values[:, cols:])

    def beside(self, mine, theirs, side, axis):
        shape = [1] * (mine.ndim + 1)
        shape[axis] = 2
        here = lax.broadcasted_iota(jnp.int32, tuple(shape), axis) == side
        return jnp.where(here, jnp.expand_dims(mine, axis), jnp.expand_dims(theirs, axis))


    def far_meet(self, values, digit):
        return {0: values} | {mask: self.meet(values, mask) for mask in masks(digit)}

    def far_join(self, found, digit):
        shape = found[0].shape
        for bit in reversed(digit):
            known = {mask for mask in found if not mask & (1 << bit)}
            found = {
                mask: self.beside(found[mask], found[mask | (1 << bit)], self.side(bit), 1)
                for mask in sorted(known)
            }
        return found[0].reshape((-1,) + shape[1:])

    def gather_far(self, values, digit):
        return self.far_join(self.far_meet(values, digit), digit)

    def gather_near(self, values, bit):
        return self.beside(values, self.meet(values, 1 << bit), self.side(bit), 1)

    def pieces(self, values, bit):
        width = values.shape[-1]
        rows = values.shape[-2] << bit
        values = values.reshape(-1, rows, width)
        return values, self.meet(values, 1 << bit)

    def gather_plane(self, values):
        return [values] + [self.meet(values, mask) for mask in masks((0, 1))]

    def plane(self, pieces):
        own = self.chip & 3
        stacked = jnp.stack(pieces, axis=1)
        parts = [
            lax.dynamic_index_in_dim(stacked, own ^ place, 1, keepdims=False) for place in range(4)
        ]
        return jnp.concatenate(parts, axis=1)

    def whole(self, pieces, bit):
        width = pieces[0].shape[-1]
        return self.beside(pieces[0], pieces[1], self.side(bit), 1).reshape(-1, width)


    def spread(self, terms, tail, windows):
        bits = tuple(range(self.bits - 1, -1, -1))
        arrays = [one.reshape([2] * self.bits + list(tail)) for one in terms]
        return [Sum([(one, bits, window) for one in arrays]) for window in windows]

    def part(self, held, fixed):
        total = None
        for array, bits, window in held.terms:
            tail = array.shape[len(bits) :]
            first, size = window if window else ((0,) * len(tail), tail)
            starts = [fixed.get(bit, 0) for bit in bits] + list(first)
            sizes = [1 if bit in fixed else 2 for bit in bits] + list(size)
            shape = [2 for bit in bits if bit not in fixed] + list(size)[-2:]
            one = lax.dynamic_slice(array, starts, sizes).reshape(shape).astype(F32)
            total = one if total is None else total + one
        return total

    def left(self, held):
        return held.terms[-1][1]

    def settled(self, held):
        return {bit: self.side(bit) for bit in range(self.bits) if bit not in self.left(held)}

    def ready(self, held, digit):
        fixed = self.settled(held)
        sent = []
        for mask in masks(digit):
            away = {bit: self.side(bit) ^ ((mask >> bit) & 1) for bit in digit}
            sent.append((self.part(held, {**fixed, **away}).astype(BF), mask))
        return Sum(held.terms, sent)

    def go(self, held):
        return Sum(held.terms, [(self.meet(one, mask), mask) for one, mask in held.flying])

    def land(self, held, digit):
        bits = tuple(bit for bit in self.left(held) if bit not in digit)
        return Sum(held.terms + [(one, bits, None) for one, _ in held.flying])

    def total(self, held):
        return self.part(held, self.settled(held))


    def slices(self, held, stream, step, far=None):
        first, second = stream, 1 - stream
        near = {first: ("side", first, 1 - min(step, 1)), second: None}
        if step > 0:
            near[second] = ("side", second, 2 - step)
        found = []
        for array, bits, window in held.terms:
            tail = array.shape[len(bits) :]
            shape = (4,) + (2,) * (len(bits) - 2) + tail
            index = [far] + [near[bit] for bit in bits[2:]]
            if window is None:
                index += [None] * len(tail)
            else:
                index += list(zip(*window))
            found.append((array.reshape(shape), index))
        return found

    def extent(self, held):
        array, bits, window = held.terms[0]
        return tuple(window[1]) if window else array.shape[len(bits) :]

    def near_ready(self, pair, step):
        if not self.kernels:
            return [self.ready(held, (stream ^ step,)) for stream, held in enumerate(pair)]
        jobs = []
        for stream, held in enumerate(pair):
            shape = (4,) + (2,) * (1 - step) + self.extent(held)
            jobs.append((BF, shape, [(self.slices(held, stream, step), None)]))
        sent = combine(self.where, jobs, self.room)
        return [
            Sum(
                held.terms,
                [(one.reshape((2,) * (3 - step) + self.extent(held)), 1 << (stream ^ step))],
            )
            for stream, (held, one) in enumerate(zip(pair, sent))
        ]

    def far_parts(self, pair, axis, far):
        parts, begin, extents = [], 0, []
        for stream, held in enumerate(pair):
            extent = self.extent(held)
            window = [slice(None)] * (2 + (far is None))
            window[axis] = slice(begin, begin + extent[axis])
            begin += extent[axis]
            extents.append(extent)
            parts.append((self.slices(held, stream, 2, far), tuple(window)))
        shape = list(extents[0])
        shape[axis] = begin
        return tuple(shape), parts

    def far_ready(self, pair, axis):
        if not self.kernels:
            held = self.far_steps(self.joined(pair, axis))
            held = self.ready(held, self.far[-1])
            own = {bit: self.side(bit) for bit in range(self.bits)}
            return self.part(held, own), [one for one, _ in held.flying]
        jobs = []
        for mask in [0] + masks(self.far[-1]):
            shape, parts = self.far_parts(pair, axis, ("far", mask >> 2))
            jobs.append((BF if mask else F32, shape, parts))
        kept, *sent = combine(self.where, jobs, self.room)
        return kept, sent

    def far_go(self, held):
        kept, sent = held
        return kept, [self.meet(one, mask) for one, mask in zip(sent, masks(self.far[-1]))]

    def far_total(self, held):
        kept, arrived = held
        for one in arrived:
            kept = kept + one.astype(F32)
        return kept

    def far_rows(self, pair, axis):
        if self.kernels:
            shape, parts = self.far_parts(pair, axis, None)
            array = combine(self.where, [(BF, (4,) + shape, parts)], self.room)[0]
        else:
            array = self.joined(pair, axis).terms[0][0]
        return lax.psum_scatter(
            array.reshape(-1, array.shape[-1]), "far", scatter_dimension=0, tiled=True
        )

    def near_go(self, pair):
        return [self.go(held) for held in pair]

    def near_land(self, pair, step):
        return [self.land(held, (stream ^ step,)) for stream, held in enumerate(pair)]

    def joined(self, pair, axis):
        sums = [self.total(held).astype(BF) for held in pair]
        return Sum([(jnp.concatenate(sums, axis=axis), self.left(pair[0]), None)])

    def far_steps(self, held):
        for digit in self.far[:-1]:
            held = self.land(self.go(self.ready(held, digit)), digit)
        return held

    def owned(self, block):
        rows = block.shape[0] // 2
        return self.pick(block[:rows], block[rows:])


def body(tokens, lengths, cotangent, *shards):
    (
        w_query,
        b_query,
        w_key,
        w_value,
        b_value,
        w_out,
        b_out,
        gain_one,
        shift_one,
        w_inner,
        b_inner,
        w_outer,
        b_outer,
        gain_two,
        shift_two,
    ) = shards
    wires = Wires()
    core = wires.core
    devices = 2 * wires.chips
    seqs, half, width = tokens.shape
    rows = seqs * half
    cols = width // 2
    slot = b_query.shape[0]
    fold = b_inner.shape[0] // slot
    plane = wires.chip & 3
    where = jnp.stack([core, wires.chip, plane, wires.side(0), wires.side(1)]).astype(jnp.int32)

    vectors = jnp.stack(
        [b_query, b_value, b_out, gain_one, shift_one, b_outer, gain_two, shift_two]
    )
    vectors = jnp.concatenate([vectors, b_inner.reshape(fold, slot)], axis=0)
    vectors = jnp.pad(vectors.T, ((0, 0), (0, LANES - vectors.shape[0])))
    mine, away = zip(*[wires.columns(one) for one in (w_query, w_key, w_value, w_out, w_inner)])
    pairs = cols // PAIR

    def by_pair(parts):
        spans = [slice(p * PAIR, (p + 1) * PAIR) for p in range(pairs)]
        return jnp.concatenate([one[:, span] for span in spans for one in parts] + [vectors], axis=1)

    def both_rows(kept, sent):
        return ordered(wires.first, kept, wires.swap_core(sent), 0)

    units = w_inner.shape[1]
    paired = 2 * slot
    layout = Layout(wires.chips, width, units)
    aligned = wires.kernels = layout.split
    wires.where = where
    first = both_rows(by_pair(mine[:3]), by_pair(away[:3]))[None]
    outer_mine, outer_away = wires.columns(w_outer)
    outer_held = both_rows(outer_mine, outer_away)[None]
    if aligned:
        parts = [jnp.concatenate([inner, out], axis=1) for out, inner in (mine[3:], away[3:])]
        second = both_rows(*parts)
        second = jnp.concatenate(
            [second[:, i : i + cols] for i in range(0, second.shape[1], cols)], axis=0
        )
        second = lax.all_gather(second, CHIPS + ("seq",), axis=0, tiled=True)
        weights = [second.reshape(wires.chips, 2, -1, cols)]
    else:
        weights = [
            lax.all_gather(one, CHIPS + ("seq",), axis=0, tiled=True)
            for one in (w_out, w_inner, w_outer)
        ]
    for digit in wires.far:
        first = wires.gather_far(first, digit)
    first, outer_held = tie((first, outer_held))
    for digit in wires.far[:-1]:
        outer_held = wires.gather_far(outer_held, digit)
    outer_held = wires.far_meet(outer_held, wires.far[-1])
    cut = (3 * pairs + 1) // 2 * LANES
    one = wires.gather_near(first[..., :cut], 1)
    two = wires.gather_near(first[..., cut:], 0)
    pieces_one, pieces_two = wires.pieces(one, 0), wires.pieces(two, 1)
    if not aligned:
        pieces_one, pieces_two = [
            (wires.whole(pieces, bit)[None],)
            for bit, pieces in enumerate((pieces_one, pieces_two))
        ]
    tok_rows = tokens.reshape(rows, width)
    tok_other = wires.swap_core(tokens)
    tok_all = ordered(wires.first, tokens, tok_other, 1).reshape(2 * rows, width)

    held = attend(0, where, lengths, tokens, tok_other, (pieces_one, pieces_two))
    w_qkv, table = held[4:]
    heads = [held[:4]]
    if aligned:
        w_qkv, table, outer_held = tie((w_qkv, table, outer_held))
        outer_held = wires.gather_plane(wires.far_join(outer_held, wires.far[-1]))
    for seq in range(1, seqs):
        heads.append(attend(seq, where, lengths, tokens, tok_other, (w_qkv, table)))
    qkv, ctx_mine, ctx_away, lse = zip(*heads)
    ctx_theirs = [wires.swap_core(one) for one in ctx_away]
    if aligned:
        ctx_theirs, outer_held = tie((ctx_theirs, outer_held))
        weights += outer_held + [wires.swap_core(one) for one in outer_held]
    kept = 8 + fold
    bias_inner = table[8:kept].reshape(fold, devices, slot).transpose(1, 0, 2).reshape(1, -1)
    results = ffn(
        layout,
        where,
        lengths,
        table,
        bias_inner,
        tok_rows,
        cotangent.reshape(rows, width),
        ctx_mine,
        ctx_theirs,
        weights,
    )
    sums_two, sums_one, sums_inner, output, resid_one, gc_mine, gc_away = results[:7]
    grad_parts = results[7:]
    if not aligned:

        def by_chip(many):
            g_outer, g_inner, g_out = many
            g_inner = g_inner.reshape(wires.chips, -1, fold, cols).transpose(0, 2, 1, 3)
            others = (g_inner.reshape(wires.chips, -1, cols), g_out.reshape(wires.chips, -1, cols))
            return g_outer.reshape(wires.chips, -1, cols), jnp.concatenate(others, axis=1)

        mine, away = by_chip(grad_parts[:3]), by_chip(grad_parts[3:])
        grad_parts = (mine[0], away[0], mine[1], away[1])
    g_outer, g_outer_away, g_rest, g_rest_away = grad_parts

    last = wires.far[-1]
    rows_chip = 2 * slot
    gc_theirs = wires.swap_core(gc_away)
    base = jnp.concatenate(
        [
            jnp.zeros((2, width), F32),
            sums_one[:3],
            sums_two[:3],
            sums_inner.reshape(devices, fold, slot).transpose(1, 0, 2).reshape(fold, width),
            jnp.zeros((TABLE - kept, width), F32),
        ],
        axis=0,
    )

    def two_windows(held, theirs):
        extent = held.shape[1]
        cut = extent // 2 // 16 * 16 if aligned else extent // 2
        return wires.spread(
            [held, theirs],
            (extent, cols),
            [((0, 0), (cut, cols)), ((cut, 0), (extent - cut, cols))],
        )

    def attention_grad(pair, held, widths):
        return attend_back(
            pair, where, lengths, qkv, lse, gc_mine, gc_theirs, tok_all, held, widths
        )

    pair_width = 3 * PAIR
    more = (3 * pairs + 1) // 2 * LANES - pair_width
    arrived = wires.swap_core(g_outer_away)
    g_rest_away = after(g_rest_away, arrived)
    outer = wires.near_ready(two_windows(g_outer, arrived), 0)
    gc_mine, outer = tie((gc_mine, outer))
    outer = wires.near_go(outer)
    grad_one, sums_first, g_first = attention_grad(0, (), (pair_width,))
    arrived = wires.swap_core(g_rest_away)
    grad_one, arrived, base = tie((grad_one, arrived, base))
    rest = wires.near_ready(two_windows(g_rest, arrived), 0)
    gc_mine, rest = tie((gc_mine, rest))
    rest = wires.near_go(rest)
    grad_two, sums_second, g_one, g_kept = attention_grad(
        1, (g_first,), (pair_width + more, pair_width - more)
    )
    grad_two, outer = tie((grad_two, outer))
    outer = wires.near_ready(wires.near_land(outer, 0), 1)
    gc_mine, outer = tie((gc_mine, outer))
    outer = wires.near_go(outer)
    grad_three, _, g_two = attention_grad(
        2,
        (g_kept, base, sums_first, sums_second),
        (2 * pair_width - more + LANES,),
    )
    grads = [grad_one, grad_two, grad_three]
    grads, rest = tie((grads, rest))
    rest = wires.near_ready(wires.near_land(rest, 0), 1)
    g_one, g_two, rest = tie((g_one, g_two, rest))
    rest = wires.near_go(rest)
    both = [wires.spread([one], (rows_chip, one.shape[1]), [None])[0] for one in (g_one, g_two)]
    both = wires.near_ready(both, 0)
    grads, both = tie((grads, both))
    both = wires.near_go(both)
    tok_keep, tok_away = token_grads(where, grads, w_qkv, resid_one, seqs)
    tok_away, tok_keep, outer = tie((tok_away, tok_keep, outer))
    g_outer = wires.far_rows(wires.near_land(outer, 1), -2)
    tok_away, rest, both = tie((tok_away, rest, both))
    wires.room = 60 << 20
    tok_theirs = wires.swap_core(tok_away)
    both = wires.near_ready(wires.near_land(both, 0), 1)
    rest = after(rest, both)
    g_rest = wires.far_rows(wires.near_land(rest, 1), -2)
    tok_keep, both = tie((tok_keep, both))
    both = wires.near_go(both)
    both, tok_theirs = tie((both, tok_theirs))
    both = wires.far_ready(wires.near_land(both, 1), -1)
    both, tok_theirs, tok_keep = tie((both, tok_theirs, tok_keep))
    both = wires.far_go(both)
    grad_tok = tok_keep + tok_theirs.astype(F32)
    g_rest = after(g_rest, both[1]).astype(F32)
    g_both = wires.far_total(both)

    columns = [g_both] + [
        g_rest[i * rows_chip : (i + 1) * rows_chip] for i in range(fold + 1)
    ]
    mine, away = wires.owned(jnp.concatenate(columns, axis=1))
    theirs = wires.swap_core(away)
    mine_outer, away = wires.owned(g_outer.astype(F32))
    g_outer = ordered(wires.first, mine_outer, wires.swap_core(away), 1)
    begin = g_both.shape[1]

    def full(spans):
        return jnp.concatenate(
            [one[:, span] for one in wires.pick(mine, theirs) for span in spans], axis=1
        )

    pieces = [
        full([slice((3 * p + i) * PAIR, (3 * p + i + 1) * PAIR) for p in range(pairs)])
        for i in range(3)
    ]
    pieces.append(full([slice(begin + fold * cols, begin + (fold + 1) * cols)]))
    pieces.append(full([slice(begin, begin + fold * cols)]))
    vectors = slice(begin - LANES, begin)
    small = (mine[:, vectors] + theirs[:, vectors]).T

    return (
        output.reshape(seqs, half, width),
        grad_tok.reshape(seqs, half, width),
        pieces[0],
        small[0],
        pieces[1],
        pieces[2],
        small[1],
        pieces[3],
        small[2],
        small[3],
        small[4],
        pieces[4],
        small[8:kept].reshape(-1),
        g_outer,
        small[5],
        small[6],
        small[7],
    )


def solution(mesh):
    cores = mesh.shape["seq"]
    split = Mesh(mesh.devices.reshape(-1, 2, 2, cores), CHIPS + ("seq",))
    every = CHIPS + ("seq",)
    matrix, vector = P(every, None), P(every)
    rows = P(CHIPS, "seq", None)
    weights = (matrix, vector, matrix, matrix, vector, matrix, vector, vector, vector)
    weights += (matrix, vector, matrix, vector, vector, vector)
    return jax.shard_map(
        body,
        mesh=split,
        in_specs=(rows, P(CHIPS), rows) + weights,
        out_specs=(rows, rows) + weights,
        check_vma=False,
    )
```

```python
import functools

import jax
import jax.numpy as jnp
from jax import lax
from jax.experimental import pallas as pl
from jax.experimental.pallas import tpu as pltpu
from jax.sharding import Mesh
from jax.sharding import PartitionSpec as P

HEAD_DIM = 64
PAIR = 2 * HEAD_DIM
LANES = 128
NEG_BIG = -1000000000.0
EPSILON = 1e-05
ROOT_HALF = 0.7071067811865476
INV_ROOT_TAU = 0.3989422804014327
BF = jnp.bfloat16
CHIPS = ("far", "mid", "low")
F32 = jnp.float32
VMEM_LIMIT = 20 << 20
SMALL = pl.CostEstimate(flops=1024, transcendentals=0, bytes_accessed=1024)

B_QUERY, B_VALUE, B_OUT, GAIN_ONE, SHIFT_ONE, B_OUTER, GAIN_TWO, SHIFT_TWO, B_INNER = range(9)
TABLE = 16


def product(left, right):
    return jnp.dot(left, right, preferred_element_type=F32)


def product_tn(left, right):
    return lax.dot_general(left, right, (((0,), (0,)), ((), ())), preferred_element_type=F32)


def product_nt(left, right):
    return lax.dot_general(left, right, (((1,), (1,)), ((), ())), preferred_element_type=F32)


def ordered(first, mine, theirs, axis):
    return jnp.concatenate([jnp.where(first, mine, theirs), jnp.where(first, theirs, mine)], axis)


def row_mean(values):
    return jnp.mean(values, axis=-1, keepdims=True)


def normalize(values):
    center = values - row_mean(values)
    inv_spread = lax.rsqrt(row_mean(center * center) + EPSILON)
    return center * inv_spread, inv_spread


def normalize_back(grad_out, normed, inv_spread, gain):
    grad_normed = grad_out * gain
    centered = grad_normed - row_mean(grad_normed)
    return inv_spread * (centered - normed * row_mean(grad_normed * normed))


def column_sums(*values):
    rows = [jnp.sum(one.astype(F32), axis=0, keepdims=True) for one in values]
    pad = jnp.zeros((8 - len(rows), rows[0].shape[1]), F32)
    return jnp.concatenate(rows + [pad], axis=0)


def attend_kernel(seq, count, where_ref, len_ref, mine_ref, theirs_ref, *refs):
    held = (refs[:count], refs[count : 2 * count])
    refs = refs[2 * count :]
    if count == 0:
        refs = refs[2:] + refs[:2]
    qkv_ref, ctx_mine_ref, ctx_theirs_ref, lse_ref, weight_ref, table_ref = refs
    core = where_ref[0]
    first = core == 0
    seen_to = len_ref[seq]
    width = weight_ref.shape[0]
    cols = width // 2

    if count > 0:
        start = 0
        for stream, pieces in enumerate(held):
            side = where_ref[3 + stream]
            extent = pieces[0].shape[-1]
            fill(weight_ref.at[:, start : start + extent], pieces, (side, 1 - side))
            start += extent
        last = weight_ref.shape[1] - LANES
        chosen = lax.broadcasted_iota(jnp.int32, (TABLE, LANES), 0)
        chosen = chosen == lax.broadcasted_iota(jnp.int32, (TABLE, LANES), 1)
        table_ref[...] = product_nt(
            jnp.where(chosen, 1.0, 0.0).astype(BF), weight_ref[:, last:]
        )

    def own(row):
        return jnp.where(first, table_ref[row : row + 1, :cols], table_ref[row : row + 1, cols:])

    tokens = ordered(first, mine_ref[seq], theirs_ref[seq], 0)
    length = tokens.shape[0]
    bias_q, bias_v = own(B_QUERY), own(B_VALUE)
    seen = lax.broadcasted_iota(jnp.int32, (length, length), 0) < seen_to
    lane = lax.broadcasted_iota(jnp.int32, (length, PAIR), 1)
    for pair in range(cols // PAIR):
        lanes = slice(pair * PAIR, (pair + 1) * PAIR)
        project = product(tokens, weight_ref[:, 3 * pair * PAIR : 3 * (pair + 1) * PAIR])
        queries = (project[:, :PAIR] + bias_q[:, lanes]).astype(BF)
        keys = project[:, PAIR : 2 * PAIR].astype(BF)
        values = (project[:, 2 * PAIR :] + bias_v[:, lanes]).astype(BF)
        qkv_ref[:, 3 * pair * PAIR : 3 * (pair + 1) * PAIR] = jnp.concatenate(
            [queries, keys, values], axis=1
        )
        queries = queries * BF(HEAD_DIM ** (-0.5))
        values_t = values.T
        parts = []
        for head in range(2):
            mask = (lane >= head * HEAD_DIM) & (lane < (head + 1) * HEAD_DIM)
            scores = product_nt(jnp.where(mask, keys, BF(0)), queries)
            scores = jnp.where(seen, scores, NEG_BIG)
            top = jnp.max(scores, axis=0, keepdims=True)
            weights = jnp.exp(scores - top)
            total = jnp.sum(weights, axis=0, keepdims=True)
            mixed = product(
                values_t[head * HEAD_DIM : (head + 1) * HEAD_DIM], weights.astype(BF)
            )
            parts.append(mixed * (1.0 / total))
            row = 2 * pair + head
            lse_ref[row : row + 1, :] = top + jnp.log(total)
        context = jnp.concatenate(parts, axis=0).T.astype(BF)
        low, high = context[: length // 2], context[length // 2 :]
        ctx_mine_ref[:, lanes] = jnp.where(first, low, high)
        ctx_theirs_ref[:, lanes] = jnp.where(first, high, low)


def attend_back_kernel(pair, extras, seqs, where_ref, len_ref, *refs):
    qkv_refs, lse_refs, refs = refs[:seqs], refs[seqs : 2 * seqs], refs[2 * seqs :]
    mine_ref, theirs_ref, tok_ref, *refs = refs
    held, refs = refs[:extras], refs[extras:]
    grad_ref, sums_ref, *weight_refs = refs
    first = where_ref[0] == 0
    scale = BF(HEAD_DIM ** (-0.5))
    length = qkv_refs[0].shape[0]
    start = 3 * pair * PAIR
    lanes = slice(pair * PAIR, (pair + 1) * PAIR)
    lane = lax.broadcasted_iota(jnp.int32, (length, PAIR), 1)
    key_row = lax.broadcasted_iota(jnp.int32, (length, length), 0)
    sums = total = None
    for seq, (qkv_ref, lse_ref) in enumerate(zip(qkv_refs, lse_refs)):
        rows = slice(seq * length, (seq + 1) * length)
        half_rows = slice(seq * length // 2, (seq + 1) * length // 2)
        seen = key_row < len_ref[seq]
        queries = qkv_ref[:, start : start + PAIR] * scale
        keys = qkv_ref[:, start + PAIR : start + 2 * PAIR]
        values = qkv_ref[:, start + 2 * PAIR : start + 3 * PAIR]
        grad = ordered(first, mine_ref[half_rows, lanes], theirs_ref[half_rows, lanes], 0)
        keys_t = (keys * scale).T
        dq, dk, dv = [], [], []
        for head in range(2):
            own = (lane >= head * HEAD_DIM) & (lane < (head + 1) * HEAD_DIM)
            scores = product_nt(jnp.where(own, keys, BF(0)), queries)
            scores = jnp.where(seen, scores, NEG_BIG)
            row = 2 * pair + head
            probs = jnp.exp(scores - lse_ref[row : row + 1, :])
            grad_probs = product_nt(jnp.where(own, values, BF(0)), grad)
            row_term = jnp.sum(probs * grad_probs, axis=0, keepdims=True)
            grad_scores = (probs * (grad_probs - row_term)).astype(BF)
            dv.append(product(probs.astype(BF), grad))
            dk.append(product(grad_scores, queries))
            dq.append(product(keys_t[head * HEAD_DIM : (head + 1) * HEAD_DIM], grad_scores))
        own = lane < HEAD_DIM
        all_three = [
            jnp.concatenate(dq, axis=0).T.astype(BF),
            jnp.where(own, dk[0], dk[1]).astype(BF),
            jnp.where(own, dv[0], dv[1]).astype(BF),
        ]
        grads = jnp.concatenate(all_three, axis=1)
        grad_ref[rows, :] = grads
        one = jnp.sum(grads.astype(F32), axis=0, keepdims=True)
        weight = product(tok_ref[rows, :].T, grads)
        sums = one if sums is None else sums + one
        total = weight if total is None else total + weight
    sums_ref[...] = sums
    found = total.astype(BF)
    extent = found.shape[1]
    if pair == 0:
        weight_refs[0][...] = found
    elif extras == 1:
        more = weight_refs[0].shape[1] - extent
        weight_refs[0][:, :extent] = held[0][...]
        weight_refs[0][:, extent:] = found[:, :more]
        weight_refs[1][...] = found[:, more:]
    else:
        kept = held[0].shape[1]
        weight_refs[0][:, :kept] = held[0][...]
        weight_refs[0][:, kept : kept + extent] = found
        many = [one[...] for one in held[2:]] + [sums]
        blank = jnp.zeros((1, many[0].shape[1] // 3 * len(many)), F32)
        table = held[1][...]
        place = lax.broadcasted_iota(jnp.int32, table.shape, 0)
        for number, begin in ((B_QUERY, 0), (B_VALUE, 2 * PAIR)):
            row = jnp.concatenate([one[:, begin : begin + PAIR] for one in many], axis=1)
            row = jnp.concatenate(
                [jnp.where(first, row, blank), jnp.where(first, blank, row)], axis=1
            )
            table = jnp.where(place == number, row, table)
        chosen = lax.broadcasted_iota(jnp.int32, (TABLE, LANES), 0)
        chosen = chosen == lax.broadcasted_iota(jnp.int32, (TABLE, LANES), 1)
        weight_refs[0][:, kept + extent :] = product_tn(
            table.astype(BF), jnp.where(chosen, 1.0, 0.0).astype(BF)
        ).astype(BF)


def attend(seq, where, lengths, mine, theirs, held):
    half, width = mine.shape[1:]
    length = 2 * half
    cols = width // 2
    outs = [
        ((length, 3 * cols), BF),
        ((half, cols), BF),
        ((half, cols), BF),
        ((cols // HEAD_DIM, length), F32),
    ]
    count = 0
    if seq == 0:
        count = len(held[0])
        total = sum(pieces[0].shape[-1] for pieces in held)
        outs += [((width, total), BF), ((TABLE, width), F32)]
        held = [one for pieces in held for one in pieces]
    return run(
        functools.partial(attend_kernel, seq, count),
        "attend",
        (where, lengths),
        (mine, theirs, *held),
        outs,
    )


def attend_back(pair, where, lengths, qkv, lse, mine, theirs, tokens, held, widths):
    rows, width = tokens.shape
    return run(
        functools.partial(attend_back_kernel, pair, len(held), len(qkv)),
        "attend_back",
        (where, lengths),
        (*qkv, *lse, mine, theirs, tokens, *held),
        (((rows, 3 * PAIR), BF), ((1, 3 * PAIR), F32))
        + tuple(((width, one), BF) for one in widths),
    )


def on_chip(count):
    return [pl.BlockSpec(memory_space=pltpu.VMEM)] * count


def run(kernel, name, scalars, arrays, outs, grid=(1,), scratch=()):
    return pl.pallas_call(
        kernel,
        out_shape=tuple(jax.ShapeDtypeStruct(shape, kind) for shape, kind in outs),
        grid_spec=pltpu.PrefetchScalarGridSpec(
            num_scalar_prefetch=len(scalars),
            grid=grid,
            in_specs=on_chip(len(arrays)),
            out_specs=tuple(on_chip(len(outs))),
            scratch_shapes=scratch,
        ),
        compiler_params=pltpu.CompilerParams(vmem_limit_bytes=VMEM_LIMIT),
        cost_estimate=SMALL,
        name=name,
    )(*scalars, *arrays)


def span(step, extent):
    if isinstance(step, int):
        return pl.ds(step * extent, extent)
    return pl.ds(pl.multiple_of(step * extent, extent), extent)


def fill(target, pieces, sides):
    for piece, side in zip(pieces, sides):
        blocks, rows, _ = piece.shape
        for block in range(blocks):
            start = block * len(pieces) * rows
            if len(pieces) > 1:
                start = pl.multiple_of(start + side * rows, rows)
            target[pl.ds(start, rows), :] = piece[block]


class Layout:
    def __init__(self, chips, width, units):
        self.chips, self.width, self.units = chips, width, units
        self.cols = width // 2
        self.rows = width // chips
        self.block = units // chips
        self.fold = units // width
        self.split = self.rows % 16 == 0 and chips == 16
        self.packed = (self.fold + 1) * self.rows

    def scratch(self, rows):
        width, units, cols = self.width, self.units, self.cols
        if self.split:
            weights = [(self.chips, self.rows, units), (self.chips, self.rows, width)]
            weights += [(4, 4, self.block, width)]
        else:
            weights = [(width, units), (width, width), (units, width)]
        full, wide = (rows, width), (rows, units)
        low = weights + [full, (rows, cols), (rows, cols), full, wide, wide, full, full]
        low += [(2, units, cols), (2, self.fold, width, cols), (2, width, cols), (2, rows, cols)]
        high = [full, full, full, full]
        return [pltpu.VMEM(one, BF) for one in low] + [pltpu.VMEM(one, F32) for one in high]


def ffn_kernel(layout, count, where_ref, len_ref, table_ref, bias_ref, *refs):
    seqs = len_ref.shape[0]
    (tok_hbm, cot_hbm), refs = refs[:2], refs[2:]
    ctx_mine_hbm, ctx_theirs_hbm, refs = refs[:seqs], refs[seqs : 2 * seqs], refs[2 * seqs :]
    weights, refs = refs[:count], refs[count:]
    grads = 4 if layout.split else 6
    sums_two_ref, sums_one_ref, sums_inner_ref = refs[:3]
    (out_hbm, resid_hbm, gc_mine_hbm, gc_theirs_hbm), refs = refs[3:7], refs[7:]
    grad_hbm, refs = refs[:grads], refs[grads:]
    (
        inner_ref,
        mix_ref,
        outer_ref,
        tok_ref,
        mine_ref,
        theirs_ref,
        cot_ref,
        active_ref,
        slope_ref,
        low_ref,
        context_ref,
        stage_outer,
        stage_inner,
        stage_mix,
        stage_ctx,
        hidden_ref,
        normed_ref,
        out_ref,
        resid_ref,
        in_sems,
        out_sems,
    ) = refs
    width, units, cols = layout.width, layout.units, layout.cols
    core = where_ref[0]
    first = core == 0
    extent = units // 4
    loads = []

    def load(source, target):
        copy = pltpu.make_async_copy(source, target, in_sems.at[len(loads)])
        copy.start()
        loads.append(copy)
        return copy

    part = mine_ref.shape[0] // seqs
    small = [load(tok_hbm, tok_ref)]
    for seq in range(seqs):
        some = slice(seq * part, (seq + 1) * part)
        small.append(load(ctx_mine_hbm[seq], mine_ref.at[some, :]))
        small.append(load(ctx_theirs_hbm[seq], theirs_ref.at[some, :]))
    if layout.split:
        together = weights[0]
        rows = layout.rows
        last = layout.fold * rows
        mix_loads = [
            load(
                together.at[:, half, last : last + rows, :],
                mix_ref.at[:, :, half * cols : (half + 1) * cols],
            )
            for half in range(2)
        ]
        inner_loads = [
            [
                load(
                    together.at[:, tile // 2, place * rows : (place + 1) * rows, :],
                    inner_ref.at[
                        :,
                        :,
                        ((tile // 2) * layout.fold + place) * cols : (
                            (tile // 2) * layout.fold + place + 1
                        )
                        * cols,
                    ],
                )
                for place in range(
                    (tile % 2) * layout.fold // 2, (tile % 2 + 1) * layout.fold // 2
                )
            ]
            for tile in range(4)
        ]
        outer_loads = []
        for other in range(2):
            half = core ^ other
            for mask in range(4):
                outer_loads.append(
                    load(
                        weights[1 + 4 * other + mask],
                        outer_ref.at[:, where_ref[2] ^ mask, :, span(half, cols)],
                    )
                )
    else:
        mix_loads = [load(weights[0], mix_ref)]
        inner_loads = [[load(weights[1], inner_ref)], [], [], []]
        outer_loads = [load(weights[2], outer_ref)]
    cot_load = load(cot_hbm, cot_ref)

    def mix_half(half):
        lanes = slice(half * cols, (half + 1) * cols)
        if layout.split:
            return mix_ref[:, :, lanes].reshape(width, cols)
        return mix_ref[:, lanes]

    def inner_tile(tile):
        if layout.split:
            return inner_ref[:, :, span(tile, extent)].reshape(width, extent)
        return inner_ref[:, span(tile, extent)]

    def outer_tile(tile):
        if layout.split:
            return outer_ref[tile].reshape(extent, width)
        return outer_ref[span(tile, extent), :]

    stores = []

    def store(source, target):
        copy = pltpu.make_async_copy(source, target, out_sems.at[len(stores)])
        copy.start()
        stores.append(copy)

    for copy in small:
        copy.wait()
    context = ordered(first, mine_ref[...], theirs_ref[...], 1)
    context_ref[...] = context
    for copy in mix_loads:
        copy.wait()
    attn = jnp.concatenate([product(context, mix_half(half)) for half in range(2)], axis=1)
    normed, inv_one = normalize(
        tok_ref[...].astype(F32) + (attn + table_ref[B_OUT : B_OUT + 1])
    )
    normed_ref[...] = normed
    hidden = normed * table_ref[GAIN_ONE : GAIN_ONE + 1] + table_ref[SHIFT_ONE : SHIFT_ONE + 1]
    hidden_ref[...] = hidden
    low_ref[...] = hidden.astype(BF)
    total = hidden_ref[...] + table_ref[B_OUTER : B_OUTER + 1]
    for tile in range(5):
        if tile < 4:
            for copy in inner_loads[tile]:
                copy.wait()
            lanes = slice(tile * extent, (tile + 1) * extent)
            pre = product(low_ref[...], inner_tile(tile)) + bias_ref[:, lanes]
            cumulative = 0.5 * (1.0 + lax.erf(pre * ROOT_HALF))
            active_ref[:, lanes] = (pre * cumulative).astype(BF)
            slope = cumulative + pre * jnp.exp(-0.5 * pre * pre) * INV_ROOT_TAU
            slope_ref[:, lanes] = slope.astype(BF)
        if tile == 1:
            for copy in outer_loads:
                copy.wait()
        if tile > 0:
            lanes = slice((tile - 1) * extent, tile * extent)
            total += product(active_ref[:, lanes], outer_tile(tile - 1))
    normed, inv = normalize(total)
    gain = table_ref[GAIN_TWO : GAIN_TWO + 1]
    out_ref[...] = normed * gain + table_ref[SHIFT_TWO : SHIFT_TWO + 1]
    store(out_ref, out_hbm)
    half_length = normed.shape[0] // seqs
    position = core * half_length + lax.broadcasted_iota(jnp.int32, (half_length, 1), 0)
    live = jnp.concatenate(
        [jnp.where(position < len_ref[s], 1.0, 0.0) for s in range(seqs)], axis=0
    )
    cot_load.wait()
    grad = cot_ref[...].astype(F32) * live
    resid = normalize_back(grad, normed, inv, gain)
    grad_outer = resid.astype(BF)
    sums_two_ref[...] = column_sums(grad_outer, grad * normed, grad)
    resid_ref[...] = resid

    def halves(values):
        left, right = values[:, :cols], values[:, cols:]
        return jnp.where(first, right, left), jnp.where(first, left, right)

    rows = layout.rows
    def outer_grad(tile):
        lanes = slice(tile * extent, (tile + 1) * extent)
        found = product(active_ref[:, lanes].T, grad_outer).astype(BF)
        for other, columns in zip((1, 0), halves(found)):
            stage_outer[other, lanes, :] = columns
            if layout.split:
                near = extent // layout.block
                for chip in range(near):
                    start = tile * extent + chip * layout.block
                    store(
                        stage_outer.at[other, start : start + layout.block, :],
                        grad_hbm[other].at[tile * near + chip],
                    )
            else:
                store(
                    stage_outer.at[other, lanes, :],
                    grad_hbm[3 * other].at[lanes, :],
                )
    low_t = low_ref[...].T
    total = resid_ref[...]
    for other in (1, 0):
        for part in range(2):
            outer_grad(2 * (1 - other) + part)
            place = 2 * (core ^ other) + part
            grad = product_nt(grad_outer, outer_tile(place))
            grad = (grad * slope_ref[:, span(place, extent)].astype(F32)).astype(BF)
            sums_inner_ref[:, span(place, extent)] = jnp.sum(
                grad.astype(F32), axis=0, keepdims=True
            )
            total += product_nt(grad, inner_tile(place))
            found = product(low_t, grad).astype(BF)
            for i in range(layout.fold // 2):
                index = part * (layout.fold // 2) + i
                stage_inner[other, index] = found[:, i * cols : (i + 1) * cols]
                if layout.split:
                    start = index * rows
                    for chip in range(layout.chips):
                        store(
                            stage_inner.at[other, index, chip * rows : (chip + 1) * rows, :],
                            grad_hbm[2 + other].at[chip, start : start + rows, :],
                        )
                else:
                    store(
                        stage_inner.at[other, index],
                        grad_hbm[3 * other + 1].at[:, index * cols : (index + 1) * cols],
                    )
    normed = normed_ref[...]
    resid = normalize_back(total, normed, inv_one, table_ref[GAIN_ONE : GAIN_ONE + 1])
    resid_ref[...] = resid
    store(resid_ref, resid_hbm)
    attn = resid.astype(BF)
    sums_one_ref[...] = column_sums(attn, total * normed, total)
    back = product_nt(attn[:, :cols], mix_half(0)) + product_nt(attn[:, cols:], mix_half(1))
    for other, columns, target in zip(
        (1, 0), halves(back.astype(BF)), (gc_theirs_hbm, gc_mine_hbm)
    ):
        stage_ctx[other] = columns
        store(stage_ctx.at[other], target)
    context_t = context_ref[...].T
    for other, columns in zip((1, 0), halves(attn)):
        stage_mix[other] = product(context_t, columns).astype(BF)
        if layout.split:
            start = layout.fold * rows
            for chip in range(layout.chips):
                store(
                    stage_mix.at[other, chip * rows : (chip + 1) * rows, :],
                    grad_hbm[2 + other].at[chip, start : start + rows, :],
                )
        else:
            store(stage_mix.at[other], grad_hbm[3 * other + 2])
    for copy in stores:
        copy.wait()


def ffn(layout, where, lengths, table, bias, tokens, cotangent, mine, theirs, weights):
    rows, width = tokens.shape
    units, cols = layout.units, layout.cols
    full, part = (rows, width), (rows, cols)
    if layout.split:
        grads = [(layout.chips, layout.block, cols)] * 2
        grads += [(layout.chips, layout.packed, cols)] * 2
        loads = 1 + 2 * len(mine) + 2 + 2 * layout.fold + 8 + 1
        stores = 4 + 2 * layout.chips * (layout.fold + 2)
    else:
        grads = [(units, cols), (width, units // 2), (width, cols)] * 2
        loads = 5 + 2 * len(mine)
        stores = 4 + 2 * (4 + layout.fold + 1)
    anywhere = pl.BlockSpec(memory_space=pl.ANY)
    arrays = (tokens, cotangent, *mine, *theirs, *weights)
    outs = [((8, width), F32), ((8, width), F32), ((1, units), F32), (full, F32), (full, F32)]
    outs += [(part, BF)] * 2 + [(one, BF) for one in grads]
    return pl.pallas_call(
        functools.partial(ffn_kernel, layout, len(weights)),
        out_shape=tuple(jax.ShapeDtypeStruct(shape, kind) for shape, kind in outs),
        grid_spec=pltpu.PrefetchScalarGridSpec(
            num_scalar_prefetch=2,
            grid=(1,),
            in_specs=on_chip(2) + [anywhere] * len(arrays),
            out_specs=tuple(on_chip(3) + [anywhere] * (len(outs) - 3)),
            scratch_shapes=layout.scratch(rows)
            + [pltpu.SemaphoreType.DMA((loads,)), pltpu.SemaphoreType.DMA((stores,))],
        ),
        compiler_params=pltpu.CompilerParams(vmem_limit_bytes=58 << 20),
        cost_estimate=SMALL,
        name="ffn",
    )(where, lengths, table, bias, *arrays)


def token_kernel(count, where_ref, *refs):
    grad_refs = refs[:count]
    weight_ref, resid_ref, keep_ref, away_ref = refs[count:]
    half = resid_ref.shape[0]
    extent = grad_refs[0].shape[1]
    mine = where_ref[0] * half
    for start, target in ((half - mine, away_ref), (mine, keep_ref)):
        rows = pl.ds(pl.multiple_of(start, half), half)
        part = product_nt(grad_refs[0][rows, :], weight_ref[:, :extent])
        for i in range(1, count):
            part += product_nt(
                grad_refs[i][rows, :], weight_ref[:, i * extent : (i + 1) * extent]
            )
        if target is keep_ref:
            part += resid_ref[...]
        target[...] = part.astype(target.dtype)


def token_grads(where, grads, weight, resid, seqs):
    rows, cols = grads[0].shape
    width = resid.shape[1]
    length = rows // seqs

    def rowwise(extent, columns):
        return pl.BlockSpec((extent, columns), lambda i, *_: (i, 0))

    return pl.pallas_call(
        functools.partial(token_kernel, len(grads)),
        out_shape=(
            jax.ShapeDtypeStruct((rows // 2, width), F32),
            jax.ShapeDtypeStruct((rows // 2, width), BF),
        ),
        grid_spec=pltpu.PrefetchScalarGridSpec(
            num_scalar_prefetch=1,
            grid=(seqs,),
            in_specs=[rowwise(length, cols)] * len(grads)
            + [pl.BlockSpec(weight.shape, lambda *_: (0, 0)), rowwise(length // 2, width)],
            out_specs=(rowwise(length // 2, width), rowwise(length // 2, width)),
        ),
        compiler_params=pltpu.CompilerParams(vmem_limit_bytes=44 << 20),
        cost_estimate=SMALL,
        name="token_grads",
    )(where, *grads, weight, resid)


def combine_kernel(plan, count, where_ref, *refs):
    arrays, refs = refs[:count], refs[count:]
    outs, refs = refs[: len(plan)], refs[len(plan) :]
    buffers, sems = refs[:-1], refs[-1]

    def place(entry):
        if entry is None:
            return slice(None)
        if entry[0] == "side":
            return ((where_ref[1] >> entry[1]) & 1) ^ entry[2]
        if entry[0] == "far":
            return (where_ref[1] >> 2) ^ entry[1]
        return pl.ds(*entry)

    copies = []
    for _, parts in plan:
        for terms, _ in parts:
            for number, index in terms:
                source = arrays[number].at[tuple(place(entry) for entry in index)]
                at = len(copies)
                copies.append(pltpu.make_async_copy(source, buffers[at], sems.at[at]))
                copies[-1].start()
    at = 0
    for (kind, parts), out in zip(plan, outs):
        for terms, window in parts:
            total = None
            for _ in terms:
                copies[at].wait()
                one = buffers[at][...].astype(F32)
                total = one if total is None else total + one
                at += 1
            if window is None:
                out[...] = total.astype(kind)
            else:
                out[window] = total.astype(kind)


def combine(where, jobs, room=None):
    arrays, plan, buffers = [], [], []

    def number(array):
        for i, one in enumerate(arrays):
            if one is array:
                return i
        arrays.append(array)
        return len(arrays) - 1

    for kind, _, parts in jobs:
        planned = []
        for terms, window in parts:
            numbered = []
            for array, index in terms:
                shape = []
                for extent, entry in zip(array.shape, index):
                    if entry is None:
                        shape.append(extent)
                    elif entry[0] not in ("side", "far"):
                        shape.append(entry[1])
                buffers.append(pltpu.VMEM(tuple(shape), array.dtype))
                numbered.append((number(array), tuple(index)))
            planned.append((numbered, window))
        plan.append((kind, planned))
    return pl.pallas_call(
        functools.partial(combine_kernel, plan, len(arrays)),
        out_shape=tuple(jax.ShapeDtypeStruct(shape, kind) for kind, shape, _ in jobs),
        grid_spec=pltpu.PrefetchScalarGridSpec(
            num_scalar_prefetch=1,
            grid=(1,),
            in_specs=[pl.BlockSpec(memory_space=pl.ANY)] * len(arrays),
            out_specs=tuple(on_chip(len(jobs))),
            scratch_shapes=buffers + [pltpu.SemaphoreType.DMA((len(buffers),))],
        ),
        compiler_params=pltpu.CompilerParams(vmem_limit_bytes=room or VMEM_LIMIT),
        cost_estimate=SMALL,
        name="combine",
    )(where, *arrays)


class Sum:
    def __init__(self, terms, flying=()):
        self.terms, self.flying = list(terms), list(flying)


jax.tree_util.register_pytree_node(
    Sum,
    lambda held: (
        ([array for array, _, _ in held.terms], [array for array, _ in held.flying]),
        (
            tuple((bits, window) for _, bits, window in held.terms),
            tuple(mask for _, mask in held.flying),
        ),
    ),
    lambda fixed, arrays: Sum(
        [(array, *about) for array, about in zip(arrays[0], fixed[0])], zip(arrays[1], fixed[1])
    ),
)


def tie(values):
    return lax.optimization_barrier(values)


def after(values, *others):
    return tie((values, others))[0]


def masks(digit):
    found = [0]
    for bit in digit:
        found += [one | (1 << bit) for one in found]
    return found[1:]


class Wires:
    def __init__(self):
        self.chips = lax.axis_size(CHIPS)
        self.bits = self.chips.bit_length() - 1
        self.chip = lax.axis_index(CHIPS)
        self.core = lax.axis_index("seq")
        self.first = self.core == 0
        self.room = None
        far = list(range(self.bits - 1, 1, -1))
        self.far = [tuple(far[i : i + 2]) for i in range(0, len(far), 2)]

    def side(self, bit):
        return (self.chip >> bit) & 1

    def meet(self, values, mask):
        return lax.ppermute(values, CHIPS, [(i, i ^ mask) for i in range(self.chips)])

    def swap_core(self, values):
        return lax.ppermute(values, "seq", [(0, 1), (1, 0)])

    def pick(self, low, high):
        return jnp.where(self.first, low, high), jnp.where(self.first, high, low)

    def columns(self, values):
        cols = values.shape[1] // 2
        return self.pick(values[:, :cols], values[:, cols:])

    def beside(self, mine, theirs, side, axis):
        shape = [1] * (mine.ndim + 1)
        shape[axis] = 2
        here = lax.broadcasted_iota(jnp.int32, tuple(shape), axis) == side
        return jnp.where(here, jnp.expand_dims(mine, axis), jnp.expand_dims(theirs, axis))


    def far_meet(self, values, digit):
        return {0: values} | {mask: self.meet(values, mask) for mask in masks(digit)}

    def far_join(self, found, digit):
        shape = found[0].shape
        for bit in reversed(digit):
            known = {mask for mask in found if not mask & (1 << bit)}
            found = {
                mask: self.beside(found[mask], found[mask | (1 << bit)], self.side(bit), 1)
                for mask in sorted(known)
            }
        return found[0].reshape((-1,) + shape[1:])

    def gather_far(self, values, digit):
        return self.far_join(self.far_meet(values, digit), digit)

    def gather_near(self, values, bit):
        return self.beside(values, self.meet(values, 1 << bit), self.side(bit), 1)

    def pieces(self, values, bit):
        width = values.shape[-1]
        rows = values.shape[-2] << bit
        values = values.reshape(-1, rows, width)
        return values, self.meet(values, 1 << bit)

    def gather_plane(self, values):
        return [values] + [self.meet(values, mask) for mask in masks((0, 1))]

    def plane(self, pieces):
        own = self.chip & 3
        stacked = jnp.stack(pieces, axis=1)
        parts = [
            lax.dynamic_index_in_dim(stacked, own ^ place, 1, keepdims=False) for place in range(4)
        ]
        return jnp.concatenate(parts, axis=1)

    def whole(self, pieces, bit):
        width = pieces[0].shape[-1]
        return self.beside(pieces[0], pieces[1], self.side(bit), 1).reshape(-1, width)


    def spread(self, terms, tail, windows):
        bits = tuple(range(self.bits - 1, -1, -1))
        arrays = [one.reshape([2] * self.bits + list(tail)) for one in terms]
        return [Sum([(one, bits, window) for one in arrays]) for window in windows]

    def part(self, held, fixed):
        total = None
        for array, bits, window in held.terms:
            tail = array.shape[len(bits) :]
            first, size = window if window else ((0,) * len(tail), tail)
            starts = [fixed.get(bit, 0) for bit in bits] + list(first)
            sizes = [1 if bit in fixed else 2 for bit in bits] + list(size)
            shape = [2 for bit in bits if bit not in fixed] + list(size)[-2:]
            one = lax.dynamic_slice(array, starts, sizes).reshape(shape).astype(F32)
            total = one if total is None else total + one
        return total

    def left(self, held):
        return held.terms[-1][1]

    def settled(self, held):
        return {bit: self.side(bit) for bit in range(self.bits) if bit not in self.left(held)}

    def ready(self, held, digit):
        fixed = self.settled(held)
        sent = []
        for mask in masks(digit):
            away = {bit: self.side(bit) ^ ((mask >> bit) & 1) for bit in digit}
            sent.append((self.part(held, {**fixed, **away}).astype(BF), mask))
        return Sum(held.terms, sent)

    def go(self, held):
        return Sum(held.terms, [(self.meet(one, mask), mask) for one, mask in held.flying])

    def land(self, held, digit):
        bits = tuple(bit for bit in self.left(held) if bit not in digit)
        return Sum(held.terms + [(one, bits, None) for one, _ in held.flying])

    def total(self, held):
        return self.part(held, self.settled(held))


    def slices(self, held, stream, step, far=None):
        first, second = stream, 1 - stream
        near = {first: ("side", first, 1 - min(step, 1)), second: None}
        if step > 0:
            near[second] = ("side", second, 2 - step)
        found = []
        for array, bits, window in held.terms:
            tail = array.shape[len(bits) :]
            shape = (4,) + (2,) * (len(bits) - 2) + tail
            index = [far] + [near[bit] for bit in bits[2:]]
            if window is None:
                index += [None] * len(tail)
            else:
                index += list(zip(*window))
            found.append((array.reshape(shape), index))
        return found

    def extent(self, held):
        array, bits, window = held.terms[0]
        return tuple(window[1]) if window else array.shape[len(bits) :]

    def near_ready(self, pair, step):
        if not self.kernels:
            return [self.ready(held, (stream ^ step,)) for stream, held in enumerate(pair)]
        jobs = []
        for stream, held in enumerate(pair):
            shape = (4,) + (2,) * (1 - step) + self.extent(held)
            jobs.append((BF, shape, [(self.slices(held, stream, step), None)]))
        sent = combine(self.where, jobs, self.room)
        return [
            Sum(
                held.terms,
                [(one.reshape((2,) * (3 - step) + self.extent(held)), 1 << (stream ^ step))],
            )
            for stream, (held, one) in enumerate(zip(pair, sent))
        ]

    def far_parts(self, pair, axis, far):
        parts, begin, extents = [], 0, []
        for stream, held in enumerate(pair):
            extent = self.extent(held)
            window = [slice(None)] * (2 + (far is None))
            window[axis] = slice(begin, begin + extent[axis])
            begin += extent[axis]
            extents.append(extent)
            parts.append((self.slices(held, stream, 2, far), tuple(window)))
        shape = list(extents[0])
        shape[axis] = begin
        return tuple(shape), parts

    def far_ready(self, pair, axis):
        if not self.kernels:
            held = self.far_steps(self.joined(pair, axis))
            held = self.ready(held, self.far[-1])
            own = {bit: self.side(bit) for bit in range(self.bits)}
            return self.part(held, own), [one for one, _ in held.flying]
        jobs = []
        for mask in [0] + masks(self.far[-1]):
            shape, parts = self.far_parts(pair, axis, ("far", mask >> 2))
            jobs.append((BF if mask else F32, shape, parts))
        kept, *sent = combine(self.where, jobs, self.room)
        return kept, sent

    def far_go(self, held):
        kept, sent = held
        return kept, [self.meet(one, mask) for one, mask in zip(sent, masks(self.far[-1]))]

    def far_total(self, held):
        kept, arrived = held
        for one in arrived:
            kept = kept + one.astype(F32)
        return kept

    def far_rows(self, pair, axis):
        if self.kernels:
            shape, parts = self.far_parts(pair, axis, None)
            array = combine(self.where, [(BF, (4,) + shape, parts)], self.room)[0]
        else:
            array = self.joined(pair, axis).terms[0][0]
        return lax.psum_scatter(
            array.reshape(-1, array.shape[-1]), "far", scatter_dimension=0, tiled=True
        )

    def near_go(self, pair):
        return [self.go(held) for held in pair]

    def near_land(self, pair, step):
        return [self.land(held, (stream ^ step,)) for stream, held in enumerate(pair)]

    def joined(self, pair, axis):
        sums = [self.total(held).astype(BF) for held in pair]
        return Sum([(jnp.concatenate(sums, axis=axis), self.left(pair[0]), None)])

    def far_steps(self, held):
        for digit in self.far[:-1]:
            held = self.land(self.go(self.ready(held, digit)), digit)
        return held

    def owned(self, block):
        rows = block.shape[0] // 2
        return self.pick(block[:rows], block[rows:])


def body(tokens, lengths, cotangent, *shards):
    (
        w_query,
        b_query,
        w_key,
        w_value,
        b_value,
        w_out,
        b_out,
        gain_one,
        shift_one,
        w_inner,
        b_inner,
        w_outer,
        b_outer,
        gain_two,
        shift_two,
    ) = shards
    wires = Wires()
    core = wires.core
    devices = 2 * wires.chips
    seqs, half, width = tokens.shape
    rows = seqs * half
    cols = width // 2
    slot = b_query.shape[0]
    fold = b_inner.shape[0] // slot
    plane = wires.chip & 3
    where = jnp.stack([core, wires.chip, plane, wires.side(0), wires.side(1)]).astype(jnp.int32)

    vectors = jnp.stack(
        [b_query, b_value, b_out, gain_one, shift_one, b_outer, gain_two, shift_two]
    )
    vectors = jnp.concatenate([vectors, b_inner.reshape(fold, slot)], axis=0)
    vectors = jnp.pad(vectors.T, ((0, 0), (0, LANES - vectors.shape[0])))
    mine, away = zip(*[wires.columns(one) for one in (w_query, w_key, w_value, w_out, w_inner)])
    pairs = cols // PAIR

    def by_pair(parts):
        spans = [slice(p * PAIR, (p + 1) * PAIR) for p in range(pairs)]
        return jnp.concatenate([one[:, span] for span in spans for one in parts] + [vectors], axis=1)

    def both_rows(kept, sent):
        return ordered(wires.first, kept, wires.swap_core(sent), 0)

    units = w_inner.shape[1]
    paired = 2 * slot
    layout = Layout(wires.chips, width, units)
    aligned = wires.kernels = layout.split
    wires.where = where
    first = both_rows(by_pair(mine[:3]), by_pair(away[:3]))[None]
    outer_mine, outer_away = wires.columns(w_outer)
    outer_held = both_rows(outer_mine, outer_away)[None]
    if aligned:
        parts = [jnp.concatenate([inner, out], axis=1) for out, inner in (mine[3:], away[3:])]
        second = both_rows(*parts)
        second = jnp.concatenate(
            [second[:, i : i + cols] for i in range(0, second.shape[1], cols)], axis=0
        )
        second = lax.all_gather(second, CHIPS + ("seq",), axis=0, tiled=True)
        weights = [second.reshape(wires.chips, 2, -1, cols)]
    else:
        weights = [
            lax.all_gather(one, CHIPS + ("seq",), axis=0, tiled=True)
            for one in (w_out, w_inner, w_outer)
        ]
    for digit in wires.far:
        first = wires.gather_far(first, digit)
    first, outer_held = tie((first, outer_held))
    for digit in wires.far[:-1]:
        outer_held = wires.gather_far(outer_held, digit)
    outer_held = wires.far_meet(outer_held, wires.far[-1])
    cut = (3 * pairs + 1) // 2 * LANES
    one = wires.gather_near(first[..., :cut], 1)
    two = wires.gather_near(first[..., cut:], 0)
    pieces_one, pieces_two = wires.pieces(one, 0), wires.pieces(two, 1)
    if not aligned:
        pieces_one, pieces_two = [
            (wires.whole(pieces, bit)[None],)
            for bit, pieces in enumerate((pieces_one, pieces_two))
        ]
    tok_rows = tokens.reshape(rows, width)
    tok_other = wires.swap_core(tokens)
    tok_all = ordered(wires.first, tokens, tok_other, 1).reshape(2 * rows, width)

    held = attend(0, where, lengths, tokens, tok_other, (pieces_one, pieces_two))
    w_qkv, table = held[4:]
    heads = [held[:4]]
    if aligned:
        w_qkv, table, outer_held = tie((w_qkv, table, outer_held))
        outer_held = wires.gather_plane(wires.far_join(outer_held, wires.far[-1]))
    for seq in range(1, seqs):
        heads.append(attend(seq, where, lengths, tokens, tok_other, (w_qkv, table)))
    qkv, ctx_mine, ctx_away, lse = zip(*heads)
    ctx_theirs = [wires.swap_core(one) for one in ctx_away]
    if aligned:
        ctx_theirs, outer_held = tie((ctx_theirs, outer_held))
        weights += outer_held + [wires.swap_core(one) for one in outer_held]
    kept = 8 + fold
    bias_inner = table[8:kept].reshape(fold, devices, slot).transpose(1, 0, 2).reshape(1, -1)
    results = ffn(
        layout,
        where,
        lengths,
        table,
        bias_inner,
        tok_rows,
        cotangent.reshape(rows, width),
        ctx_mine,
        ctx_theirs,
        weights,
    )
    sums_two, sums_one, sums_inner, output, resid_one, gc_mine, gc_away = results[:7]
    grad_parts = results[7:]
    if not aligned:

        def by_chip(many):
            g_outer, g_inner, g_out = many
            g_inner = g_inner.reshape(wires.chips, -1, fold, cols).transpose(0, 2, 1, 3)
            others = (g_inner.reshape(wires.chips, -1, cols), g_out.reshape(wires.chips, -1, cols))
            return g_outer.reshape(wires.chips, -1, cols), jnp.concatenate(others, axis=1)

        mine, away = by_chip(grad_parts[:3]), by_chip(grad_parts[3:])
        grad_parts = (mine[0], away[0], mine[1], away[1])
    g_outer, g_outer_away, g_rest, g_rest_away = grad_parts

    last = wires.far[-1]
    rows_chip = 2 * slot
    gc_theirs = wires.swap_core(gc_away)
    base = jnp.concatenate(
        [
            jnp.zeros((2, width), F32),
            sums_one[:3],
            sums_two[:3],
            sums_inner.reshape(devices, fold, slot).transpose(1, 0, 2).reshape(fold, width),
            jnp.zeros((TABLE - kept, width), F32),
        ],
        axis=0,
    )

    def two_windows(held, theirs):
        extent = held.shape[1]
        cut = extent // 2 // 16 * 16 if aligned else extent // 2
        return wires.spread(
            [held, theirs],
            (extent, cols),
            [((0, 0), (cut, cols)), ((cut, 0), (extent - cut, cols))],
        )

    def attention_grad(pair, held, widths):
        return attend_back(
            pair, where, lengths, qkv, lse, gc_mine, gc_theirs, tok_all, held, widths
        )

    pair_width = 3 * PAIR
    more = (3 * pairs + 1) // 2 * LANES - pair_width
    arrived = wires.swap_core(g_outer_away)
    g_rest_away = after(g_rest_away, arrived)
    outer = wires.near_ready(two_windows(g_outer, arrived), 0)
    gc_mine, outer = tie((gc_mine, outer))
    outer = wires.near_go(outer)
    grad_one, sums_first, g_first = attention_grad(0, (), (pair_width,))
    arrived = wires.swap_core(g_rest_away)
    grad_one, arrived, base = tie((grad_one, arrived, base))
    rest = wires.near_ready(two_windows(g_rest, arrived), 0)
    gc_mine, rest = tie((gc_mine, rest))
    rest = wires.near_go(rest)
    grad_two, sums_second, g_one, g_kept = attention_grad(
        1, (g_first,), (pair_width + more, pair_width - more)
    )
    grad_two, outer = tie((grad_two, outer))
    outer = wires.near_ready(wires.near_land(outer, 0), 1)
    gc_mine, outer = tie((gc_mine, outer))
    outer = wires.near_go(outer)
    grad_three, _, g_two = attention_grad(
        2,
        (g_kept, base, sums_first, sums_second),
        (2 * pair_width - more + LANES,),
    )
    grads = [grad_one, grad_two, grad_three]
    grads, rest = tie((grads, rest))
    rest = wires.near_ready(wires.near_land(rest, 0), 1)
    g_one, g_two, rest = tie((g_one, g_two, rest))
    rest = wires.near_go(rest)
    both = [wires.spread([one], (rows_chip, one.shape[1]), [None])[0] for one in (g_one, g_two)]
    both = wires.near_ready(both, 0)
    grads, both = tie((grads, both))
    both = wires.near_go(both)
    tok_keep, tok_away = token_grads(where, grads, w_qkv, resid_one, seqs)
    tok_away, tok_keep, outer = tie((tok_away, tok_keep, outer))
    g_outer = wires.far_rows(wires.near_land(outer, 1), -2)
    tok_away, rest, both = tie((tok_away, rest, both))
    wires.room = 60 << 20
    tok_theirs = wires.swap_core(tok_away)
    both = wires.near_ready(wires.near_land(both, 0), 1)
    rest = after(rest, both)
    g_rest = wires.far_rows(wires.near_land(rest, 1), -2)
    tok_keep, both = tie((tok_keep, both))
    both = wires.near_go(both)
    both, tok_theirs = tie((both, tok_theirs))
    both = wires.far_ready(wires.near_land(both, 1), -1)
    both, tok_theirs, tok_keep = tie((both, tok_theirs, tok_keep))
    both = wires.far_go(both)
    grad_tok = tok_keep + tok_theirs.astype(F32)
    g_rest = after(g_rest, both[1]).astype(F32)
    g_both = wires.far_total(both)

    columns = [g_both] + [
        g_rest[i * rows_chip : (i + 1) * rows_chip] for i in range(fold + 1)
    ]
    mine, away = wires.owned(jnp.concatenate(columns, axis=1))
    theirs = wires.swap_core(away)
    mine_outer, away = wires.owned(g_outer.astype(F32))
    g_outer = ordered(wires.first, mine_outer, wires.swap_core(away), 1)
    begin = g_both.shape[1]

    def full(spans):
        return jnp.concatenate(
            [one[:, span] for one in wires.pick(mine, theirs) for span in spans], axis=1
        )

    pieces = [
        full([slice((3 * p + i) * PAIR, (3 * p + i + 1) * PAIR) for p in range(pairs)])
        for i in range(3)
    ]
    pieces.append(full([slice(begin + fold * cols, begin + (fold + 1) * cols)]))
    pieces.append(full([slice(begin, begin + fold * cols)]))
    vectors = slice(begin - LANES, begin)
    small = (mine[:, vectors] + theirs[:, vectors]).T

    return (
        output.reshape(seqs, half, width),
        grad_tok.reshape(seqs, half, width),
        pieces[0],
        small[0],
        pieces[1],
        pieces[2],
        small[1],
        pieces[3],
        small[2],
        small[3],
        small[4],
        pieces[4],
        small[8:kept].reshape(-1),
        g_outer,
        small[5],
        small[6],
        small[7],
    )


def solution(mesh):
    cores = mesh.shape["seq"]
    split = Mesh(mesh.devices.reshape(-1, 2, 2, cores), CHIPS + ("seq",))
    every = CHIPS + ("seq",)
    matrix, vector = P(every, None), P(every)
    rows = P(CHIPS, "seq", None)
    weights = (matrix, vector, matrix, matrix, vector, matrix, vector, vector, vector)
    weights += (matrix, vector, matrix, vector, vector, vector)
    return jax.shard_map(
        body,
        mesh=split,
        in_specs=(rows, P(CHIPS), rows) + weights,
        out_specs=(rows, rows) + weights,
        check_vma=False,
    )
```
